256 devices in a mesh: ctx: 8 (over x, y_hi), chan: 32 (over z, y_lo, core).
Axes of the slice: x: 4, y: 4 (y_hi: 2, y_lo: 2; y = y_hi * 2 + y_lo), z: 8, core: 2. Of those that a mesh axis runs over, the one named last changes fastest.
Arguments:
- inputs: bfloat16 [4096, 4096], P('ctx', 'chan'), may hold values from -6 to 6
- w_in: bfloat16 [4096, 3, 4096], P(None, None, 'chan'), may hold values from -0.09375 to 0.09375
- conv_taps: bfloat16 [3, 3, 4096], P(None, None, 'chan'), may hold values from -3.59375 to 3.59375
- skip_gain: float32 [4096], P('chan'), may hold values from 0.5 to 1.5
- filter_taps: bfloat16 [4096, 4096], P('ctx', 'chan'), may hold values from -0.09375 to 0.09375
- w_out: bfloat16 [4096, 4096], P('chan'), may hold values from -0.1875 to 0.1875
Outputs:
- result: bfloat16 [4096, 4096], P('ctx', 'chan')
The draws below stay inside these ranges and needn't reach their ends.
All inputs are finite; a program needn't handle non-finite values.
Results may differ from the reference program's by a relative error of at most 0.024.
Values may be sent and summed in bfloat16 or wider, within the bound.
A program may use at most 64 MiB of HBM per device.

```python
import math
import jax
import jax.numpy as jnp

D = 4096
KERNEL = 3
SPAN = 512
LEN = 4096
N_CTX = 8


def spiked(result, key, source, target, shards_of, factor):
    owner, partner = [(jnp.arange(result.shape[axis_at]) // (result.shape[axis_at] // shards_of)).reshape([-1 if axis == axis_at else 1 for axis in range(result.ndim)]) for axis_at in (source, target)]
    chosen = jax.random.permutation(key, shards_of)[partner]
    strong = (owner == chosen) | (owner == (partner + shards_of // 2) % shards_of)
    return jnp.where(strong, factor * result, result)


def block_levels(key, extent, pieces, smallest, high):
    def one(dim, parts):
        draws = jax.random.uniform(jax.random.fold_in(jax.random.fold_in(key, 6), dim), (parts,), jnp.float32, smallest / len(pieces), high / len(pieces))
        return jnp.repeat(jnp.exp(draws), extent[dim] // parts).reshape((-1,) + (1,) * (len(extent) - dim - 1))

    gain = one(*pieces[0])
    for cut in pieces[1:]:
        gain = gain * one(*cut)
    return gain


def noise(rng, extent, scale, most, split=(), kind=jnp.bfloat16):
    gain = block_levels(rng, extent, split, -0.22, 0.18) if split else 1.0
    entries = jax.random.normal(rng, extent, jnp.float32) * scale * gain
    return jnp.minimum(jnp.maximum(entries, -most), most).astype(kind)


def bell_draw_with(stream_key, shape, deviation, bound, shards, heavy, kind=jnp.bfloat16):
    entries = deviation * jax.random.normal(stream_key, shape, jnp.float32)
    if shards:
        entries = entries * block_levels(stream_key, shape, shards, -0.22, 0.18)
    return jnp.clip(spiked(entries, jax.random.fold_in(stream_key, 3), *heavy), -bound, bound).astype(kind)


def setup_inputs(seed: int = 0) -> dict:
    key_of = jax.random.split(jax.random.key(seed), 7)
    inputs = noise(key_of[0], (LEN, D), 1.0, 6.0, ((0, 8), (1, 32)))
    w_in = noise(key_of[1], (D, 3, D), D ** -0.5, 0.09375, ((2, 32),))
    conv_taps = noise(key_of[2], (KERNEL, 3, D), 0.6, 3.59375, ((2, 32),))
    skip_gain = jnp.clip(0.5 + 1.0 * jax.random.uniform(key_of[3], (D,), jnp.float32) ** block_levels(key_of[3], (D,), ((0, 32),), -0.2, 0.2), 0.5, 1.5)
    filter_taps = noise(key_of[4], (LEN, D), LEN ** -0.5, 0.09375, ((0, 8), (1, 32)))
    w_out = bell_draw_with(key_of[5], (D, D), D ** -0.5, 0.1875, ((0, 32),), (0, 1, 32, 2.75))
    return dict(inputs=inputs, w_in=w_in, conv_taps=conv_taps, skip_gain=skip_gain, filter_taps=filter_taps, w_out=w_out)


def angles(row_count, col_count, double_len):
    row_ids = jnp.arange(row_count, dtype=jnp.int32)[:, None]
    col_ids = jnp.arange(col_count, dtype=jnp.int32)[None, :]
    return (2.0 * math.pi / double_len) * ((row_ids * col_ids) % double_len).astype(jnp.float32)


def tables(span_len):
    double_len = 2 * span_len
    first = angles(double_len, span_len, double_len)
    forward_in = jnp.concatenate([jnp.cos(first), -jnp.sin(first)], 0).astype(jnp.bfloat16)
    second = angles(double_len, double_len, double_len)
    forward_taps = jnp.concatenate([jnp.cos(second), -jnp.sin(second)], 0).astype(jnp.bfloat16)
    third = angles(span_len, double_len, double_len)
    inverse = (jnp.concatenate([jnp.cos(third), -jnp.sin(third)], 1) / double_len).astype(jnp.bfloat16)
    return forward_in, forward_taps, inverse


def spectral_product(taps_spec, input_spec, double_len):
    real_g = taps_spec[:double_len].astype(jnp.float32)
    imag_g = taps_spec[double_len:].astype(jnp.float32)
    real_u = input_spec[:double_len].astype(jnp.float32)
    imag_u = input_spec[double_len:].astype(jnp.float32)
    return jnp.concatenate([real_g * real_u - imag_g * imag_u, real_g * imag_u + imag_g * real_u], 0)


def reference(inputs, w_in, conv_taps, skip_gain, filter_taps, w_out):
    span_len = SPAN
    double_len = 2 * span_len
    projected = jnp.dot(inputs, w_in.reshape(D, 3 * D), preferred_element_type=jnp.float32)
    projected = projected.astype(jnp.bfloat16).reshape(LEN, 3, D)
    padded = jnp.concatenate([jnp.zeros((KERNEL - 1, 3, D), jnp.bfloat16), projected], 0)
    filtered = jnp.zeros((LEN, 3, D), jnp.float32)
    for lag in range(KERNEL):
        start_row = KERNEL - 1 - lag
        filtered = filtered + conv_taps[lag].astype(jnp.float32) * padded[start_row:start_row + LEN].astype(jnp.float32)
    streams = filtered.astype(jnp.bfloat16)
    gate_out = streams[:, 0]
    gated_in = (streams[:, 1].astype(jnp.float32) * streams[:, 2].astype(jnp.float32)).astype(jnp.bfloat16)
    forward_in, forward_taps, inverse = tables(span_len)
    blocks = gated_in.reshape(N_CTX, span_len, D)
    spectra_in = jnp.einsum("fb,kbd->kfd", forward_in.astype(jnp.float32), blocks.astype(jnp.float32)).astype(jnp.bfloat16)
    lag_blocks = filter_taps.reshape(N_CTX, span_len, D)
    previous = jnp.concatenate([jnp.zeros((1, span_len, D), jnp.bfloat16), lag_blocks[:-1]], 0)
    padded_taps = jnp.concatenate([lag_blocks, jnp.zeros((N_CTX, 1, D), jnp.bfloat16), previous[:, 1:]], 1)
    spectra_taps = jnp.einsum("fm,kmd->kfd", forward_taps.astype(jnp.float32), padded_taps.astype(jnp.float32)).astype(jnp.bfloat16)
    outputs = []
    for target in range(N_CTX):
        mixture = jnp.zeros((2 * double_len, D), jnp.float32)
        for source in range(target + 1):
            mixture = mixture + spectral_product(spectra_taps[target - source], spectra_in[source], double_len)
        long_out = jnp.dot(inverse, mixture.astype(jnp.bfloat16), preferred_element_type=jnp.float32)
        long_out = long_out + skip_gain.astype(jnp.float32) * blocks[target].astype(jnp.float32)
        gate_rows = gate_out[target * span_len:(target + 1) * span_len].astype(jnp.float32)
        outputs.append((gate_rows * long_out).astype(jnp.bfloat16))
    gated_out = jnp.concatenate(outputs, 0)
    return jnp.dot(gated_out, w_out, preferred_element_type=jnp.float32).astype(jnp.bfloat16)
```

```python
import math

import jax
import jax.numpy as jnp
from jax import lax
from jax.sharding import PartitionSpec as P

KERNEL = 3


def dft_table(double_len):
    step = 32
    hi_ids = jnp.arange(double_len // step, dtype=jnp.int32)[:, None]
    lo_ids = jnp.arange(step, dtype=jnp.int32)[:, None]
    cols = jnp.arange(double_len, dtype=jnp.int32)[None, :]
    scale = 2.0 * math.pi / double_len
    hi_angle = scale * (hi_ids * step * cols % double_len).astype(jnp.float32)
    lo_angle = scale * (lo_ids * cols % double_len).astype(jnp.float32)
    hc, hs = jnp.cos(hi_angle)[:, None], jnp.sin(hi_angle)[:, None]
    lc, ls = jnp.cos(lo_angle)[None], jnp.sin(lo_angle)[None]
    cos = (hc * lc - hs * ls).reshape(double_len, double_len)
    sin = (hs * lc + hc * ls).reshape(double_len, double_len)
    return jnp.concatenate([cos, -sin], 0).astype(jnp.bfloat16)


def body(inputs, w_in, conv_taps, skip_gain, filter_taps, w_out):
    span_len, width_dev = inputs.shape
    double_len = 2 * span_len
    groups = lax.axis_size("ctx")
    position = lax.axis_index("ctx")
    own = width_dev // groups

    with jax.named_scope("out_weight_columns"):
        w_cols = lax.all_to_all(w_out, "chan", 1, 0, tiled=True)

    with jax.named_scope("filter_to_owner"):
        taps_t = filter_taps.T.reshape(groups, own, span_len)
        taps_t = lax.all_to_all(taps_t, "ctx", 0, 0, tiled=True)

    with jax.named_scope("input_projection"):
        inputs_t = lax.all_gather(inputs.T, "chan", axis=0, tiled=True)
        w_flat = w_in.reshape(w_in.shape[0], 3 * width_dev)
        proj_t = lax.dot_general(
            w_flat, inputs_t, (((0,), (0,)), ((), ())), preferred_element_type=jnp.float32
        ).astype(jnp.bfloat16)

    with jax.named_scope("projection_to_owner"):
        proj_t = proj_t.reshape(3, groups, own, span_len)
        proj_t = lax.all_to_all(proj_t, "ctx", 1, 1, tiled=True)

    with jax.named_scope("short_conv"):
        start = position * own
        taps = lax.dynamic_slice_in_dim(conv_taps, start, own, axis=2)
        rim = jnp.pad(proj_t[:, :-1, :, span_len - (KERNEL - 1) :], ((0, 0), (1, 0), (0, 0), (0, 0)))
        padded = jnp.concatenate([rim, proj_t], 3)
        filtered = jnp.zeros(proj_t.shape, jnp.float32)
        for lag in range(KERNEL):
            start_row = KERNEL - 1 - lag
            filtered = filtered + taps[lag].astype(jnp.float32)[:, None, :, None] * padded[
                ..., start_row : start_row + span_len
            ].astype(jnp.float32)
        streams = filtered.astype(jnp.bfloat16)
        gate_out = streams[0]
        gated_in = (streams[1].astype(jnp.float32) * streams[2].astype(jnp.float32)).astype(
            jnp.bfloat16
        )

    with jax.named_scope("spectra"):
        table = dft_table(double_len)
        forward_in = table[:, :span_len]
        spectra_in = jnp.einsum(
            "jdb,fb->jdf", gated_in, forward_in, preferred_element_type=jnp.float32
        ).astype(jnp.bfloat16)
        previous = jnp.pad(taps_t[:-1, :, 1:], ((1, 0), (0, 0), (0, 0)))
        padded_taps = jnp.concatenate(
            [taps_t, jnp.zeros((groups, own, 1), jnp.bfloat16), previous], 2
        )
        spectra_taps = jnp.einsum(
            "kdm,fm->kdf", padded_taps, table, preferred_element_type=jnp.float32
        ).astype(jnp.bfloat16)

    with jax.named_scope("mixture"):
        real_g = spectra_taps[:, :, :double_len].astype(jnp.float32)
        imag_g = spectra_taps[:, :, double_len:].astype(jnp.float32)
        real_u = spectra_in[:, :, :double_len].astype(jnp.float32)
        imag_u = spectra_in[:, :, double_len:].astype(jnp.float32)
        mixed = []
        for target in range(groups):
            acc_r = jnp.zeros((own, double_len), jnp.float32)
            acc_i = jnp.zeros((own, double_len), jnp.float32)
            for source in range(target + 1):
                lag = target - source
                acc_r = acc_r + (real_g[lag] * real_u[source] - imag_g[lag] * imag_u[source])
                acc_i = acc_i + (real_g[lag] * imag_u[source] + imag_g[lag] * real_u[source])
            mixed.append(jnp.concatenate([acc_r, acc_i], 1))
        mixture = jnp.stack(mixed, 0).astype(jnp.bfloat16)

    with jax.named_scope("inverse_and_gate"):
        long_out = jnp.einsum(
            "idf,fa->ida", mixture, forward_in, preferred_element_type=jnp.float32
        ) * (1.0 / double_len)
        gain = lax.dynamic_slice_in_dim(skip_gain, start, own)
        long_out = long_out + gain[None, :, None] * gated_in.astype(jnp.float32)
        gated_out = (gate_out.astype(jnp.float32) * long_out).astype(jnp.bfloat16)

    with jax.named_scope("gated_back_to_rows"):
        gated_out = lax.all_to_all(gated_out, "ctx", 0, 0, tiled=True)
        gated_out = gated_out.reshape(width_dev, span_len)

    with jax.named_scope("output_projection"):
        gathered = lax.all_gather(gated_out, "chan", axis=0, tiled=True)
        result = lax.dot_general(
            gathered, w_cols, (((0,), (0,)), ((), ())), preferred_element_type=jnp.float32
        ).astype(jnp.bfloat16)
    return result


def solution(mesh):
    return jax.shard_map(
        body,
        mesh=mesh,
        in_specs=(
            P("ctx", "chan"),
            P(None, None, "chan"),
            P(None, None, "chan"),
            P("chan"),
            P("ctx", "chan"),
            P("chan", None),
        ),
        out_specs=P("ctx", "chan"),
        check_vma=False,
    )
```

```python
import math

import functools

import jax
import jax.numpy as jnp
from jax import lax
from jax.experimental import pallas as pl
from jax.experimental.pallas import tpu as pltpu
from jax.sharding import PartitionSpec as P

KERNEL = 3
MESH = pl.DeviceIdType.MESH
PER_Z = 4


def gather_kernel(chips, x_ref, out_ref, local_sem, cross_send, cross_recv, ring_send, ring_recv,
                  sib_send, sib_recv):
    row = lax.axis_index("ctx")
    me = lax.axis_index("chan")
    z = me // PER_Z
    y_lo = (me // 2) % 2
    core = me % 2
    way = 1 - 2 * core
    after = ((z + way + chips) % chips) * PER_Z + y_lo * 2 + core
    before = ((z - way + chips) % chips) * PER_Z + y_lo * 2 + core
    sibling = me + 1 - 2 * core
    across = me + 2 - 4 * y_lo
    diagonal = across + 1 - 2 * core
    partners = (sibling, across, diagonal)

    barrier = pltpu.get_barrier_semaphore()
    for peer in partners + (after, before):
        pl.semaphore_signal(barrier, inc=1, device_id=(row, peer), device_id_type=MESH)
    pl.semaphore_wait(barrier, 5)

    local = pltpu.make_async_copy(x_ref, out_ref.at[me], local_sem)
    local.start()

    def cross(k, peer, slot):
        return pltpu.make_async_remote_copy(
            src_ref=x_ref, dst_ref=out_ref.at[slot], send_sem=cross_send.at[k],
            recv_sem=cross_recv.at[k], device_id=(row, peer), device_id_type=MESH)

    for k, peer in enumerate(partners):
        cross(k, peer, me).start()
    local.wait()
    for k, peer in enumerate(partners):
        cross(k, peer, me).wait_send()
        cross(k, peer, peer).wait_recv()

    def group(chip):
        return out_ref.at[pl.ds(pl.multiple_of(chip * PER_Z, PER_Z), PER_Z)]

    def ring(s, chip):
        return pltpu.make_async_remote_copy(
            src_ref=group(chip), dst_ref=group(chip), send_sem=ring_send.at[s],
            recv_sem=ring_recv.at[s], device_id=(row, after), device_id_type=MESH)

    def sib(s, chip):
        return pltpu.make_async_remote_copy(
            src_ref=group(chip), dst_ref=group(chip), send_sem=sib_send.at[s],
            recv_sem=sib_recv.at[s], device_id=(row, sibling), device_id_type=MESH)

    longest = chips // 2
    for s in range(longest):
        active = jnp.logical_or(core == 0, s < chips - 1 - longest)
        sent = (z - way * s + chips) % chips
        got = (z - way * (s + 1) + chips) % chips

        @pl.when(active)
        def _():
            ring(s, sent).start()
            ring(s, got).wait_recv()
            sib(s, got).start()

    for s in range(longest):
        active = jnp.logical_or(core == 0, s < chips - 1 - longest)
        sent = (z - way * s + chips) % chips
        got = (z - way * (s + 1) + chips) % chips
        other = jnp.logical_or(core == 1, s < chips - 1 - longest)
        theirs = (z + way * (s + 1) + chips) % chips

        @pl.when(active)
        def _():
            ring(s, sent).wait_send()
            sib(s, got).wait_send()

        @pl.when(other)
        def _():
            sib(s, theirs).wait_recv()


def chan_gather(x, collective_id):
    size = lax.axis_size("chan")
    chips = size // PER_Z
    longest = chips // 2
    return pl.pallas_call(
        functools.partial(gather_kernel, chips),
        out_shape=jax.ShapeDtypeStruct((size,) + x.shape, x.dtype),
        in_specs=[pl.BlockSpec(memory_space=pltpu.VMEM)],
        out_specs=pl.BlockSpec(memory_space=pltpu.VMEM),
        scratch_shapes=[
            pltpu.SemaphoreType.DMA(()),
            pltpu.SemaphoreType.DMA((3,)),
            pltpu.SemaphoreType.DMA((3,)),
            pltpu.SemaphoreType.DMA((longest,)),
            pltpu.SemaphoreType.DMA((longest,)),
            pltpu.SemaphoreType.DMA((longest,)),
            pltpu.SemaphoreType.DMA((longest,)),
        ],
        compiler_params=pltpu.CompilerParams(collective_id=collective_id, has_side_effects=True),
    )(x).reshape(size * x.shape[0], x.shape[1])


def dft_table(double_len):
    step = 32
    hi_ids = jnp.arange(double_len // step, dtype=jnp.int32)[:, None]
    lo_ids = jnp.arange(step, dtype=jnp.int32)[:, None]
    cols = jnp.arange(double_len, dtype=jnp.int32)[None, :]
    scale = 2.0 * math.pi / double_len
    hi_angle = scale * (hi_ids * step * cols % double_len).astype(jnp.float32)
    lo_angle = scale * (lo_ids * cols % double_len).astype(jnp.float32)
    hc, hs = jnp.cos(hi_angle)[:, None], jnp.sin(hi_angle)[:, None]
    lc, ls = jnp.cos(lo_angle)[None], jnp.sin(lo_angle)[None]
    cos = (hc * lc - hs * ls).reshape(double_len, double_len)
    sin = (hs * lc + hc * ls).reshape(double_len, double_len)
    return jnp.concatenate([cos, -sin], 0).astype(jnp.bfloat16)


def body(inputs, w_in, conv_taps, skip_gain, filter_taps, w_out):
    span_len, width_dev = inputs.shape
    double_len = 2 * span_len
    groups = lax.axis_size("ctx")
    position = lax.axis_index("ctx")
    own = width_dev // groups

    with jax.named_scope("out_weight_columns"):
        w_cols = lax.all_to_all(w_out, "chan", 1, 0, tiled=True)

    with jax.named_scope("filter_to_owner"):
        taps_t = filter_taps.T.reshape(groups, own, span_len)
        taps_t = lax.all_to_all(taps_t, "ctx", 0, 0, tiled=True)

    with jax.named_scope("input_projection"):
        inputs_t = chan_gather(inputs.T, 0)
        w_flat = w_in.reshape(w_in.shape[0], 3 * width_dev)
        proj_t = lax.dot_general(
            w_flat, inputs_t, (((0,), (0,)), ((), ())), preferred_element_type=jnp.float32
        ).astype(jnp.bfloat16)

    with jax.named_scope("projection_to_owner"):
        proj_t = proj_t.reshape(3, groups, own, span_len)
        proj_t = lax.all_to_all(proj_t, "ctx", 1, 1, tiled=True)

    with jax.named_scope("short_conv"):
        start = position * own
        taps = lax.dynamic_slice_in_dim(conv_taps, start, own, axis=2)
        rim = jnp.pad(proj_t[:, :-1, :, span_len - (KERNEL - 1) :], ((0, 0), (1, 0), (0, 0), (0, 0)))
        padded = jnp.concatenate([rim, proj_t], 3)
        filtered = jnp.zeros(proj_t.shape, jnp.float32)
        for lag in range(KERNEL):
            start_row = KERNEL - 1 - lag
            filtered = filtered + taps[lag].astype(jnp.float32)[:, None, :, None] * padded[
                ..., start_row : start_row + span_len
            ].astype(jnp.float32)
        streams = filtered.astype(jnp.bfloat16)
        gate_out = streams[0]
        gated_in = (streams[1].astype(jnp.float32) * streams[2].astype(jnp.float32)).astype(
            jnp.bfloat16
        )

    with jax.named_scope("spectra"):
        table = dft_table(double_len)
        forward_in = table[:, :span_len]
        spectra_in = jnp.einsum(
            "jdb,fb->jdf", gated_in, forward_in, preferred_element_type=jnp.float32
        ).astype(jnp.bfloat16)
        previous = jnp.pad(taps_t[:-1, :, 1:], ((1, 0), (0, 0), (0, 0)))
        padded_taps = jnp.concatenate(
            [taps_t, jnp.zeros((groups, own, 1), jnp.bfloat16), previous], 2
        )
        spectra_taps = jnp.einsum(
            "kdm,fm->kdf", padded_taps, table, preferred_element_type=jnp.float32
        ).astype(jnp.bfloat16)

    with jax.named_scope("mixture"):
        real_g = spectra_taps[:, :, :double_len].astype(jnp.float32)
        imag_g = spectra_taps[:, :, double_len:].astype(jnp.float32)
        real_u = spectra_in[:, :, :double_len].astype(jnp.float32)
        imag_u = spectra_in[:, :, double_len:].astype(jnp.float32)
        mixed = []
        for target in range(groups):
            acc_r = jnp.zeros((own, double_len), jnp.float32)
            acc_i = jnp.zeros((own, double_len), jnp.float32)
            for source in range(target + 1):
                lag = target - source
                acc_r = acc_r + (real_g[lag] * real_u[source] - imag_g[lag] * imag_u[source])
                acc_i = acc_i + (real_g[lag] * imag_u[source] + imag_g[lag] * real_u[source])
            mixed.append(jnp.concatenate([acc_r, acc_i], 1))
        mixture = jnp.stack(mixed, 0).astype(jnp.bfloat16)

    with jax.named_scope("inverse_and_gate"):
        long_out = jnp.einsum(
            "idf,fa->ida", mixture, forward_in, preferred_element_type=jnp.float32
        ) * (1.0 / double_len)
        gain = lax.dynamic_slice_in_dim(skip_gain, start, own)
        long_out = long_out + gain[None, :, None] * gated_in.astype(jnp.float32)
        gated_out = (gate_out.astype(jnp.float32) * long_out).astype(jnp.bfloat16)

    with jax.named_scope("gated_back_to_rows"):
        gated_out = lax.all_to_all(gated_out, "ctx", 0, 0, tiled=True)
        gated_out = gated_out.reshape(width_dev, span_len)

    with jax.named_scope("output_projection"):
        gathered = chan_gather(gated_out, 1)
        result = lax.dot_general(
            gathered, w_cols, (((0,), (0,)), ((), ())), preferred_element_type=jnp.float32
        ).astype(jnp.bfloat16)
    return result


def solution(mesh):
    return jax.shard_map(
        body,
        mesh=mesh,
        in_specs=(
            P("ctx", "chan"),
            P(None, None, "chan"),
            P(None, None, "chan"),
            P("chan"),
            P("ctx", "chan"),
            P("chan", None),
        ),
        out_specs=P("ctx", "chan"),
        check_vma=False,
    )
```

```python
import math

import functools

import jax
import jax.numpy as jnp
from jax import lax
from jax.experimental import pallas as pl
from jax.experimental.pallas import tpu as pltpu
from jax.sharding import PartitionSpec as P

KERNEL = 3
MESH = pl.DeviceIdType.MESH
PER_Z = 4


def gather_kernel(chips, x_ref, out_ref, local_sem, cross_send, cross_recv, ring_send, ring_recv,
                  sib_send, sib_recv):
    row = lax.axis_index("ctx")
    me = lax.axis_index("chan")
    z = me // PER_Z
    y_lo = (me // 2) % 2
    core = me % 2
    way = 1 - 2 * core
    after = ((z + way + chips) % chips) * PER_Z + y_lo * 2 + core
    before = ((z - way + chips) % chips) * PER_Z + y_lo * 2 + core
    sibling = me + 1 - 2 * core
    across = me + 2 - 4 * y_lo
    diagonal = across + 1 - 2 * core
    partners = (sibling, across, diagonal)

    barrier = pltpu.get_barrier_semaphore()
    for peer in partners + (after, before):
        pl.semaphore_signal(barrier, inc=1, device_id=(row, peer), device_id_type=MESH)
    pl.semaphore_wait(barrier, 5)

    local = pltpu.make_async_copy(x_ref, out_ref.at[me], local_sem)
    local.start()

    def cross(k, peer, slot):
        return pltpu.make_async_remote_copy(
            src_ref=x_ref, dst_ref=out_ref.at[slot], send_sem=cross_send.at[k],
            recv_sem=cross_recv.at[k], device_id=(row, peer), device_id_type=MESH)

    for k, peer in enumerate(partners):
        cross(k, peer, me).start()
    local.wait()
    for k, peer in enumerate(partners):
        cross(k, peer, me).wait_send()
        cross(k, peer, peer).wait_recv()

    def group(chip):
        return out_ref.at[pl.ds(pl.multiple_of(chip * PER_Z, PER_Z), PER_Z)]

    def ring(s, chip):
        return pltpu.make_async_remote_copy(
            src_ref=group(chip), dst_ref=group(chip), send_sem=ring_send.at[s],
            recv_sem=ring_recv.at[s], device_id=(row, after), device_id_type=MESH)

    def sib(s, chip):
        return pltpu.make_async_remote_copy(
            src_ref=group(chip), dst_ref=group(chip), send_sem=sib_send.at[s],
            recv_sem=sib_recv.at[s], device_id=(row, sibling), device_id_type=MESH)

    longest = chips // 2
    for s in range(longest):
        active = jnp.logical_or(core == 0, s < chips - 1 - longest)
        sent = (z - way * s + chips) % chips
        got = (z - way * (s + 1) + chips) % chips

        @pl.when(active)
        def _():
            ring(s, sent).start()
            ring(s, got).wait_recv()
            sib(s, got).start()

    for s in range(longest):
        active = jnp.logical_or(core == 0, s < chips - 1 - longest)
        sent = (z - way * s + chips) % chips
        got = (z - way * (s + 1) + chips) % chips
        other = jnp.logical_or(core == 1, s < chips - 1 - longest)
        theirs = (z + way * (s + 1) + chips) % chips

        @pl.when(active)
        def _():
            ring(s, sent).wait_send()
            sib(s, got).wait_send()

        @pl.when(other)
        def _():
            sib(s, theirs).wait_recv()


def exchange_kernel(groups, x_ref, out_ref, local_sem, send_sem, recv_sem):
    me = lax.axis_index("ctx")
    col = lax.axis_index("chan")
    barrier = pltpu.get_barrier_semaphore()
    for k in range(1, groups):
        pl.semaphore_signal(barrier, inc=1, device_id=((me + k) % groups, col),
                            device_id_type=MESH)
    pl.semaphore_wait(barrier, groups - 1)

    local = pltpu.make_async_copy(x_ref.at[me], out_ref.at[me], local_sem)
    local.start()

    def send(k, peer, slot):
        return pltpu.make_async_remote_copy(
            src_ref=x_ref.at[peer], dst_ref=out_ref.at[slot], send_sem=send_sem.at[k - 1],
            recv_sem=recv_sem.at[k - 1], device_id=(peer, col), device_id_type=MESH)

    for k in range(1, groups):
        send(k, (me + k) % groups, me).start()
    local.wait()
    for k in range(1, groups):
        send(k, (me + k) % groups, me).wait_send()
        source = (me - k + groups) % groups
        send(k, source, source).wait_recv()


def ctx_exchange(x, collective_id):
    groups = lax.axis_size("ctx")
    return pl.pallas_call(
        functools.partial(exchange_kernel, groups),
        out_shape=jax.ShapeDtypeStruct(x.shape, x.dtype),
        in_specs=[pl.BlockSpec(memory_space=pltpu.VMEM)],
        out_specs=pl.BlockSpec(memory_space=pltpu.VMEM),
        scratch_shapes=[
            pltpu.SemaphoreType.DMA(()),
            pltpu.SemaphoreType.DMA((groups - 1,)),
            pltpu.SemaphoreType.DMA((groups - 1,)),
        ],
        compiler_params=pltpu.CompilerParams(collective_id=collective_id, has_side_effects=True),
    )(x)


def chan_gather(x, collective_id):
    size = lax.axis_size("chan")
    chips = size // PER_Z
    longest = chips // 2
    return pl.pallas_call(
        functools.partial(gather_kernel, chips),
        out_shape=jax.ShapeDtypeStruct((size,) + x.shape, x.dtype),
        in_specs=[pl.BlockSpec(memory_space=pltpu.VMEM)],
        out_specs=pl.BlockSpec(memory_space=pltpu.VMEM),
        scratch_shapes=[
            pltpu.SemaphoreType.DMA(()),
            pltpu.SemaphoreType.DMA((3,)),
            pltpu.SemaphoreType.DMA((3,)),
            pltpu.SemaphoreType.DMA((longest,)),
            pltpu.SemaphoreType.DMA((longest,)),
            pltpu.SemaphoreType.DMA((longest,)),
            pltpu.SemaphoreType.DMA((longest,)),
        ],
        compiler_params=pltpu.CompilerParams(collective_id=collective_id, has_side_effects=True),
    )(x).reshape(size * x.shape[0], x.shape[1])


def dft_table(double_len):
    step = 32
    hi_ids = jnp.arange(double_len // step, dtype=jnp.int32)[:, None]
    lo_ids = jnp.arange(step, dtype=jnp.int32)[:, None]
    cols = jnp.arange(double_len, dtype=jnp.int32)[None, :]
    scale = 2.0 * math.pi / double_len
    hi_angle = scale * (hi_ids * step * cols % double_len).astype(jnp.float32)
    lo_angle = scale * (lo_ids * cols % double_len).astype(jnp.float32)
    hc, hs = jnp.cos(hi_angle)[:, None], jnp.sin(hi_angle)[:, None]
    lc, ls = jnp.cos(lo_angle)[None], jnp.sin(lo_angle)[None]
    cos = (hc * lc - hs * ls).reshape(double_len, double_len)
    sin = (hs * lc + hc * ls).reshape(double_len, double_len)
    return jnp.concatenate([cos, -sin], 0).astype(jnp.bfloat16)


def body(inputs, w_in, conv_taps, skip_gain, filter_taps, w_out):
    span_len, width_dev = inputs.shape
    double_len = 2 * span_len
    groups = lax.axis_size("ctx")
    position = lax.axis_index("ctx")
    own = width_dev // groups

    with jax.named_scope("out_weight_columns"):
        w_cols = lax.all_to_all(w_out, "chan", 1, 0, tiled=True)

    with jax.named_scope("filter_to_owner"):
        taps_t = filter_taps.T.reshape(groups, own, span_len)
        taps_t = ctx_exchange(taps_t, 2)

    with jax.named_scope("input_projection"):
        inputs_t = chan_gather(inputs.T, 0)
        w_flat = w_in.reshape(w_in.shape[0], 3 * width_dev)
        proj_t = lax.dot_general(
            w_flat, inputs_t, (((0,), (0,)), ((), ())), preferred_element_type=jnp.float32
        ).astype(jnp.bfloat16)

    with jax.named_scope("projection_to_owner"):
        proj_t = proj_t.reshape(3, groups, own, span_len).transpose(1, 0, 2, 3)
        proj_t = ctx_exchange(proj_t, 3)

    with jax.named_scope("short_conv"):
        start = position * own
        taps = lax.dynamic_slice_in_dim(conv_taps, start, own, axis=2)
        rim = jnp.pad(proj_t[:-1, :, :, span_len - (KERNEL - 1) :], ((1, 0), (0, 0), (0, 0), (0, 0)))
        padded = jnp.concatenate([rim, proj_t], 3)
        filtered = jnp.zeros(proj_t.shape, jnp.float32)
        for lag in range(KERNEL):
            start_row = KERNEL - 1 - lag
            filtered = filtered + taps[lag].astype(jnp.float32)[None, :, :, None] * padded[
                ..., start_row : start_row + span_len
            ].astype(jnp.float32)
        streams = filtered.astype(jnp.bfloat16)
        gate_out = streams[:, 0]
        gated_in = (streams[:, 1].astype(jnp.float32) * streams[:, 2].astype(jnp.float32)).astype(
            jnp.bfloat16
        )

    with jax.named_scope("spectra"):
        table = dft_table(double_len)
        forward_in = table[:, :span_len]
        spectra_in = jnp.einsum(
            "jdb,fb->jdf", gated_in, forward_in, preferred_element_type=jnp.float32
        ).astype(jnp.bfloat16)
        previous = jnp.pad(taps_t[:-1, :, 1:], ((1, 0), (0, 0), (0, 0)))
        padded_taps = jnp.concatenate(
            [taps_t, jnp.zeros((groups, own, 1), jnp.bfloat16), previous], 2
        )
        spectra_taps = jnp.einsum(
            "kdm,fm->kdf", padded_taps, table, preferred_element_type=jnp.float32
        ).astype(jnp.bfloat16)

    with jax.named_scope("mixture"):
        real_g = spectra_taps[:, :, :double_len].astype(jnp.float32)
        imag_g = spectra_taps[:, :, double_len:].astype(jnp.float32)
        real_u = spectra_in[:, :, :double_len].astype(jnp.float32)
        imag_u = spectra_in[:, :, double_len:].astype(jnp.float32)
        mixed = []
        for target in range(groups):
            acc_r = jnp.zeros((own, double_len), jnp.float32)
            acc_i = jnp.zeros((own, double_len), jnp.float32)
            for source in range(target + 1):
                lag = target - source
                acc_r = acc_r + (real_g[lag] * real_u[source] - imag_g[lag] * imag_u[source])
                acc_i = acc_i + (real_g[lag] * imag_u[source] + imag_g[lag] * real_u[source])
            mixed.append(jnp.concatenate([acc_r, acc_i], 1))
        mixture = jnp.stack(mixed, 0).astype(jnp.bfloat16)

    with jax.named_scope("inverse_and_gate"):
        long_out = jnp.einsum(
            "idf,fa->ida", mixture, forward_in, preferred_element_type=jnp.float32
        ) * (1.0 / double_len)
        gain = lax.dynamic_slice_in_dim(skip_gain, start, own)
        long_out = long_out + gain[None, :, None] * gated_in.astype(jnp.float32)
        gated_out = (gate_out.astype(jnp.float32) * long_out).astype(jnp.bfloat16)

    with jax.named_scope("gated_back_to_rows"):
        gated_out = ctx_exchange(gated_out, 4)
        gated_out = gated_out.reshape(width_dev, span_len)

    with jax.named_scope("output_projection"):
        gathered = chan_gather(gated_out, 1)
        result = lax.dot_general(
            gathered, w_cols, (((0,), (0,)), ((), ())), preferred_element_type=jnp.float32
        ).astype(jnp.bfloat16)
    return result


def solution(mesh):
    return jax.shard_map(
        body,
        mesh=mesh,
        in_specs=(
            P("ctx", "chan"),
            P(None, None, "chan"),
            P(None, None, "chan"),
            P("chan"),
            P("ctx", "chan"),
            P("chan", None),
        ),
        out_specs=P("ctx", "chan"),
        check_vma=False,
    )
```

```python
import math

import functools

import jax
import jax.numpy as jnp
from jax import lax
from jax.experimental import pallas as pl
from jax.experimental.pallas import tpu as pltpu
from jax.sharding import PartitionSpec as P

KERNEL = 3
MESH = pl.DeviceIdType.MESH
PER_Z = 4


def gather_kernel(chips, groups, *refs):
    if groups:
        (x_ref, t_ref, out_ref, t_out_ref, local_sem, cross_send, cross_recv, ring_send, ring_recv,
         sib_send, sib_recv, t_local_sem, t_send, t_recv) = refs
    else:
        (x_ref, out_ref, local_sem, cross_send, cross_recv, ring_send, ring_recv,
         sib_send, sib_recv) = refs
    row = lax.axis_index("ctx")
    me = lax.axis_index("chan")
    z = me // PER_Z
    y_lo = (me // 2) % 2
    core = me % 2
    way = 1 - 2 * core
    after = ((z + way + chips) % chips) * PER_Z + y_lo * 2 + core
    before = ((z - way + chips) % chips) * PER_Z + y_lo * 2 + core
    sibling = me + 1 - 2 * core
    across = me + 2 - 4 * y_lo
    diagonal = across + 1 - 2 * core
    partners = (sibling, across, diagonal)

    barrier = pltpu.get_barrier_semaphore()
    for peer in partners + (after, before):
        pl.semaphore_signal(barrier, inc=1, device_id=(row, peer), device_id_type=MESH)
    for peer in ctx_peers(groups) if groups else ():
        pl.semaphore_signal(barrier, inc=1, device_id=(peer, me), device_id_type=MESH)
    pl.semaphore_wait(barrier, 5 + max(groups - 1, 0))

    if groups:
        t_local, t_sends, t_receipts = exchange_copies(
            groups, t_ref, t_out_ref, t_local_sem, t_send, t_recv)
        t_local.start()
        for copy in t_sends:
            copy.start()

    local = pltpu.make_async_copy(x_ref, out_ref.at[me], local_sem)
    local.start()

    def cross(k, peer, slot):
        return pltpu.make_async_remote_copy(
            src_ref=x_ref, dst_ref=out_ref.at[slot], send_sem=cross_send.at[k],
            recv_sem=cross_recv.at[k], device_id=(row, peer), device_id_type=MESH)

    for k, peer in enumerate(partners):
        cross(k, peer, me).start()
    local.wait()
    for k, peer in enumerate(partners):
        cross(k, peer, me).wait_send()
        cross(k, peer, peer).wait_recv()

    def group(chip):
        return out_ref.at[pl.ds(pl.multiple_of(chip * PER_Z, PER_Z), PER_Z)]

    def ring(s, chip):
        return pltpu.make_async_remote_copy(
            src_ref=group(chip), dst_ref=group(chip), send_sem=ring_send.at[s],
            recv_sem=ring_recv.at[s], device_id=(row, after), device_id_type=MESH)

    def sib(s, chip):
        return pltpu.make_async_remote_copy(
            src_ref=group(chip), dst_ref=group(chip), send_sem=sib_send.at[s],
            recv_sem=sib_recv.at[s], device_id=(row, sibling), device_id_type=MESH)

    longest = chips // 2
    for s in range(longest):
        active = jnp.logical_or(core == 0, s < chips - 1 - longest)
        sent = (z - way * s + chips) % chips
        got = (z - way * (s + 1) + chips) % chips

        @pl.when(active)
        def _():
            ring(s, sent).start()
            ring(s, got).wait_recv()
            sib(s, got).start()

    for s in range(longest):
        active = jnp.logical_or(core == 0, s < chips - 1 - longest)
        sent = (z - way * s + chips) % chips
        got = (z - way * (s + 1) + chips) % chips
        other = jnp.logical_or(core == 1, s < chips - 1 - longest)
        theirs = (z + way * (s + 1) + chips) % chips

        @pl.when(active)
        def _():
            ring(s, sent).wait_send()
            sib(s, got).wait_send()

        @pl.when(other)
        def _():
            sib(s, theirs).wait_recv()

    if groups:
        t_local.wait()
        for copy, receipt in zip(t_sends, t_receipts):
            copy.wait_send()
            receipt.wait_recv()


def exchange_copies(groups, x_ref, out_ref, local_sem, send_sem, recv_sem):
    me = lax.axis_index("ctx")
    col = lax.axis_index("chan")
    local = pltpu.make_async_copy(x_ref.at[me], out_ref.at[me], local_sem)

    def send(k, peer, slot):
        return pltpu.make_async_remote_copy(
            src_ref=x_ref.at[peer], dst_ref=out_ref.at[slot], send_sem=send_sem.at[k - 1],
            recv_sem=recv_sem.at[k - 1], device_id=(peer, col), device_id_type=MESH)

    sends = [send(k, (me + k) % groups, me) for k in range(1, groups)]
    sources = [(me - k + groups) % groups for k in range(1, groups)]
    receipts = [send(k, source, source) for k, source in zip(range(1, groups), sources)]
    return local, sends, receipts


def ctx_peers(groups):
    me = lax.axis_index("ctx")
    return [(me + k) % groups for k in range(1, groups)]


def exchange_kernel(groups, x_ref, out_ref, local_sem, send_sem, recv_sem):
    col = lax.axis_index("chan")
    barrier = pltpu.get_barrier_semaphore()
    for peer in ctx_peers(groups):
        pl.semaphore_signal(barrier, inc=1, device_id=(peer, col), device_id_type=MESH)
    pl.semaphore_wait(barrier, groups - 1)
    local, sends, receipts = exchange_copies(groups, x_ref, out_ref, local_sem, send_sem, recv_sem)
    local.start()
    for copy in sends:
        copy.start()
    local.wait()
    for copy, receipt in zip(sends, receipts):
        copy.wait_send()
        receipt.wait_recv()


def ctx_exchange(x, collective_id):
    groups = lax.axis_size("ctx")
    return pl.pallas_call(
        functools.partial(exchange_kernel, groups),
        out_shape=jax.ShapeDtypeStruct(x.shape, x.dtype),
        in_specs=[pl.BlockSpec(memory_space=pltpu.VMEM)],
        out_specs=pl.BlockSpec(memory_space=pltpu.VMEM),
        scratch_shapes=[
            pltpu.SemaphoreType.DMA(()),
            pltpu.SemaphoreType.DMA((groups - 1,)),
            pltpu.SemaphoreType.DMA((groups - 1,)),
        ],
        compiler_params=pltpu.CompilerParams(collective_id=collective_id, has_side_effects=True),
    )(x)


def chan_gather(x, t, collective_id):
    size = lax.axis_size("chan")
    groups = lax.axis_size("ctx") if t is not None else 0
    chips = size // PER_Z
    longest = chips // 2
    operands = (x,) if t is None else (x, t)
    out_shape = [jax.ShapeDtypeStruct((size,) + x.shape, x.dtype)]
    scratch = [
        pltpu.SemaphoreType.DMA(()),
        pltpu.SemaphoreType.DMA((3,)),
        pltpu.SemaphoreType.DMA((3,)),
        pltpu.SemaphoreType.DMA((longest,)),
        pltpu.SemaphoreType.DMA((longest,)),
        pltpu.SemaphoreType.DMA((longest,)),
        pltpu.SemaphoreType.DMA((longest,)),
    ]
    if t is not None:
        out_shape.append(jax.ShapeDtypeStruct(t.shape, t.dtype))
        scratch += [
            pltpu.SemaphoreType.DMA(()),
            pltpu.SemaphoreType.DMA((groups - 1,)),
            pltpu.SemaphoreType.DMA((groups - 1,)),
        ]
    outs = pl.pallas_call(
        functools.partial(gather_kernel, chips, groups),
        out_shape=tuple(out_shape),
        in_specs=[pl.BlockSpec(memory_space=pltpu.VMEM)] * len(operands),
        out_specs=[pl.BlockSpec(memory_space=pltpu.VMEM)] * len(out_shape),
        scratch_shapes=scratch,
        compiler_params=pltpu.CompilerParams(collective_id=collective_id, has_side_effects=True),
    )(*operands)
    gathered = outs[0].reshape(size * x.shape[0], x.shape[1])
    return gathered if t is None else (gathered, outs[1])


def dft_table(double_len):
    step = 32
    hi_ids = jnp.arange(double_len // step, dtype=jnp.int32)[:, None]
    lo_ids = jnp.arange(step, dtype=jnp.int32)[:, None]
    cols = jnp.arange(double_len, dtype=jnp.int32)[None, :]
    scale = 2.0 * math.pi / double_len
    hi_angle = scale * (hi_ids * step * cols % double_len).astype(jnp.float32)
    lo_angle = scale * (lo_ids * cols % double_len).astype(jnp.float32)
    hc, hs = jnp.cos(hi_angle)[:, None], jnp.sin(hi_angle)[:, None]
    lc, ls = jnp.cos(lo_angle)[None], jnp.sin(lo_angle)[None]
    cos = (hc * lc - hs * ls).reshape(double_len, double_len)
    sin = (hs * lc + hc * ls).reshape(double_len, double_len)
    return jnp.concatenate([cos, -sin], 0).astype(jnp.bfloat16)


def body(inputs, w_in, conv_taps, skip_gain, filter_taps, w_out):
    span_len, width_dev = inputs.shape
    double_len = 2 * span_len
    groups = lax.axis_size("ctx")
    position = lax.axis_index("ctx")
    own = width_dev // groups

    with jax.named_scope("input_gather_and_filter_to_owner"):
        taps_t = filter_taps.T.reshape(groups, own, span_len)
        inputs_t, taps_t = chan_gather(inputs.T, taps_t, 0)

    with jax.named_scope("out_weight_columns"):
        w_late, inputs_t = lax.optimization_barrier((w_out, inputs_t))
        w_cols = lax.all_to_all(w_late, "chan", 1, 0, tiled=True)

    with jax.named_scope("input_projection"):
        w_flat = w_in.reshape(w_in.shape[0], 3 * width_dev)
        proj_t = lax.dot_general(
            w_flat, inputs_t, (((0,), (0,)), ((), ())), preferred_element_type=jnp.float32
        ).astype(jnp.bfloat16)

    with jax.named_scope("projection_to_owner"):
        proj_t = proj_t.reshape(3, groups, own, span_len).transpose(1, 0, 2, 3)
        proj_t = ctx_exchange(proj_t, 3)

    with jax.named_scope("short_conv"):
        start = position * own
        taps = lax.dynamic_slice_in_dim(conv_taps, start, own, axis=2)
        rim = jnp.pad(proj_t[:-1, :, :, span_len - (KERNEL - 1) :], ((1, 0), (0, 0), (0, 0), (0, 0)))
        padded = jnp.concatenate([rim, proj_t], 3)
        filtered = jnp.zeros(proj_t.shape, jnp.float32)
        for lag in range(KERNEL):
            start_row = KERNEL - 1 - lag
            filtered = filtered + taps[lag].astype(jnp.float32)[None, :, :, None] * padded[
                ..., start_row : start_row + span_len
            ].astype(jnp.float32)
        streams = filtered.astype(jnp.bfloat16)
        gate_out = streams[:, 0]
        gated_in = (streams[:, 1].astype(jnp.float32) * streams[:, 2].astype(jnp.float32)).astype(
            jnp.bfloat16
        )

    with jax.named_scope("spectra"):
        w_cols, gated_in = lax.optimization_barrier((w_cols, gated_in))
        table = dft_table(double_len)
        forward_in = table[:, :span_len]
        spectra_in = jnp.einsum(
            "jdb,fb->jdf", gated_in, forward_in, preferred_element_type=jnp.float32
        ).astype(jnp.bfloat16)
        previous = jnp.pad(taps_t[:-1, :, 1:], ((1, 0), (0, 0), (0, 0)))
        padded_taps = jnp.concatenate(
            [taps_t, jnp.zeros((groups, own, 1), jnp.bfloat16), previous], 2
        )
        spectra_taps = jnp.einsum(
            "kdm,fm->kdf", padded_taps, table, preferred_element_type=jnp.float32
        ).astype(jnp.bfloat16)

    with jax.named_scope("mixture"):
        real_g = spectra_taps[:, :, :double_len].astype(jnp.float32)
        imag_g = spectra_taps[:, :, double_len:].astype(jnp.float32)
        real_u = spectra_in[:, :, :double_len].astype(jnp.float32)
        imag_u = spectra_in[:, :, double_len:].astype(jnp.float32)
        mixed = []
        for target in range(groups):
            acc_r = jnp.zeros((own, double_len), jnp.float32)
            acc_i = jnp.zeros((own, double_len), jnp.float32)
            for source in range(target + 1):
                lag = target - source
                acc_r = acc_r + (real_g[lag] * real_u[source] - imag_g[lag] * imag_u[source])
                acc_i = acc_i + (real_g[lag] * imag_u[source] + imag_g[lag] * real_u[source])
            mixed.append(jnp.concatenate([acc_r, acc_i], 1))
        mixture = jnp.stack(mixed, 0).astype(jnp.bfloat16)

    with jax.named_scope("inverse_and_gate"):
        long_out = jnp.einsum(
            "idf,fa->ida", mixture, forward_in, preferred_element_type=jnp.float32
        ) * (1.0 / double_len)
        gain = lax.dynamic_slice_in_dim(skip_gain, start, own)
        long_out = long_out + gain[None, :, None] * gated_in.astype(jnp.float32)
        gated_out = (gate_out.astype(jnp.float32) * long_out).astype(jnp.bfloat16)

    with jax.named_scope("gated_back_to_rows"):
        gated_out = ctx_exchange(gated_out, 4)
        gated_out = gated_out.reshape(width_dev, span_len)

    with jax.named_scope("output_projection"):
        gathered = chan_gather(gated_out, None, 1)
        result = lax.dot_general(
            gathered, w_cols, (((0,), (0,)), ((), ())), preferred_element_type=jnp.float32
        ).astype(jnp.bfloat16)
    return result


def solution(mesh):
    return jax.shard_map(
        body,
        mesh=mesh,
        in_specs=(
            P("ctx", "chan"),
            P(None, None, "chan"),
            P(None, None, "chan"),
            P("chan"),
            P("ctx", "chan"),
            P("chan", None),
        ),
        out_specs=P("ctx", "chan"),
        check_vma=False,
    )
```

```python
import math

import functools

import jax
import jax.numpy as jnp
from jax import lax
from jax.experimental import pallas as pl
from jax.experimental.pallas import tpu as pltpu
from jax.sharding import PartitionSpec as P

KERNEL = 3
MESH = pl.DeviceIdType.MESH
PER_Z = 4


def gather_kernel(chips, groups, *refs):
    if groups:
        (x_ref, t_ref, out_ref, t_out_ref, local_sem, cross_send, cross_recv, ring_send, ring_recv,
         sib_send, sib_recv, t_local_sem, t_send, t_recv) = refs
    else:
        (x_ref, out_ref, local_sem, cross_send, cross_recv, ring_send, ring_recv,
         sib_send, sib_recv) = refs
    row = lax.axis_index("ctx")
    me = lax.axis_index("chan")
    z = me // PER_Z
    y_lo = (me // 2) % 2
    core = me % 2
    way = 1 - 2 * core
    after = ((z + way + chips) % chips) * PER_Z + y_lo * 2 + core
    before = ((z - way + chips) % chips) * PER_Z + y_lo * 2 + core
    sibling = me + 1 - 2 * core
    across = me + 2 - 4 * y_lo
    diagonal = across + 1 - 2 * core
    partners = (sibling, across, diagonal)

    barrier = pltpu.get_barrier_semaphore()
    for peer in partners + (after, before):
        pl.semaphore_signal(barrier, inc=1, device_id=(row, peer), device_id_type=MESH)
    for peer in ctx_peers(groups) if groups else ():
        pl.semaphore_signal(barrier, inc=1, device_id=(peer, me), device_id_type=MESH)
    pl.semaphore_wait(barrier, 5 + max(groups - 1, 0))

    if groups:
        t_local, t_sends, t_receipts = exchange_copies(
            groups, t_ref, t_out_ref, t_local_sem, t_send, t_recv)
        t_local.start()
        for copy in t_sends:
            copy.start()

    local = pltpu.make_async_copy(x_ref, out_ref.at[me], local_sem)
    local.start()

    def cross(k, peer, slot):
        return pltpu.make_async_remote_copy(
            src_ref=x_ref, dst_ref=out_ref.at[slot], send_sem=cross_send.at[k],
            recv_sem=cross_recv.at[k], device_id=(row, peer), device_id_type=MESH)

    for k, peer in enumerate(partners):
        cross(k, peer, me).start()
    local.wait()
    for k, peer in enumerate(partners):
        cross(k, peer, me).wait_send()
        cross(k, peer, peer).wait_recv()

    def group(chip):
        return out_ref.at[pl.ds(pl.multiple_of(chip * PER_Z, PER_Z), PER_Z)]

    def ring(s, chip):
        return pltpu.make_async_remote_copy(
            src_ref=group(chip), dst_ref=group(chip), send_sem=ring_send.at[s],
            recv_sem=ring_recv.at[s], device_id=(row, after), device_id_type=MESH)

    def sib(s, chip):
        return pltpu.make_async_remote_copy(
            src_ref=group(chip), dst_ref=group(chip), send_sem=sib_send.at[s],
            recv_sem=sib_recv.at[s], device_id=(row, sibling), device_id_type=MESH)

    longest = chips // 2
    for s in range(longest):
        active = jnp.logical_or(core == 0, s < chips - 1 - longest)
        sent = (z - way * s + chips) % chips
        got = (z - way * (s + 1) + chips) % chips

        @pl.when(active)
        def _():
            ring(s, sent).start()
            ring(s, got).wait_recv()
            sib(s, got).start()

    for s in range(longest):
        active = jnp.logical_or(core == 0, s < chips - 1 - longest)
        sent = (z - way * s + chips) % chips
        got = (z - way * (s + 1) + chips) % chips
        other = jnp.logical_or(core == 1, s < chips - 1 - longest)
        theirs = (z + way * (s + 1) + chips) % chips

        @pl.when(active)
        def _():
            ring(s, sent).wait_send()
            sib(s, got).wait_send()

        @pl.when(other)
        def _():
            sib(s, theirs).wait_recv()

    if groups:
        t_local.wait()
        for copy, receipt in zip(t_sends, t_receipts):
            copy.wait_send()
            receipt.wait_recv()


def exchange_copies(groups, x_ref, out_ref, local_sem, send_sem, recv_sem):
    me = lax.axis_index("ctx")
    col = lax.axis_index("chan")
    local = pltpu.make_async_copy(x_ref.at[me], out_ref.at[me], local_sem)

    def send(k, peer, slot):
        return pltpu.make_async_remote_copy(
            src_ref=x_ref.at[peer], dst_ref=out_ref.at[slot], send_sem=send_sem.at[k - 1],
            recv_sem=recv_sem.at[k - 1], device_id=(peer, col), device_id_type=MESH)

    sends = [send(k, (me + k) % groups, me) for k in range(1, groups)]
    sources = [(me - k + groups) % groups for k in range(1, groups)]
    receipts = [send(k, source, source) for k, source in zip(range(1, groups), sources)]
    return local, sends, receipts


def ctx_peers(groups):
    me = lax.axis_index("ctx")
    return [(me + k) % groups for k in range(1, groups)]


def exchange_kernel(groups, x_ref, out_ref, local_sem, send_sem, recv_sem):
    col = lax.axis_index("chan")
    barrier = pltpu.get_barrier_semaphore()
    for peer in ctx_peers(groups):
        pl.semaphore_signal(barrier, inc=1, device_id=(peer, col), device_id_type=MESH)
    pl.semaphore_wait(barrier, groups - 1)
    local, sends, receipts = exchange_copies(groups, x_ref, out_ref, local_sem, send_sem, recv_sem)
    local.start()
    for copy in sends:
        copy.start()
    local.wait()
    for copy, receipt in zip(sends, receipts):
        copy.wait_send()
        receipt.wait_recv()


def ctx_exchange(x, collective_id):
    groups = lax.axis_size("ctx")
    return pl.pallas_call(
        functools.partial(exchange_kernel, groups),
        out_shape=jax.ShapeDtypeStruct(x.shape, x.dtype),
        in_specs=[pl.BlockSpec(memory_space=pltpu.VMEM)],
        out_specs=pl.BlockSpec(memory_space=pltpu.VMEM),
        scratch_shapes=[
            pltpu.SemaphoreType.DMA(()),
            pltpu.SemaphoreType.DMA((groups - 1,)),
            pltpu.SemaphoreType.DMA((groups - 1,)),
        ],
        compiler_params=pltpu.CompilerParams(collective_id=collective_id, has_side_effects=True),
    )(x)


def chan_gather(x, t, collective_id):
    size = lax.axis_size("chan")
    groups = lax.axis_size("ctx") if t is not None else 0
    chips = size // PER_Z
    longest = chips // 2
    operands = (x,) if t is None else (x, t)
    out_shape = [jax.ShapeDtypeStruct((size,) + x.shape, x.dtype)]
    scratch = [
        pltpu.SemaphoreType.DMA(()),
        pltpu.SemaphoreType.DMA((3,)),
        pltpu.SemaphoreType.DMA((3,)),
        pltpu.SemaphoreType.DMA((longest,)),
        pltpu.SemaphoreType.DMA((longest,)),
        pltpu.SemaphoreType.DMA((longest,)),
        pltpu.SemaphoreType.DMA((longest,)),
    ]
    if t is not None:
        out_shape.append(jax.ShapeDtypeStruct(t.shape, t.dtype))
        scratch += [
            pltpu.SemaphoreType.DMA(()),
            pltpu.SemaphoreType.DMA((groups - 1,)),
            pltpu.SemaphoreType.DMA((groups - 1,)),
        ]
    outs = pl.pallas_call(
        functools.partial(gather_kernel, chips, groups),
        out_shape=tuple(out_shape),
        in_specs=[pl.BlockSpec(memory_space=pltpu.VMEM)] * len(operands),
        out_specs=[pl.BlockSpec(memory_space=pltpu.VMEM)] * len(out_shape),
        scratch_shapes=scratch,
        compiler_params=pltpu.CompilerParams(collective_id=collective_id, has_side_effects=True),
    )(*operands)
    gathered = outs[0].reshape(size * x.shape[0], x.shape[1])
    return gathered if t is None else (gathered, outs[1])


def dft_table(double_len):
    step = 32
    hi_ids = jnp.arange(double_len // step, dtype=jnp.int32)[:, None]
    lo_ids = jnp.arange(step, dtype=jnp.int32)[:, None]
    cols = jnp.arange(double_len, dtype=jnp.int32)[None, :]
    scale = 2.0 * math.pi / double_len
    hi_angle = scale * (hi_ids * step * cols % double_len).astype(jnp.float32)
    lo_angle = scale * (lo_ids * cols % double_len).astype(jnp.float32)
    hc, hs = jnp.cos(hi_angle)[:, None], jnp.sin(hi_angle)[:, None]
    lc, ls = jnp.cos(lo_angle)[None], jnp.sin(lo_angle)[None]
    cos = (hc * lc - hs * ls).reshape(double_len, double_len)
    sin = (hs * lc + hc * ls).reshape(double_len, double_len)
    return jnp.concatenate([cos, -sin], 0).astype(jnp.bfloat16)


def body(inputs, w_in, conv_taps, skip_gain, filter_taps, w_out):
    span_len, width_dev = inputs.shape
    double_len = 2 * span_len
    groups = lax.axis_size("ctx")
    position = lax.axis_index("ctx")
    own = width_dev // groups

    with jax.named_scope("input_gather_and_filter_to_owner"):
        taps_t = filter_taps.T.reshape(groups, own, span_len)
        inputs_t = inputs.T
        half = width_dev // 2
        by_offload = lax.all_gather(inputs_t[:half], "chan", axis=0, tiled=True)
        by_kernel, taps_t = chan_gather(inputs_t[half:], taps_t, 0)

    with jax.named_scope("out_weight_columns"):
        w_late, by_kernel = lax.optimization_barrier((w_out, by_kernel))
        w_cols = lax.all_to_all(w_late, "chan", 1, 0, tiled=True)

    with jax.named_scope("input_projection"):
        w_split = w_in.reshape(-1, width_dev, 3 * width_dev)
        proj_t = lax.dot_general(
            w_split[:, :half].reshape(-1, 3 * width_dev), by_offload, (((0,), (0,)), ((), ())),
            preferred_element_type=jnp.float32,
        ) + lax.dot_general(
            w_split[:, half:].reshape(-1, 3 * width_dev), by_kernel, (((0,), (0,)), ((), ())),
            preferred_element_type=jnp.float32,
        )
        proj_t = proj_t.astype(jnp.bfloat16)

    with jax.named_scope("projection_to_owner"):
        proj_t = proj_t.reshape(3, groups, own, span_len).transpose(1, 0, 2, 3)
        proj_t = ctx_exchange(proj_t, 3)

    with jax.named_scope("short_conv"):
        start = position * own
        taps = lax.dynamic_slice_in_dim(conv_taps, start, own, axis=2)
        rim = jnp.pad(proj_t[:-1, :, :, span_len - (KERNEL - 1) :], ((1, 0), (0, 0), (0, 0), (0, 0)))
        padded = jnp.concatenate([rim, proj_t], 3)
        filtered = jnp.zeros(proj_t.shape, jnp.float32)
        for lag in range(KERNEL):
            start_row = KERNEL - 1 - lag
            filtered = filtered + taps[lag].astype(jnp.float32)[None, :, :, None] * padded[
                ..., start_row : start_row + span_len
            ].astype(jnp.float32)
        streams = filtered.astype(jnp.bfloat16)
        gate_out = streams[:, 0]
        gated_in = (streams[:, 1].astype(jnp.float32) * streams[:, 2].astype(jnp.float32)).astype(
            jnp.bfloat16
        )

    with jax.named_scope("spectra"):
        w_cols, gated_in = lax.optimization_barrier((w_cols, gated_in))
        table = dft_table(double_len)
        forward_in = table[:, :span_len]
        spectra_in = jnp.einsum(
            "jdb,fb->jdf", gated_in, forward_in, preferred_element_type=jnp.float32
        ).astype(jnp.bfloat16)
        previous = jnp.pad(taps_t[:-1, :, 1:], ((1, 0), (0, 0), (0, 0)))
        padded_taps = jnp.concatenate(
            [taps_t, jnp.zeros((groups, own, 1), jnp.bfloat16), previous], 2
        )
        spectra_taps = jnp.einsum(
            "kdm,fm->kdf", padded_taps, table, preferred_element_type=jnp.float32
        ).astype(jnp.bfloat16)

    with jax.named_scope("mixture"):
        real_g = spectra_taps[:, :, :double_len].astype(jnp.float32)
        imag_g = spectra_taps[:, :, double_len:].astype(jnp.float32)
        real_u = spectra_in[:, :, :double_len].astype(jnp.float32)
        imag_u = spectra_in[:, :, double_len:].astype(jnp.float32)
        mixed = []
        for target in range(groups):
            acc_r = jnp.zeros((own, double_len), jnp.float32)
            acc_i = jnp.zeros((own, double_len), jnp.float32)
            for source in range(target + 1):
                lag = target - source
                acc_r = acc_r + (real_g[lag] * real_u[source] - imag_g[lag] * imag_u[source])
                acc_i = acc_i + (real_g[lag] * imag_u[source] + imag_g[lag] * real_u[source])
            mixed.append(jnp.concatenate([acc_r, acc_i], 1))
        mixture = jnp.stack(mixed, 0).astype(jnp.bfloat16)

    with jax.named_scope("inverse_and_gate"):
        long_out = jnp.einsum(
            "idf,fa->ida", mixture, forward_in, preferred_element_type=jnp.float32
        ) * (1.0 / double_len)
        gain = lax.dynamic_slice_in_dim(skip_gain, start, own)
        long_out = long_out + gain[None, :, None] * gated_in.astype(jnp.float32)
        gated_out = (gate_out.astype(jnp.float32) * long_out).astype(jnp.bfloat16)

    with jax.named_scope("gated_back_to_rows"):
        gated_out = ctx_exchange(gated_out, 4)
        gated_out = gated_out.reshape(width_dev, span_len)

    with jax.named_scope("output_projection"):
        gathered = chan_gather(gated_out, None, 1)
        result = lax.dot_general(
            gathered, w_cols, (((0,), (0,)), ((), ())), preferred_element_type=jnp.float32
        ).astype(jnp.bfloat16)
    return result


def solution(mesh):
    return jax.shard_map(
        body,
        mesh=mesh,
        in_specs=(
            P("ctx", "chan"),
            P(None, None, "chan"),
            P(None, None, "chan"),
            P("chan"),
            P("ctx", "chan"),
            P("chan", None),
        ),
        out_specs=P("ctx", "chan"),
        check_vma=False,
    )
```

```python
import math

import functools

import jax
import jax.numpy as jnp
from jax import lax
from jax.experimental import pallas as pl
from jax.experimental.pallas import tpu as pltpu
from jax.sharding import PartitionSpec as P

KERNEL = 3
MESH = pl.DeviceIdType.MESH
PER_Z = 4


def gather_kernel(chips, groups, *refs):
    if groups:
        (x_ref, t_ref, out_ref, t_out_ref, local_sem, cross_send, cross_recv, ring_send, ring_recv,
         sib_send, sib_recv, t_local_sem, t_send, t_recv) = refs
    else:
        (x_ref, out_ref, local_sem, cross_send, cross_recv, ring_send, ring_recv,
         sib_send, sib_recv) = refs
    row = lax.axis_index("ctx")
    me = lax.axis_index("chan")
    z = me // PER_Z
    y_lo = (me // 2) % 2
    core = me % 2
    way = 1 - 2 * core
    after = ((z + way + chips) % chips) * PER_Z + y_lo * 2 + core
    before = ((z - way + chips) % chips) * PER_Z + y_lo * 2 + core
    sibling = me + 1 - 2 * core
    across = me + 2 - 4 * y_lo
    diagonal = across + 1 - 2 * core
    partners = (sibling, across, diagonal)

    barrier = pltpu.get_barrier_semaphore()
    for peer in partners + (after, before):
        pl.semaphore_signal(barrier, inc=1, device_id=(row, peer), device_id_type=MESH)
    for peer in ctx_peers(groups) if groups else ():
        pl.semaphore_signal(barrier, inc=1, device_id=(peer, me), device_id_type=MESH)
    pl.semaphore_wait(barrier, 5 + max(groups - 1, 0))

    if groups:
        t_local, t_sends, t_receipts = exchange_copies(
            groups, t_ref, t_out_ref, t_local_sem, t_send, t_recv)
        t_local.start()
        for copy in t_sends:
            copy.start()

    local = pltpu.make_async_copy(x_ref, out_ref.at[me], local_sem)
    local.start()

    def cross(k, peer, slot):
        return pltpu.make_async_remote_copy(
            src_ref=x_ref, dst_ref=out_ref.at[slot], send_sem=cross_send.at[k],
            recv_sem=cross_recv.at[k], device_id=(row, peer), device_id_type=MESH)

    for k, peer in enumerate(partners):
        cross(k, peer, me).start()
    local.wait()
    for k, peer in enumerate(partners):
        cross(k, peer, me).wait_send()
        cross(k, peer, peer).wait_recv()

    def group(chip):
        return out_ref.at[pl.ds(pl.multiple_of(chip * PER_Z, PER_Z), PER_Z)]

    def ring(s, chip):
        return pltpu.make_async_remote_copy(
            src_ref=group(chip), dst_ref=group(chip), send_sem=ring_send.at[s],
            recv_sem=ring_recv.at[s], device_id=(row, after), device_id_type=MESH)

    def sib(s, chip):
        return pltpu.make_async_remote_copy(
            src_ref=group(chip), dst_ref=group(chip), send_sem=sib_send.at[s],
            recv_sem=sib_recv.at[s], device_id=(row, sibling), device_id_type=MESH)

    longest = chips // 2
    for s in range(longest):
        active = jnp.logical_or(core == 0, s < chips - 1 - longest)
        sent = (z - way * s + chips) % chips
        got = (z - way * (s + 1) + chips) % chips

        @pl.when(active)
        def _():
            ring(s, sent).start()
            ring(s, got).wait_recv()
            sib(s, got).start()

    for s in range(longest):
        active = jnp.logical_or(core == 0, s < chips - 1 - longest)
        sent = (z - way * s + chips) % chips
        got = (z - way * (s + 1) + chips) % chips
        other = jnp.logical_or(core == 1, s < chips - 1 - longest)
        theirs = (z + way * (s + 1) + chips) % chips

        @pl.when(active)
        def _():
            ring(s, sent).wait_send()
            sib(s, got).wait_send()

        @pl.when(other)
        def _():
            sib(s, theirs).wait_recv()

    if groups:
        t_local.wait()
        for copy, receipt in zip(t_sends, t_receipts):
            copy.wait_send()
            receipt.wait_recv()


def exchange_copies(groups, x_ref, out_ref, local_sem, send_sem, recv_sem):
    me = lax.axis_index("ctx")
    col = lax.axis_index("chan")
    local = pltpu.make_async_copy(x_ref.at[me], out_ref.at[me], local_sem)

    def send(k, peer, slot):
        return pltpu.make_async_remote_copy(
            src_ref=x_ref.at[peer], dst_ref=out_ref.at[slot], send_sem=send_sem.at[k - 1],
            recv_sem=recv_sem.at[k - 1], device_id=(peer, col), device_id_type=MESH)

    sends = [send(k, (me + k) % groups, me) for k in range(1, groups)]
    sources = [(me - k + groups) % groups for k in range(1, groups)]
    receipts = [send(k, source, source) for k, source in zip(range(1, groups), sources)]
    return local, sends, receipts


def ctx_peers(groups):
    me = lax.axis_index("ctx")
    return [(me + k) % groups for k in range(1, groups)]


def exchange_kernel(groups, x_ref, out_ref, local_sem, send_sem, recv_sem):
    col = lax.axis_index("chan")
    barrier = pltpu.get_barrier_semaphore()
    for peer in ctx_peers(groups):
        pl.semaphore_signal(barrier, inc=1, device_id=(peer, col), device_id_type=MESH)
    pl.semaphore_wait(barrier, groups - 1)
    local, sends, receipts = exchange_copies(groups, x_ref, out_ref, local_sem, send_sem, recv_sem)
    local.start()
    for copy in sends:
        copy.start()
    local.wait()
    for copy, receipt in zip(sends, receipts):
        copy.wait_send()
        receipt.wait_recv()


def ctx_exchange(x, collective_id):
    groups = lax.axis_size("ctx")
    return pl.pallas_call(
        functools.partial(exchange_kernel, groups),
        out_shape=jax.ShapeDtypeStruct(x.shape, x.dtype),
        in_specs=[pl.BlockSpec(memory_space=pltpu.VMEM)],
        out_specs=pl.BlockSpec(memory_space=pltpu.VMEM),
        scratch_shapes=[
            pltpu.SemaphoreType.DMA(()),
            pltpu.SemaphoreType.DMA((groups - 1,)),
            pltpu.SemaphoreType.DMA((groups - 1,)),
        ],
        compiler_params=pltpu.CompilerParams(collective_id=collective_id, has_side_effects=True),
    )(x)


def chan_gather(x, t, collective_id):
    size = lax.axis_size("chan")
    groups = lax.axis_size("ctx") if t is not None else 0
    chips = size // PER_Z
    longest = chips // 2
    operands = (x,) if t is None else (x, t)
    out_shape = [jax.ShapeDtypeStruct((size,) + x.shape, x.dtype)]
    scratch = [
        pltpu.SemaphoreType.DMA(()),
        pltpu.SemaphoreType.DMA((3,)),
        pltpu.SemaphoreType.DMA((3,)),
        pltpu.SemaphoreType.DMA((longest,)),
        pltpu.SemaphoreType.DMA((longest,)),
        pltpu.SemaphoreType.DMA((longest,)),
        pltpu.SemaphoreType.DMA((longest,)),
    ]
    if t is not None:
        out_shape.append(jax.ShapeDtypeStruct(t.shape, t.dtype))
        scratch += [
            pltpu.SemaphoreType.DMA(()),
            pltpu.SemaphoreType.DMA((groups - 1,)),
            pltpu.SemaphoreType.DMA((groups - 1,)),
        ]
    outs = pl.pallas_call(
        functools.partial(gather_kernel, chips, groups),
        out_shape=tuple(out_shape),
        in_specs=[pl.BlockSpec(memory_space=pltpu.VMEM)] * len(operands),
        out_specs=[pl.BlockSpec(memory_space=pltpu.VMEM)] * len(out_shape),
        scratch_shapes=scratch,
        compiler_params=pltpu.CompilerParams(collective_id=collective_id, has_side_effects=True),
    )(*operands)
    gathered = outs[0].reshape(size * x.shape[0], x.shape[1])
    return gathered if t is None else (gathered, outs[1])


def half_gather_kernel(chips, x_ref, out_ref, local_sem, cross_send, cross_recv, up_send, up_recv,
                       down_send, down_recv):
    row = lax.axis_index("ctx")
    me = lax.axis_index("chan")
    z = me // PER_Z
    y_lo = (me // 2) % 2
    core = me % 2
    across = me + 2 - 4 * y_lo
    ahead = ((z + 1) % chips) * PER_Z + y_lo * 2 + core
    behind = ((z + chips - 1) % chips) * PER_Z + y_lo * 2 + core
    mine = me // 2
    theirs = across // 2

    barrier = pltpu.get_barrier_semaphore()
    for peer in (across, ahead, behind):
        pl.semaphore_signal(barrier, inc=1, device_id=(row, peer), device_id_type=MESH)
    pl.semaphore_wait(barrier, 3)

    local = pltpu.make_async_copy(x_ref, out_ref.at[mine], local_sem)
    local.start()

    def cross(slot):
        return pltpu.make_async_remote_copy(
            src_ref=x_ref, dst_ref=out_ref.at[slot], send_sem=cross_send,
            recv_sem=cross_recv, device_id=(row, across), device_id_type=MESH)

    cross(mine).start()
    local.wait()
    cross(mine).wait_send()
    cross(theirs).wait_recv()

    def pair(chip):
        return out_ref.at[pl.ds(pl.multiple_of(chip * 2, 2), 2)]

    def up(s, chip):
        return pltpu.make_async_remote_copy(
            src_ref=pair(chip), dst_ref=pair(chip), send_sem=up_send.at[s],
            recv_sem=up_recv.at[s], device_id=(row, ahead), device_id_type=MESH)

    def down(s, chip):
        return pltpu.make_async_remote_copy(
            src_ref=pair(chip), dst_ref=pair(chip), send_sem=down_send.at[s],
            recv_sem=down_recv.at[s], device_id=(row, behind), device_id_type=MESH)

    ups = chips // 2
    downs = chips - 1 - ups
    for s in range(ups):
        if s > 0:
            up(s - 1, (z - s + chips) % chips).wait_recv()
        up(s, (z - s + chips) % chips).start()
        if s < downs:
            if s > 0:
                down(s - 1, (z + s) % chips).wait_recv()
            down(s, (z + s) % chips).start()
    up(ups - 1, (z - ups + chips) % chips).wait_recv()
    down(downs - 1, (z + downs) % chips).wait_recv()
    for s in range(ups):
        up(s, (z - s + chips) % chips).wait_send()
    for s in range(downs):
        down(s, (z + s) % chips).wait_send()


def half_gather(x, collective_id):
    size = lax.axis_size("chan")
    chips = size // PER_Z
    ups = chips // 2
    downs = chips - 1 - ups
    out = pl.pallas_call(
        functools.partial(half_gather_kernel, chips),
        out_shape=jax.ShapeDtypeStruct((size // 2,) + x.shape, x.dtype),
        in_specs=[pl.BlockSpec(memory_space=pltpu.VMEM)],
        out_specs=pl.BlockSpec(memory_space=pltpu.VMEM),
        scratch_shapes=[
            pltpu.SemaphoreType.DMA(()),
            pltpu.SemaphoreType.DMA(()),
            pltpu.SemaphoreType.DMA(()),
            pltpu.SemaphoreType.DMA((ups,)),
            pltpu.SemaphoreType.DMA((ups,)),
            pltpu.SemaphoreType.DMA((downs,)),
            pltpu.SemaphoreType.DMA((downs,)),
        ],
        compiler_params=pltpu.CompilerParams(collective_id=collective_id, has_side_effects=True),
    )(x)
    return out.reshape(size // 2 * x.shape[0], x.shape[1])


def dft_table(double_len):
    step = 32
    hi_ids = jnp.arange(double_len // step, dtype=jnp.int32)[:, None]
    lo_ids = jnp.arange(step, dtype=jnp.int32)[:, None]
    cols = jnp.arange(double_len, dtype=jnp.int32)[None, :]
    scale = 2.0 * math.pi / double_len
    hi_angle = scale * (hi_ids * step * cols % double_len).astype(jnp.float32)
    lo_angle = scale * (lo_ids * cols % double_len).astype(jnp.float32)
    hc, hs = jnp.cos(hi_angle)[:, None], jnp.sin(hi_angle)[:, None]
    lc, ls = jnp.cos(lo_angle)[None], jnp.sin(lo_angle)[None]
    cos = (hc * lc - hs * ls).reshape(double_len, double_len)
    sin = (hs * lc + hc * ls).reshape(double_len, double_len)
    return jnp.concatenate([cos, -sin], 0).astype(jnp.bfloat16)


def body(inputs, w_in, conv_taps, skip_gain, filter_taps, w_out):
    span_len, width_dev = inputs.shape
    double_len = 2 * span_len
    groups = lax.axis_size("ctx")
    position = lax.axis_index("ctx")
    own = width_dev // groups

    with jax.named_scope("input_gather_and_filter_to_owner"):
        taps_t = filter_taps.T.reshape(groups, own, span_len)
        inputs_t, taps_t = chan_gather(inputs.T, taps_t, 0)

    with jax.named_scope("out_weight_columns"):
        w_late, inputs_t = lax.optimization_barrier((w_out, inputs_t))
        size = lax.axis_size("chan")
        same_core = [list(range(c, size, 2)) for c in range(2)]
        w_cols = lax.all_to_all(w_late, "chan", 1, 0, tiled=True, axis_index_groups=same_core)

    with jax.named_scope("input_projection"):
        w_flat = w_in.reshape(w_in.shape[0], 3 * width_dev)
        proj_t = lax.dot_general(
            w_flat, inputs_t, (((0,), (0,)), ((), ())), preferred_element_type=jnp.float32
        ).astype(jnp.bfloat16)

    with jax.named_scope("projection_to_owner"):
        proj_t = proj_t.reshape(3, groups, own, span_len).transpose(1, 0, 2, 3)
        proj_t = ctx_exchange(proj_t, 3)

    with jax.named_scope("short_conv"):
        start = position * own
        taps = lax.dynamic_slice_in_dim(conv_taps, start, own, axis=2)
        rim = jnp.pad(proj_t[:-1, :, :, span_len - (KERNEL - 1) :], ((1, 0), (0, 0), (0, 0), (0, 0)))
        padded = jnp.concatenate([rim, proj_t], 3)
        filtered = jnp.zeros(proj_t.shape, jnp.float32)
        for lag in range(KERNEL):
            start_row = KERNEL - 1 - lag
            filtered = filtered + taps[lag].astype(jnp.float32)[None, :, :, None] * padded[
                ..., start_row : start_row + span_len
            ].astype(jnp.float32)
        streams = filtered.astype(jnp.bfloat16)
        gate_out = streams[:, 0]
        gated_in = (streams[:, 1].astype(jnp.float32) * streams[:, 2].astype(jnp.float32)).astype(
            jnp.bfloat16
        )

    with jax.named_scope("spectra"):
        w_cols, gated_in = lax.optimization_barrier((w_cols, gated_in))
        table = dft_table(double_len)
        forward_in = table[:, :span_len]
        spectra_in = jnp.einsum(
            "jdb,fb->jdf", gated_in, forward_in, preferred_element_type=jnp.float32
        ).astype(jnp.bfloat16)
        previous = jnp.pad(taps_t[:-1, :, 1:], ((1, 0), (0, 0), (0, 0)))
        padded_taps = jnp.concatenate(
            [taps_t, jnp.zeros((groups, own, 1), jnp.bfloat16), previous], 2
        )
        spectra_taps = jnp.einsum(
            "kdm,fm->kdf", padded_taps, table, preferred_element_type=jnp.float32
        ).astype(jnp.bfloat16)

    with jax.named_scope("mixture"):
        real_g = spectra_taps[:, :, :double_len].astype(jnp.float32)
        imag_g = spectra_taps[:, :, double_len:].astype(jnp.float32)
        real_u = spectra_in[:, :, :double_len].astype(jnp.float32)
        imag_u = spectra_in[:, :, double_len:].astype(jnp.float32)
        mixed = []
        for target in range(groups):
            acc_r = jnp.zeros((own, double_len), jnp.float32)
            acc_i = jnp.zeros((own, double_len), jnp.float32)
            for source in range(target + 1):
                lag = target - source
                acc_r = acc_r + (real_g[lag] * real_u[source] - imag_g[lag] * imag_u[source])
                acc_i = acc_i + (real_g[lag] * imag_u[source] + imag_g[lag] * real_u[source])
            mixed.append(jnp.concatenate([acc_r, acc_i], 1))
        mixture = jnp.stack(mixed, 0).astype(jnp.bfloat16)

    with jax.named_scope("inverse_and_gate"):
        long_out = jnp.einsum(
            "idf,fa->ida", mixture, forward_in, preferred_element_type=jnp.float32
        ) * (1.0 / double_len)
        gain = lax.dynamic_slice_in_dim(skip_gain, start, own)
        long_out = long_out + gain[None, :, None] * gated_in.astype(jnp.float32)
        gated_out = (gate_out.astype(jnp.float32) * long_out).astype(jnp.bfloat16)

    with jax.named_scope("gated_back_to_rows"):
        gated_out = ctx_exchange(gated_out, 4)
        gated_out = gated_out.reshape(width_dev, span_len)

    with jax.named_scope("output_projection"):
        gathered = half_gather(gated_out, 1)
        partial = lax.dot_general(
            gathered, w_cols, (((0,), (0,)), ((), ())), preferred_element_type=jnp.float32
        )
        core = lax.axis_index("chan") % 2
        mine = lax.dynamic_slice_in_dim(partial, core * width_dev, width_dev, axis=1)
        other = lax.dynamic_slice_in_dim(partial, (1 - core) * width_dev, width_dev, axis=1)
        pairs = [(h, h + 1 - 2 * (h % 2)) for h in range(lax.axis_size("chan"))]
        result = (mine + lax.ppermute(other, "chan", pairs)).astype(jnp.bfloat16)
    return result


def solution(mesh):
    return jax.shard_map(
        body,
        mesh=mesh,
        in_specs=(
            P("ctx", "chan"),
            P(None, None, "chan"),
            P(None, None, "chan"),
            P("chan"),
            P("ctx", "chan"),
            P("chan", None),
        ),
        out_specs=P("ctx", "chan"),
        check_vma=False,
    )
```

```python
import math

import functools

import jax
import jax.numpy as jnp
from jax import lax
from jax.experimental import pallas as pl
from jax.experimental.pallas import tpu as pltpu
from jax.sharding import PartitionSpec as P

KERNEL = 3
MESH = pl.DeviceIdType.MESH
PER_Z = 4


def gather_kernel(chips, groups, *refs):
    if groups:
        (x_ref, t_ref, out_ref, t_out_ref, local_sem, cross_send, cross_recv, ring_send, ring_recv,
         sib_send, sib_recv, t_local_sem, t_send, t_recv) = refs
    else:
        (x_ref, out_ref, local_sem, cross_send, cross_recv, ring_send, ring_recv,
         sib_send, sib_recv) = refs
    row = lax.axis_index("ctx")
    me = lax.axis_index("chan")
    z = me // PER_Z
    y_lo = (me // 2) % 2
    core = me % 2
    way = 1 - 2 * core
    after = ((z + way + chips) % chips) * PER_Z + y_lo * 2 + core
    before = ((z - way + chips) % chips) * PER_Z + y_lo * 2 + core
    sibling = me + 1 - 2 * core
    across = me + 2 - 4 * y_lo
    diagonal = across + 1 - 2 * core
    partners = (sibling, across, diagonal)

    barrier = pltpu.get_barrier_semaphore()
    for peer in partners + (after, before):
        pl.semaphore_signal(barrier, inc=1, device_id=(row, peer), device_id_type=MESH)
    for peer in ctx_peers(groups) if groups else ():
        pl.semaphore_signal(barrier, inc=1, device_id=(peer, me), device_id_type=MESH)
    pl.semaphore_wait(barrier, 5 + max(groups - 1, 0))

    if groups:
        t_local, t_sends, t_receipts = exchange_copies(
            groups, t_ref, t_out_ref, t_local_sem, t_send, t_recv)
        t_local.start()
        for copy in t_sends:
            copy.start()

    local = pltpu.make_async_copy(x_ref, out_ref.at[me], local_sem)
    local.start()

    def cross(k, peer, slot):
        return pltpu.make_async_remote_copy(
            src_ref=x_ref, dst_ref=out_ref.at[slot], send_sem=cross_send.at[k],
            recv_sem=cross_recv.at[k], device_id=(row, peer), device_id_type=MESH)

    for k, peer in enumerate(partners):
        cross(k, peer, me).start()
    local.wait()
    for k, peer in enumerate(partners):
        cross(k, peer, me).wait_send()
        cross(k, peer, peer).wait_recv()

    def group(chip):
        return out_ref.at[pl.ds(pl.multiple_of(chip * PER_Z, PER_Z), PER_Z)]

    def ring(s, chip):
        return pltpu.make_async_remote_copy(
            src_ref=group(chip), dst_ref=group(chip), send_sem=ring_send.at[s],
            recv_sem=ring_recv.at[s], device_id=(row, after), device_id_type=MESH)

    def sib(s, chip):
        return pltpu.make_async_remote_copy(
            src_ref=group(chip), dst_ref=group(chip), send_sem=sib_send.at[s],
            recv_sem=sib_recv.at[s], device_id=(row, sibling), device_id_type=MESH)

    longest = chips // 2
    for s in range(longest):
        active = jnp.logical_or(core == 0, s < chips - 1 - longest)
        sent = (z - way * s + chips) % chips
        got = (z - way * (s + 1) + chips) % chips

        @pl.when(active)
        def _():
            ring(s, sent).start()
            ring(s, got).wait_recv()
            sib(s, got).start()

    for s in range(longest):
        active = jnp.logical_or(core == 0, s < chips - 1 - longest)
        sent = (z - way * s + chips) % chips
        got = (z - way * (s + 1) + chips) % chips
        other = jnp.logical_or(core == 1, s < chips - 1 - longest)
        theirs = (z + way * (s + 1) + chips) % chips

        @pl.when(active)
        def _():
            ring(s, sent).wait_send()
            sib(s, got).wait_send()

        @pl.when(other)
        def _():
            sib(s, theirs).wait_recv()

    if groups:
        t_local.wait()
        for copy, receipt in zip(t_sends, t_receipts):
            copy.wait_send()
            receipt.wait_recv()


def exchange_copies(groups, x_ref, out_ref, local_sem, send_sem, recv_sem):
    me = lax.axis_index("ctx")
    col = lax.axis_index("chan")
    local = pltpu.make_async_copy(x_ref.at[me], out_ref.at[me], local_sem)

    def send(k, peer, slot):
        return pltpu.make_async_remote_copy(
            src_ref=x_ref.at[peer], dst_ref=out_ref.at[slot], send_sem=send_sem.at[k - 1],
            recv_sem=recv_sem.at[k - 1], device_id=(peer, col), device_id_type=MESH)

    sends = [send(k, (me + k) % groups, me) for k in range(1, groups)]
    sources = [(me - k + groups) % groups for k in range(1, groups)]
    receipts = [send(k, source, source) for k, source in zip(range(1, groups), sources)]
    return local, sends, receipts


def ctx_peers(groups):
    me = lax.axis_index("ctx")
    return [(me + k) % groups for k in range(1, groups)]


def exchange_kernel(groups, x_ref, out_ref, local_sem, send_sem, recv_sem):
    col = lax.axis_index("chan")
    barrier = pltpu.get_barrier_semaphore()
    for peer in ctx_peers(groups):
        pl.semaphore_signal(barrier, inc=1, device_id=(peer, col), device_id_type=MESH)
    pl.semaphore_wait(barrier, groups - 1)
    local, sends, receipts = exchange_copies(groups, x_ref, out_ref, local_sem, send_sem, recv_sem)
    local.start()
    for copy in sends:
        copy.start()
    local.wait()
    for copy, receipt in zip(sends, receipts):
        copy.wait_send()
        receipt.wait_recv()


def ctx_exchange(x, collective_id):
    groups = lax.axis_size("ctx")
    return pl.pallas_call(
        functools.partial(exchange_kernel, groups),
        out_shape=jax.ShapeDtypeStruct(x.shape, x.dtype),
        in_specs=[pl.BlockSpec(memory_space=pltpu.VMEM)],
        out_specs=pl.BlockSpec(memory_space=pltpu.VMEM),
        scratch_shapes=[
            pltpu.SemaphoreType.DMA(()),
            pltpu.SemaphoreType.DMA((groups - 1,)),
            pltpu.SemaphoreType.DMA((groups - 1,)),
        ],
        compiler_params=pltpu.CompilerParams(collective_id=collective_id, has_side_effects=True),
    )(x)


def chan_gather(x, t, collective_id):
    size = lax.axis_size("chan")
    groups = lax.axis_size("ctx") if t is not None else 0
    chips = size // PER_Z
    longest = chips // 2
    operands = (x,) if t is None else (x, t)
    out_shape = [jax.ShapeDtypeStruct((size,) + x.shape, x.dtype)]
    scratch = [
        pltpu.SemaphoreType.DMA(()),
        pltpu.SemaphoreType.DMA((3,)),
        pltpu.SemaphoreType.DMA((3,)),
        pltpu.SemaphoreType.DMA((longest,)),
        pltpu.SemaphoreType.DMA((longest,)),
        pltpu.SemaphoreType.DMA((longest,)),
        pltpu.SemaphoreType.DMA((longest,)),
    ]
    if t is not None:
        out_shape.append(jax.ShapeDtypeStruct(t.shape, t.dtype))
        scratch += [
            pltpu.SemaphoreType.DMA(()),
            pltpu.SemaphoreType.DMA((groups - 1,)),
            pltpu.SemaphoreType.DMA((groups - 1,)),
        ]
    outs = pl.pallas_call(
        functools.partial(gather_kernel, chips, groups),
        out_shape=tuple(out_shape),
        in_specs=[pl.BlockSpec(memory_space=pltpu.VMEM)] * len(operands),
        out_specs=[pl.BlockSpec(memory_space=pltpu.VMEM)] * len(out_shape),
        scratch_shapes=scratch,
        compiler_params=pltpu.CompilerParams(collective_id=collective_id, has_side_effects=True),
    )(*operands)
    gathered = outs[0].reshape(size * x.shape[0], x.shape[1])
    return gathered if t is None else (gathered, outs[1])


def half_gather_kernel(chips, x_ref, out_ref, local_sem, cross_send, cross_recv, up_send, up_recv,
                       down_send, down_recv):
    row = lax.axis_index("ctx")
    me = lax.axis_index("chan")
    z = me // PER_Z
    y_lo = (me // 2) % 2
    core = me % 2
    across = me + 2 - 4 * y_lo
    ahead = ((z + 1) % chips) * PER_Z + y_lo * 2 + core
    behind = ((z + chips - 1) % chips) * PER_Z + y_lo * 2 + core
    mine = me // 2
    theirs = across // 2

    barrier = pltpu.get_barrier_semaphore()
    for peer in (across, ahead, behind):
        pl.semaphore_signal(barrier, inc=1, device_id=(row, peer), device_id_type=MESH)
    pl.semaphore_wait(barrier, 3)

    local = pltpu.make_async_copy(x_ref, out_ref.at[mine], local_sem)
    local.start()

    def cross(slot):
        return pltpu.make_async_remote_copy(
            src_ref=x_ref, dst_ref=out_ref.at[slot], send_sem=cross_send,
            recv_sem=cross_recv, device_id=(row, across), device_id_type=MESH)

    cross(mine).start()
    local.wait()
    cross(mine).wait_send()
    cross(theirs).wait_recv()

    def pair(chip):
        return out_ref.at[pl.ds(pl.multiple_of(chip * 2, 2), 2)]

    def up(s, chip):
        return pltpu.make_async_remote_copy(
            src_ref=pair(chip), dst_ref=pair(chip), send_sem=up_send.at[s],
            recv_sem=up_recv.at[s], device_id=(row, ahead), device_id_type=MESH)

    def down(s, chip):
        return pltpu.make_async_remote_copy(
            src_ref=pair(chip), dst_ref=pair(chip), send_sem=down_send.at[s],
            recv_sem=down_recv.at[s], device_id=(row, behind), device_id_type=MESH)

    ups = chips // 2
    downs = chips - 1 - ups
    for s in range(ups):
        if s > 0:
            up(s - 1, (z - s + chips) % chips).wait_recv()
        up(s, (z - s + chips) % chips).start()
        if s < downs:
            if s > 0:
                down(s - 1, (z + s) % chips).wait_recv()
            down(s, (z + s) % chips).start()
    up(ups - 1, (z - ups + chips) % chips).wait_recv()
    down(downs - 1, (z + downs) % chips).wait_recv()
    for s in range(ups):
        up(s, (z - s + chips) % chips).wait_send()
    for s in range(downs):
        down(s, (z + s) % chips).wait_send()


def half_gather(x, collective_id):
    size = lax.axis_size("chan")
    chips = size // PER_Z
    ups = chips // 2
    downs = chips - 1 - ups
    out = pl.pallas_call(
        functools.partial(half_gather_kernel, chips),
        out_shape=jax.ShapeDtypeStruct((size // 2,) + x.shape, x.dtype),
        in_specs=[pl.BlockSpec(memory_space=pltpu.VMEM)],
        out_specs=pl.BlockSpec(memory_space=pltpu.VMEM),
        scratch_shapes=[
            pltpu.SemaphoreType.DMA(()),
            pltpu.SemaphoreType.DMA(()),
            pltpu.SemaphoreType.DMA(()),
            pltpu.SemaphoreType.DMA((ups,)),
            pltpu.SemaphoreType.DMA((ups,)),
            pltpu.SemaphoreType.DMA((downs,)),
            pltpu.SemaphoreType.DMA((downs,)),
        ],
        compiler_params=pltpu.CompilerParams(collective_id=collective_id, has_side_effects=True),
    )(x)
    return out.reshape(size // 2 * x.shape[0], x.shape[1])


def dft_table(double_len):
    step = 32
    hi_ids = jnp.arange(double_len // step, dtype=jnp.int32)[:, None]
    lo_ids = jnp.arange(step, dtype=jnp.int32)[:, None]
    cols = jnp.arange(double_len, dtype=jnp.int32)[None, :]
    scale = 2.0 * math.pi / double_len
    hi_angle = scale * (hi_ids * step * cols % double_len).astype(jnp.float32)
    lo_angle = scale * (lo_ids * cols % double_len).astype(jnp.float32)
    hc, hs = jnp.cos(hi_angle)[:, None], jnp.sin(hi_angle)[:, None]
    lc, ls = jnp.cos(lo_angle)[None], jnp.sin(lo_angle)[None]
    cos = (hc * lc - hs * ls).reshape(double_len, double_len)
    sin = (hs * lc + hc * ls).reshape(double_len, double_len)
    return jnp.concatenate([cos, -sin], 0).astype(jnp.bfloat16)


def body(inputs, w_in, conv_taps, skip_gain, filter_taps, w_out):
    span_len, width_dev = inputs.shape
    double_len = 2 * span_len
    groups = lax.axis_size("ctx")
    position = lax.axis_index("ctx")
    own = width_dev // groups

    with jax.named_scope("input_gather_and_filter_to_owner"):
        taps_t = filter_taps.T.reshape(groups, own, span_len)
        inputs_t, taps_t = chan_gather(inputs.T, taps_t, 0)

    with jax.named_scope("input_projection"):
        w_flat = w_in.reshape(w_in.shape[0], 3 * width_dev)
        proj_t = lax.dot_general(
            w_flat, inputs_t, (((0,), (0,)), ((), ())), preferred_element_type=jnp.float32
        ).astype(jnp.bfloat16)

    with jax.named_scope("projection_to_owner"):
        proj_t = proj_t.reshape(3, groups, own, span_len).transpose(1, 0, 2, 3)
        proj_t = ctx_exchange(proj_t, 3)

    with jax.named_scope("out_weight_columns"):
        w_late, proj_t = lax.optimization_barrier((w_out, proj_t))
        size = lax.axis_size("chan")
        same_core = [list(range(c, size, 2)) for c in range(2)]
        w_cols = lax.all_to_all(w_late, "chan", 1, 0, tiled=True, axis_index_groups=same_core)

    with jax.named_scope("short_conv"):
        start = position * own
        taps = lax.dynamic_slice_in_dim(conv_taps, start, own, axis=2)
        rim = jnp.pad(proj_t[:-1, :, :, span_len - (KERNEL - 1) :], ((1, 0), (0, 0), (0, 0), (0, 0)))
        padded = jnp.concatenate([rim, proj_t], 3)
        filtered = jnp.zeros(proj_t.shape, jnp.float32)
        for lag in range(KERNEL):
            start_row = KERNEL - 1 - lag
            filtered = filtered + taps[lag].astype(jnp.float32)[None, :, :, None] * padded[
                ..., start_row : start_row + span_len
            ].astype(jnp.float32)
        streams = filtered.astype(jnp.bfloat16)
        gate_out = streams[:, 0]
        gated_in = (streams[:, 1].astype(jnp.float32) * streams[:, 2].astype(jnp.float32)).astype(
            jnp.bfloat16
        )

    with jax.named_scope("spectra"):
        table = dft_table(double_len)
        forward_in = table[:, :span_len]
        spectra_in = jnp.einsum(
            "jdb,fb->jdf", gated_in, forward_in, preferred_element_type=jnp.float32
        ).astype(jnp.bfloat16)
        previous = jnp.pad(taps_t[:-1, :, 1:], ((1, 0), (0, 0), (0, 0)))
        padded_taps = jnp.concatenate(
            [taps_t, jnp.zeros((groups, own, 1), jnp.bfloat16), previous], 2
        )
        spectra_taps = jnp.einsum(
            "kdm,fm->kdf", padded_taps, table, preferred_element_type=jnp.float32
        ).astype(jnp.bfloat16)

    with jax.named_scope("mixture"):
        real_g = spectra_taps[:, :, :double_len].astype(jnp.float32)
        imag_g = spectra_taps[:, :, double_len:].astype(jnp.float32)
        real_u = spectra_in[:, :, :double_len].astype(jnp.float32)
        imag_u = spectra_in[:, :, double_len:].astype(jnp.float32)
        mixed = []
        for target in range(groups):
            acc_r = jnp.zeros((own, double_len), jnp.float32)
            acc_i = jnp.zeros((own, double_len), jnp.float32)
            for source in range(target + 1):
                lag = target - source
                acc_r = acc_r + (real_g[lag] * real_u[source] - imag_g[lag] * imag_u[source])
                acc_i = acc_i + (real_g[lag] * imag_u[source] + imag_g[lag] * real_u[source])
            mixed.append(jnp.concatenate([acc_r, acc_i], 1))
        mixture = jnp.stack(mixed, 0).astype(jnp.bfloat16)

    with jax.named_scope("inverse_and_gate"):
        long_out = jnp.einsum(
            "idf,fa->ida", mixture, forward_in, preferred_element_type=jnp.float32
        ) * (1.0 / double_len)
        gain = lax.dynamic_slice_in_dim(skip_gain, start, own)
        long_out = long_out + gain[None, :, None] * gated_in.astype(jnp.float32)
        gated_out = (gate_out.astype(jnp.float32) * long_out).astype(jnp.bfloat16)

    with jax.named_scope("gated_back_to_rows"):
        w_cols, gated_out = lax.optimization_barrier((w_cols, gated_out))
        gated_out = ctx_exchange(gated_out, 4)
        gated_out = gated_out.reshape(width_dev, span_len)

    with jax.named_scope("output_projection"):
        gathered = half_gather(gated_out, 1)
        partial = lax.dot_general(
            gathered, w_cols, (((0,), (0,)), ((), ())), preferred_element_type=jnp.float32
        )
        core = lax.axis_index("chan") % 2
        mine = lax.dynamic_slice_in_dim(partial, core * width_dev, width_dev, axis=1)
        other = lax.dynamic_slice_in_dim(partial, (1 - core) * width_dev, width_dev, axis=1)
        pairs = [(h, h + 1 - 2 * (h % 2)) for h in range(lax.axis_size("chan"))]
        result = (mine + lax.ppermute(other, "chan", pairs)).astype(jnp.bfloat16)
    return result


def solution(mesh):
    return jax.shard_map(
        body,
        mesh=mesh,
        in_specs=(
            P("ctx", "chan"),
            P(None, None, "chan"),
            P(None, None, "chan"),
            P("chan"),
            P("ctx", "chan"),
            P("chan", None),
        ),
        out_specs=P("ctx", "chan"),
        check_vma=False,
    )
```

```python
import math

import functools

import jax
import jax.numpy as jnp
from jax import lax
from jax.experimental import pallas as pl
from jax.experimental.pallas import tpu as pltpu
from jax.sharding import PartitionSpec as P

KERNEL = 3
MESH = pl.DeviceIdType.MESH
PER_Z = 4


def gather_kernel(chips, groups, *refs):
    if groups:
        (x_ref, t_ref, out_ref, t_out_ref, local_sem, cross_send, cross_recv, ring_send, ring_recv,
         sib_send, sib_recv, t_local_sem, t_send, t_recv) = refs
    else:
        (x_ref, out_ref, local_sem, cross_send, cross_recv, ring_send, ring_recv,
         sib_send, sib_recv) = refs
    row = lax.axis_index("ctx")
    me = lax.axis_index("chan")
    z = me // PER_Z
    y_lo = (me // 2) % 2
    core = me % 2
    way = 1 - 2 * core
    after = ((z + way + chips) % chips) * PER_Z + y_lo * 2 + core
    before = ((z - way + chips) % chips) * PER_Z + y_lo * 2 + core
    sibling = me + 1 - 2 * core
    across = me + 2 - 4 * y_lo
    diagonal = across + 1 - 2 * core
    partners = (sibling, across, diagonal)

    barrier = pltpu.get_barrier_semaphore()
    for peer in partners + (after, before):
        pl.semaphore_signal(barrier, inc=1, device_id=(row, peer), device_id_type=MESH)
    for peer in ctx_peers(groups) if groups else ():
        pl.semaphore_signal(barrier, inc=1, device_id=(peer, me), device_id_type=MESH)
    pl.semaphore_wait(barrier, 5 + max(groups - 1, 0))

    if groups:
        t_local, t_sends, t_receipts = exchange_copies(
            groups, t_ref, t_out_ref, t_local_sem, t_send, t_recv)
        t_local.start()
        for copy in t_sends:
            copy.start()

    local = pltpu.make_async_copy(x_ref, out_ref.at[me], local_sem)
    local.start()

    def cross(k, peer, slot):
        return pltpu.make_async_remote_copy(
            src_ref=x_ref, dst_ref=out_ref.at[slot], send_sem=cross_send.at[k],
            recv_sem=cross_recv.at[k], device_id=(row, peer), device_id_type=MESH)

    for k, peer in enumerate(partners):
        cross(k, peer, me).start()
    local.wait()
    for k, peer in enumerate(partners):
        cross(k, peer, me).wait_send()
        cross(k, peer, peer).wait_recv()

    last = chips // 2 - 1

    def part(chip, s, half):
        if s < last:
            return out_ref.at[pl.ds(pl.multiple_of(chip * PER_Z, PER_Z), PER_Z)]
        start = pl.multiple_of(chip * PER_Z + half * (PER_Z // 2), PER_Z // 2)
        return out_ref.at[pl.ds(start, PER_Z // 2)]

    def ring(s, chip):
        return pltpu.make_async_remote_copy(
            src_ref=part(chip, s, core), dst_ref=part(chip, s, core), send_sem=ring_send.at[s],
            recv_sem=ring_recv.at[s], device_id=(row, after), device_id_type=MESH)

    def sib(s, chip, half):
        return pltpu.make_async_remote_copy(
            src_ref=part(chip, s, half), dst_ref=part(chip, s, half), send_sem=sib_send.at[s],
            recv_sem=sib_recv.at[s], device_id=(row, sibling), device_id_type=MESH)

    for s in range(last + 1):
        sent = (z - way * s + chips) % chips
        got = (z - way * (s + 1) + chips) % chips
        ring(s, sent).start()
        ring(s, got).wait_recv()
        sib(s, got, core).start()

    for s in range(last + 1):
        sent = (z - way * s + chips) % chips
        got = (z - way * (s + 1) + chips) % chips
        theirs = (z + way * (s + 1) + chips) % chips
        ring(s, sent).wait_send()
        sib(s, got, core).wait_send()
        sib(s, theirs, 1 - core).wait_recv()

    if groups:
        t_local.wait()
        for copy, receipt in zip(t_sends, t_receipts):
            copy.wait_send()
            receipt.wait_recv()


def exchange_copies(groups, x_ref, out_ref, local_sem, send_sem, recv_sem):
    me = lax.axis_index("ctx")
    col = lax.axis_index("chan")
    local = pltpu.make_async_copy(x_ref.at[me], out_ref.at[me], local_sem)

    def send(k, peer, slot):
        return pltpu.make_async_remote_copy(
            src_ref=x_ref.at[peer], dst_ref=out_ref.at[slot], send_sem=send_sem.at[k - 1],
            recv_sem=recv_sem.at[k - 1], device_id=(peer, col), device_id_type=MESH)

    sends = [send(k, (me + k) % groups, me) for k in range(1, groups)]
    sources = [(me - k + groups) % groups for k in range(1, groups)]
    receipts = [send(k, source, source) for k, source in zip(range(1, groups), sources)]
    return local, sends, receipts


def ctx_peers(groups):
    me = lax.axis_index("ctx")
    return [(me + k) % groups for k in range(1, groups)]


def exchange_kernel(groups, x_ref, out_ref, local_sem, send_sem, recv_sem):
    col = lax.axis_index("chan")
    barrier = pltpu.get_barrier_semaphore()
    for peer in ctx_peers(groups):
        pl.semaphore_signal(barrier, inc=1, device_id=(peer, col), device_id_type=MESH)
    pl.semaphore_wait(barrier, groups - 1)
    local, sends, receipts = exchange_copies(groups, x_ref, out_ref, local_sem, send_sem, recv_sem)
    local.start()
    for copy in sends:
        copy.start()
    local.wait()
    for copy, receipt in zip(sends, receipts):
        copy.wait_send()
        receipt.wait_recv()


def ctx_exchange(x, collective_id):
    groups = lax.axis_size("ctx")
    return pl.pallas_call(
        functools.partial(exchange_kernel, groups),
        out_shape=jax.ShapeDtypeStruct(x.shape, x.dtype),
        in_specs=[pl.BlockSpec(memory_space=pltpu.VMEM)],
        out_specs=pl.BlockSpec(memory_space=pltpu.VMEM),
        scratch_shapes=[
            pltpu.SemaphoreType.DMA(()),
            pltpu.SemaphoreType.DMA((groups - 1,)),
            pltpu.SemaphoreType.DMA((groups - 1,)),
        ],
        compiler_params=pltpu.CompilerParams(collective_id=collective_id, has_side_effects=True),
    )(x)


def chan_gather(x, t, collective_id):
    size = lax.axis_size("chan")
    groups = lax.axis_size("ctx") if t is not None else 0
    chips = size // PER_Z
    longest = chips // 2
    assert chips % 2 == 0
    operands = (x,) if t is None else (x, t)
    out_shape = [jax.ShapeDtypeStruct((size,) + x.shape, x.dtype)]
    scratch = [
        pltpu.SemaphoreType.DMA(()),
        pltpu.SemaphoreType.DMA((3,)),
        pltpu.SemaphoreType.DMA((3,)),
        pltpu.SemaphoreType.DMA((longest,)),
        pltpu.SemaphoreType.DMA((longest,)),
        pltpu.SemaphoreType.DMA((longest,)),
        pltpu.SemaphoreType.DMA((longest,)),
    ]
    if t is not None:
        out_shape.append(jax.ShapeDtypeStruct(t.shape, t.dtype))
        scratch += [
            pltpu.SemaphoreType.DMA(()),
            pltpu.SemaphoreType.DMA((groups - 1,)),
            pltpu.SemaphoreType.DMA((groups - 1,)),
        ]
    outs = pl.pallas_call(
        functools.partial(gather_kernel, chips, groups),
        out_shape=tuple(out_shape),
        in_specs=[pl.BlockSpec(memory_space=pltpu.VMEM)] * len(operands),
        out_specs=[pl.BlockSpec(memory_space=pltpu.VMEM)] * len(out_shape),
        scratch_shapes=scratch,
        compiler_params=pltpu.CompilerParams(collective_id=collective_id, has_side_effects=True),
    )(*operands)
    gathered = outs[0].reshape(size * x.shape[0], x.shape[1])
    return gathered if t is None else (gathered, outs[1])


def half_gather_kernel(chips, x_ref, out_ref, local_sem, cross_send, cross_recv, up_send, up_recv,
                       down_send, down_recv):
    row = lax.axis_index("ctx")
    me = lax.axis_index("chan")
    z = me // PER_Z
    y_lo = (me // 2) % 2
    core = me % 2
    across = me + 2 - 4 * y_lo
    ahead = ((z + 1) % chips) * PER_Z + y_lo * 2 + core
    behind = ((z + chips - 1) % chips) * PER_Z + y_lo * 2 + core
    mine = me // 2
    theirs = across // 2

    barrier = pltpu.get_barrier_semaphore()
    for peer in (across, ahead, behind):
        pl.semaphore_signal(barrier, inc=1, device_id=(row, peer), device_id_type=MESH)
    pl.semaphore_wait(barrier, 3)

    local = pltpu.make_async_copy(x_ref, out_ref.at[mine], local_sem)
    local.start()

    def cross(slot):
        return pltpu.make_async_remote_copy(
            src_ref=x_ref, dst_ref=out_ref.at[slot], send_sem=cross_send,
            recv_sem=cross_recv, device_id=(row, across), device_id_type=MESH)

    cross(mine).start()
    local.wait()
    cross(mine).wait_send()
    cross(theirs).wait_recv()

    def pair(chip):
        return out_ref.at[pl.ds(pl.multiple_of(chip * 2, 2), 2)]

    steps = chips // 2

    def piece(chip, s, half):
        if s < steps - 1:
            return pair(chip)
        return out_ref.at[pl.ds(chip * 2 + half, 1)]

    def up(s, chip):
        return pltpu.make_async_remote_copy(
            src_ref=piece(chip, s, 0), dst_ref=piece(chip, s, 0), send_sem=up_send.at[s],
            recv_sem=up_recv.at[s], device_id=(row, ahead), device_id_type=MESH)

    def down(s, chip):
        return pltpu.make_async_remote_copy(
            src_ref=piece(chip, s, 1), dst_ref=piece(chip, s, 1), send_sem=down_send.at[s],
            recv_sem=down_recv.at[s], device_id=(row, behind), device_id_type=MESH)

    for s in range(steps):
        if s > 0:
            up(s - 1, (z - s + chips) % chips).wait_recv()
        up(s, (z - s + chips) % chips).start()
        if s > 0:
            down(s - 1, (z + s) % chips).wait_recv()
        down(s, (z + s) % chips).start()
    up(steps - 1, (z - steps + chips) % chips).wait_recv()
    down(steps - 1, (z + steps) % chips).wait_recv()
    for s in range(steps):
        up(s, (z - s + chips) % chips).wait_send()
        down(s, (z + s) % chips).wait_send()


def half_gather(x, collective_id):
    size = lax.axis_size("chan")
    chips = size // PER_Z
    assert chips % 2 == 0
    ups = downs = chips // 2
    out = pl.pallas_call(
        functools.partial(half_gather_kernel, chips),
        out_shape=jax.ShapeDtypeStruct((size // 2,) + x.shape, x.dtype),
        in_specs=[pl.BlockSpec(memory_space=pltpu.VMEM)],
        out_specs=pl.BlockSpec(memory_space=pltpu.VMEM),
        scratch_shapes=[
            pltpu.SemaphoreType.DMA(()),
            pltpu.SemaphoreType.DMA(()),
            pltpu.SemaphoreType.DMA(()),
            pltpu.SemaphoreType.DMA((ups,)),
            pltpu.SemaphoreType.DMA((ups,)),
            pltpu.SemaphoreType.DMA((downs,)),
            pltpu.SemaphoreType.DMA((downs,)),
        ],
        compiler_params=pltpu.CompilerParams(collective_id=collective_id, has_side_effects=True),
    )(x)
    return out.reshape(size // 2 * x.shape[0], x.shape[1])


def dft_table(double_len):
    step = 32
    hi_ids = jnp.arange(double_len // step, dtype=jnp.int32)[:, None]
    lo_ids = jnp.arange(step, dtype=jnp.int32)[:, None]
    cols = jnp.arange(double_len, dtype=jnp.int32)[None, :]
    scale = 2.0 * math.pi / double_len
    hi_angle = scale * (hi_ids * step * cols % double_len).astype(jnp.float32)
    lo_angle = scale * (lo_ids * cols % double_len).astype(jnp.float32)
    hc, hs = jnp.cos(hi_angle)[:, None], jnp.sin(hi_angle)[:, None]
    lc, ls = jnp.cos(lo_angle)[None], jnp.sin(lo_angle)[None]
    cos = (hc * lc - hs * ls).reshape(double_len, double_len)
    sin = (hs * lc + hc * ls).reshape(double_len, double_len)
    return jnp.concatenate([cos, -sin], 0).astype(jnp.bfloat16)


def body(inputs, w_in, conv_taps, skip_gain, filter_taps, w_out):
    span_len, width_dev = inputs.shape
    double_len = 2 * span_len
    groups = lax.axis_size("ctx")
    position = lax.axis_index("ctx")
    own = width_dev // groups

    with jax.named_scope("input_gather_and_filter_to_owner"):
        taps_t = filter_taps.T.reshape(groups, own, span_len)
        inputs_t, taps_t = chan_gather(inputs.T, taps_t, 0)

    with jax.named_scope("out_weight_columns"):
        w_late, inputs_t = lax.optimization_barrier((w_out, inputs_t))
        size = lax.axis_size("chan")
        same_core = [list(range(c, size, 2)) for c in range(2)]
        w_cols = lax.all_to_all(w_late, "chan", 1, 0, tiled=True, axis_index_groups=same_core)

    with jax.named_scope("input_projection"):
        w_flat = w_in.reshape(w_in.shape[0], 3 * width_dev)
        proj_t = lax.dot_general(
            w_flat, inputs_t, (((0,), (0,)), ((), ())), preferred_element_type=jnp.float32
        ).astype(jnp.bfloat16)

    with jax.named_scope("projection_to_owner"):
        proj_t = proj_t.reshape(3, groups, own, span_len).transpose(1, 0, 2, 3)
        proj_t = ctx_exchange(proj_t, 3)

    with jax.named_scope("short_conv"):
        start = position * own
        taps = lax.dynamic_slice_in_dim(conv_taps, start, own, axis=2)
        rim = jnp.pad(proj_t[:-1, :, :, span_len - (KERNEL - 1) :], ((1, 0), (0, 0), (0, 0), (0, 0)))
        padded = jnp.concatenate([rim, proj_t], 3)
        filtered = jnp.zeros(proj_t.shape, jnp.float32)
        for lag in range(KERNEL):
            start_row = KERNEL - 1 - lag
            filtered = filtered + taps[lag].astype(jnp.float32)[None, :, :, None] * padded[
                ..., start_row : start_row + span_len
            ].astype(jnp.float32)
        streams = filtered.astype(jnp.bfloat16)
        gate_out = streams[:, 0]
        gated_in = (streams[:, 1].astype(jnp.float32) * streams[:, 2].astype(jnp.float32)).astype(
            jnp.bfloat16
        )

    with jax.named_scope("spectra"):
        table = dft_table(double_len)
        forward_in = table[:, :span_len]
        spectra_in = jnp.einsum(
            "jdb,fb->jdf", gated_in, forward_in, preferred_element_type=jnp.float32
        ).astype(jnp.bfloat16)
        previous = jnp.pad(taps_t[:-1, :, 1:], ((1, 0), (0, 0), (0, 0)))
        padded_taps = jnp.concatenate(
            [taps_t, jnp.zeros((groups, own, 1), jnp.bfloat16), previous], 2
        )
        spectra_taps = jnp.einsum(
            "kdm,fm->kdf", padded_taps, table, preferred_element_type=jnp.float32
        ).astype(jnp.bfloat16)

    with jax.named_scope("mixture"):
        real_g = spectra_taps[:, :, :double_len].astype(jnp.float32)
        imag_g = spectra_taps[:, :, double_len:].astype(jnp.float32)
        real_u = spectra_in[:, :, :double_len].astype(jnp.float32)
        imag_u = spectra_in[:, :, double_len:].astype(jnp.float32)
        mixed = []
        for target in range(groups):
            acc_r = jnp.zeros((own, double_len), jnp.float32)
            acc_i = jnp.zeros((own, double_len), jnp.float32)
            for source in range(target + 1):
                lag = target - source
                acc_r = acc_r + (real_g[lag] * real_u[source] - imag_g[lag] * imag_u[source])
                acc_i = acc_i + (real_g[lag] * imag_u[source] + imag_g[lag] * real_u[source])
            mixed.append(jnp.concatenate([acc_r, acc_i], 1))
        mixture = jnp.stack(mixed, 0).astype(jnp.bfloat16)

    with jax.named_scope("inverse_and_gate"):
        long_out = jnp.einsum(
            "idf,fa->ida", mixture, forward_in, preferred_element_type=jnp.float32
        ) * (1.0 / double_len)
        gain = lax.dynamic_slice_in_dim(skip_gain, start, own)
        long_out = long_out + gain[None, :, None] * gated_in.astype(jnp.float32)
        gated_out = (gate_out.astype(jnp.float32) * long_out).astype(jnp.bfloat16)

    with jax.named_scope("gated_back_to_rows"):
        gated_out = ctx_exchange(gated_out, 4)
        w_cols, gated_out = lax.optimization_barrier((w_cols, gated_out))
        gated_out = gated_out.reshape(width_dev, span_len)

    with jax.named_scope("output_projection"):
        gathered = half_gather(gated_out, 1)
        partial = lax.dot_general(
            gathered, w_cols, (((0,), (0,)), ((), ())), preferred_element_type=jnp.float32
        )
        core = lax.axis_index("chan") % 2
        mine = lax.dynamic_slice_in_dim(partial, core * width_dev, width_dev, axis=1)
        other = lax.dynamic_slice_in_dim(partial, (1 - core) * width_dev, width_dev, axis=1)
        pairs = [(h, h + 1 - 2 * (h % 2)) for h in range(lax.axis_size("chan"))]
        result = (mine + lax.ppermute(other, "chan", pairs)).astype(jnp.bfloat16)
    return result


def solution(mesh):
    return jax.shard_map(
        body,
        mesh=mesh,
        in_specs=(
            P("ctx", "chan"),
            P(None, None, "chan"),
            P(None, None, "chan"),
            P("chan"),
            P("ctx", "chan"),
            P("chan", None),
        ),
        out_specs=P("ctx", "chan"),
        check_vma=False,
    )
```

```python
import math

import functools

import jax
import jax.numpy as jnp
from jax import lax
from jax.experimental import pallas as pl
from jax.experimental.pallas import tpu as pltpu
from jax.sharding import PartitionSpec as P

KERNEL = 3
MESH = pl.DeviceIdType.MESH
PER_Z = 4


def gather_kernel(chips, groups, *refs):
    if groups:
        (x_ref, t_ref, out_ref, t_out_ref, local_sem, cross_send, cross_recv, ring_send, ring_recv,
         sib_send, sib_recv, t_local_sem, t_send, t_recv) = refs
    else:
        (x_ref, out_ref, local_sem, cross_send, cross_recv, ring_send, ring_recv,
         sib_send, sib_recv) = refs
    row = lax.axis_index("ctx")
    me = lax.axis_index("chan")
    z = me // PER_Z
    y_lo = (me // 2) % 2
    core = me % 2
    way = 1 - 2 * core
    after = ((z + way + chips) % chips) * PER_Z + y_lo * 2 + core
    before = ((z - way + chips) % chips) * PER_Z + y_lo * 2 + core
    sibling = me + 1 - 2 * core
    across = me + 2 - 4 * y_lo
    diagonal = across + 1 - 2 * core
    partners = (sibling, across, diagonal)

    barrier = pltpu.get_barrier_semaphore()
    for peer in partners + (after, before):
        pl.semaphore_signal(barrier, inc=1, device_id=(row, peer), device_id_type=MESH)
    for peer in ctx_peers(groups) if groups else ():
        pl.semaphore_signal(barrier, inc=1, device_id=(peer, me), device_id_type=MESH)
    pl.semaphore_wait(barrier, 5 + max(groups - 1, 0))

    if groups:
        t_local, t_sends, t_receipts = exchange_copies(
            groups, t_ref, t_out_ref, t_local_sem, t_send, t_recv)
        t_local.start()
        for copy in t_sends:
            copy.start()

    local = pltpu.make_async_copy(x_ref, out_ref.at[me], local_sem)
    local.start()

    def cross(k, peer, slot):
        return pltpu.make_async_remote_copy(
            src_ref=x_ref, dst_ref=out_ref.at[slot], send_sem=cross_send.at[k],
            recv_sem=cross_recv.at[k], device_id=(row, peer), device_id_type=MESH)

    for k, peer in enumerate(partners):
        cross(k, peer, me).start()
    local.wait()
    for k, peer in enumerate(partners):
        cross(k, peer, me).wait_send()
        cross(k, peer, peer).wait_recv()

    last = chips // 2 - 1

    def part(chip, s, half):
        if s < last:
            return out_ref.at[pl.ds(pl.multiple_of(chip * PER_Z, PER_Z), PER_Z)]
        start = pl.multiple_of(chip * PER_Z + half * (PER_Z // 2), PER_Z // 2)
        return out_ref.at[pl.ds(start, PER_Z // 2)]

    def ring(s, chip):
        return pltpu.make_async_remote_copy(
            src_ref=part(chip, s, core), dst_ref=part(chip, s, core), send_sem=ring_send.at[s],
            recv_sem=ring_recv.at[s], device_id=(row, after), device_id_type=MESH)

    def sib(s, chip, half):
        return pltpu.make_async_remote_copy(
            src_ref=part(chip, s, half), dst_ref=part(chip, s, half), send_sem=sib_send.at[s],
            recv_sem=sib_recv.at[s], device_id=(row, sibling), device_id_type=MESH)

    for s in range(last + 1):
        sent = (z - way * s + chips) % chips
        got = (z - way * (s + 1) + chips) % chips
        ring(s, sent).start()
        ring(s, got).wait_recv()
        sib(s, got, core).start()

    for s in range(last + 1):
        sent = (z - way * s + chips) % chips
        got = (z - way * (s + 1) + chips) % chips
        theirs = (z + way * (s + 1) + chips) % chips
        ring(s, sent).wait_send()
        sib(s, got, core).wait_send()
        sib(s, theirs, 1 - core).wait_recv()

    if groups:
        t_local.wait()
        for copy, receipt in zip(t_sends, t_receipts):
            copy.wait_send()
            receipt.wait_recv()


def exchange_copies(groups, x_ref, out_ref, local_sem, send_sem, recv_sem):
    me = lax.axis_index("ctx")
    col = lax.axis_index("chan")
    local = pltpu.make_async_copy(x_ref.at[me], out_ref.at[me], local_sem)

    def send(k, peer, slot):
        return pltpu.make_async_remote_copy(
            src_ref=x_ref.at[peer], dst_ref=out_ref.at[slot], send_sem=send_sem.at[k - 1],
            recv_sem=recv_sem.at[k - 1], device_id=(peer, col), device_id_type=MESH)

    sends = [send(k, (me + k) % groups, me) for k in range(1, groups)]
    sources = [(me - k + groups) % groups for k in range(1, groups)]
    receipts = [send(k, source, source) for k, source in zip(range(1, groups), sources)]
    return local, sends, receipts


def ctx_peers(groups):
    me = lax.axis_index("ctx")
    return [(me + k) % groups for k in range(1, groups)]


def exchange_kernel(groups, x_ref, out_ref, local_sem, send_sem, recv_sem):
    col = lax.axis_index("chan")
    barrier = pltpu.get_barrier_semaphore()
    for peer in ctx_peers(groups):
        pl.semaphore_signal(barrier, inc=1, device_id=(peer, col), device_id_type=MESH)
    pl.semaphore_wait(barrier, groups - 1)
    local, sends, receipts = exchange_copies(groups, x_ref, out_ref, local_sem, send_sem, recv_sem)
    local.start()
    for copy in sends:
        copy.start()
    local.wait()
    for copy, receipt in zip(sends, receipts):
        copy.wait_send()
        receipt.wait_recv()


def ctx_exchange(x, collective_id):
    groups = lax.axis_size("ctx")
    return pl.pallas_call(
        functools.partial(exchange_kernel, groups),
        out_shape=jax.ShapeDtypeStruct(x.shape, x.dtype),
        in_specs=[pl.BlockSpec(memory_space=pltpu.VMEM)],
        out_specs=pl.BlockSpec(memory_space=pltpu.VMEM),
        scratch_shapes=[
            pltpu.SemaphoreType.DMA(()),
            pltpu.SemaphoreType.DMA((groups - 1,)),
            pltpu.SemaphoreType.DMA((groups - 1,)),
        ],
        compiler_params=pltpu.CompilerParams(collective_id=collective_id, has_side_effects=True),
    )(x)


def chan_gather(x, t, collective_id):
    size = lax.axis_size("chan")
    groups = lax.axis_size("ctx") if t is not None else 0
    chips = size // PER_Z
    longest = chips // 2
    assert chips % 2 == 0
    operands = (x,) if t is None else (x, t)
    out_shape = [jax.ShapeDtypeStruct((size,) + x.shape, x.dtype)]
    scratch = [
        pltpu.SemaphoreType.DMA(()),
        pltpu.SemaphoreType.DMA((3,)),
        pltpu.SemaphoreType.DMA((3,)),
        pltpu.SemaphoreType.DMA((longest,)),
        pltpu.SemaphoreType.DMA((longest,)),
        pltpu.SemaphoreType.DMA((longest,)),
        pltpu.SemaphoreType.DMA((longest,)),
    ]
    if t is not None:
        out_shape.append(jax.ShapeDtypeStruct(t.shape, t.dtype))
        scratch += [
            pltpu.SemaphoreType.DMA(()),
            pltpu.SemaphoreType.DMA((groups - 1,)),
            pltpu.SemaphoreType.DMA((groups - 1,)),
        ]
    outs = pl.pallas_call(
        functools.partial(gather_kernel, chips, groups),
        out_shape=tuple(out_shape),
        in_specs=[pl.BlockSpec(memory_space=pltpu.VMEM)] * len(operands),
        out_specs=[pl.BlockSpec(memory_space=pltpu.VMEM)] * len(out_shape),
        scratch_shapes=scratch,
        compiler_params=pltpu.CompilerParams(collective_id=collective_id, has_side_effects=True),
    )(*operands)
    gathered = outs[0].reshape(size * x.shape[0], x.shape[1])
    return gathered if t is None else (gathered, outs[1])


def half_gather_kernel(chips, x_ref, out_ref, local_sem, cross_send, cross_recv, up_send, up_recv,
                       down_send, down_recv):
    row = lax.axis_index("ctx")
    me = lax.axis_index("chan")
    z = me // PER_Z
    y_lo = (me // 2) % 2
    core = me % 2
    across = me + 2 - 4 * y_lo
    ahead = ((z + 1) % chips) * PER_Z + y_lo * 2 + core
    behind = ((z + chips - 1) % chips) * PER_Z + y_lo * 2 + core
    mine = me // 2
    theirs = across // 2

    barrier = pltpu.get_barrier_semaphore()
    for peer in (across, ahead, behind):
        pl.semaphore_signal(barrier, inc=1, device_id=(row, peer), device_id_type=MESH)
    pl.semaphore_wait(barrier, 3)

    local = pltpu.make_async_copy(x_ref, out_ref.at[mine], local_sem)
    local.start()

    def cross(slot):
        return pltpu.make_async_remote_copy(
            src_ref=x_ref, dst_ref=out_ref.at[slot], send_sem=cross_send,
            recv_sem=cross_recv, device_id=(row, across), device_id_type=MESH)

    cross(mine).start()
    local.wait()
    cross(mine).wait_send()
    cross(theirs).wait_recv()

    def pair(chip):
        return out_ref.at[pl.ds(pl.multiple_of(chip * 2, 2), 2)]

    steps = chips // 2

    def piece(chip, s, half):
        if s < steps - 1:
            return pair(chip)
        return out_ref.at[pl.ds(chip * 2 + half, 1)]

    def up(s, chip):
        return pltpu.make_async_remote_copy(
            src_ref=piece(chip, s, 0), dst_ref=piece(chip, s, 0), send_sem=up_send.at[s],
            recv_sem=up_recv.at[s], device_id=(row, ahead), device_id_type=MESH)

    def down(s, chip):
        return pltpu.make_async_remote_copy(
            src_ref=piece(chip, s, 1), dst_ref=piece(chip, s, 1), send_sem=down_send.at[s],
            recv_sem=down_recv.at[s], device_id=(row, behind), device_id_type=MESH)

    for s in range(steps):
        if s > 0:
            up(s - 1, (z - s + chips) % chips).wait_recv()
        up(s, (z - s + chips) % chips).start()
        if s > 0:
            down(s - 1, (z + s) % chips).wait_recv()
        down(s, (z + s) % chips).start()
    up(steps - 1, (z - steps + chips) % chips).wait_recv()
    down(steps - 1, (z + steps) % chips).wait_recv()
    for s in range(steps):
        up(s, (z - s + chips) % chips).wait_send()
        down(s, (z + s) % chips).wait_send()


def half_gather(x, collective_id):
    size = lax.axis_size("chan")
    chips = size // PER_Z
    assert chips % 2 == 0
    ups = downs = chips // 2
    out = pl.pallas_call(
        functools.partial(half_gather_kernel, chips),
        out_shape=jax.ShapeDtypeStruct((size // 2,) + x.shape, x.dtype),
        in_specs=[pl.BlockSpec(memory_space=pltpu.VMEM)],
        out_specs=pl.BlockSpec(memory_space=pltpu.VMEM),
        scratch_shapes=[
            pltpu.SemaphoreType.DMA(()),
            pltpu.SemaphoreType.DMA(()),
            pltpu.SemaphoreType.DMA(()),
            pltpu.SemaphoreType.DMA((ups,)),
            pltpu.SemaphoreType.DMA((ups,)),
            pltpu.SemaphoreType.DMA((downs,)),
            pltpu.SemaphoreType.DMA((downs,)),
        ],
        compiler_params=pltpu.CompilerParams(collective_id=collective_id, has_side_effects=True),
    )(x)
    return out.reshape(size // 2 * x.shape[0], x.shape[1])


def dft_table(double_len):
    step = 32
    hi_ids = jnp.arange(double_len // step, dtype=jnp.int32)[:, None]
    lo_ids = jnp.arange(step, dtype=jnp.int32)[:, None]
    cols = jnp.arange(double_len, dtype=jnp.int32)[None, :]
    scale = 2.0 * math.pi / double_len
    hi_angle = scale * (hi_ids * step * cols % double_len).astype(jnp.float32)
    lo_angle = scale * (lo_ids * cols % double_len).astype(jnp.float32)
    hc, hs = jnp.cos(hi_angle)[:, None], jnp.sin(hi_angle)[:, None]
    lc, ls = jnp.cos(lo_angle)[None], jnp.sin(lo_angle)[None]
    cos = (hc * lc - hs * ls).reshape(double_len, double_len)
    sin = (hs * lc + hc * ls).reshape(double_len, double_len)
    return jnp.concatenate([cos, -sin], 0).astype(jnp.bfloat16)


def body(inputs, w_in, conv_taps, skip_gain, filter_taps, w_out):
    span_len, width_dev = inputs.shape
    double_len = 2 * span_len
    groups = lax.axis_size("ctx")
    position = lax.axis_index("ctx")
    own = width_dev // groups

    with jax.named_scope("input_gather_and_filter_to_owner"):
        taps_t = filter_taps.T.reshape(groups, own, span_len)
        inputs_t, taps_t = chan_gather(inputs.T, taps_t, 0)

    with jax.named_scope("input_projection"):
        w_flat = w_in.reshape(w_in.shape[0], 3 * width_dev)
        proj_t = lax.dot_general(
            w_flat, inputs_t, (((0,), (0,)), ((), ())), preferred_element_type=jnp.float32
        ).astype(jnp.bfloat16)

    with jax.named_scope("projection_to_owner"):
        proj_t = proj_t.reshape(3, groups, own, span_len).transpose(1, 0, 2, 3)
        proj_t = ctx_exchange(proj_t, 3)

    with jax.named_scope("out_weight_columns"):
        w_late, proj_t = lax.optimization_barrier((w_out, proj_t))
        size = lax.axis_size("chan")
        same_core = [list(range(c, size, 2)) for c in range(2)]
        w_cols = lax.all_to_all(w_late, "chan", 1, 0, tiled=True, axis_index_groups=same_core)

    with jax.named_scope("short_conv"):
        start = position * own
        taps = lax.dynamic_slice_in_dim(conv_taps, start, own, axis=2)
        rim = jnp.pad(proj_t[:-1, :, :, span_len - (KERNEL - 1) :], ((1, 0), (0, 0), (0, 0), (0, 0)))
        padded = jnp.concatenate([rim, proj_t], 3)
        filtered = jnp.zeros(proj_t.shape, jnp.float32)
        for lag in range(KERNEL):
            start_row = KERNEL - 1 - lag
            filtered = filtered + taps[lag].astype(jnp.float32)[None, :, :, None] * padded[
                ..., start_row : start_row + span_len
            ].astype(jnp.float32)
        streams = filtered.astype(jnp.bfloat16)
        gate_out = streams[:, 0]
        gated_in = (streams[:, 1].astype(jnp.float32) * streams[:, 2].astype(jnp.float32)).astype(
            jnp.bfloat16
        )

    with jax.named_scope("spectra"):
        table = dft_table(double_len)
        forward_in = table[:, :span_len]
        spectra_in = jnp.einsum(
            "jdb,fb->jdf", gated_in, forward_in, preferred_element_type=jnp.float32
        ).astype(jnp.bfloat16)
        previous = jnp.pad(taps_t[:-1, :, 1:], ((1, 0), (0, 0), (0, 0)))
        padded_taps = jnp.concatenate(
            [taps_t, jnp.zeros((groups, own, 1), jnp.bfloat16), previous], 2
        )
        spectra_taps = jnp.einsum(
            "kdm,fm->kdf", padded_taps, table, preferred_element_type=jnp.float32
        ).astype(jnp.bfloat16)

    with jax.named_scope("mixture"):
        real_g = spectra_taps[:, :, :double_len].astype(jnp.float32)
        imag_g = spectra_taps[:, :, double_len:].astype(jnp.float32)
        real_u = spectra_in[:, :, :double_len].astype(jnp.float32)
        imag_u = spectra_in[:, :, double_len:].astype(jnp.float32)
        mixed = []
        for target in range(groups):
            acc_r = jnp.zeros((own, double_len), jnp.float32)
            acc_i = jnp.zeros((own, double_len), jnp.float32)
            for source in range(target + 1):
                lag = target - source
                acc_r = acc_r + (real_g[lag] * real_u[source] - imag_g[lag] * imag_u[source])
                acc_i = acc_i + (real_g[lag] * imag_u[source] + imag_g[lag] * real_u[source])
            mixed.append(jnp.concatenate([acc_r, acc_i], 1))
        mixture = jnp.stack(mixed, 0).astype(jnp.bfloat16)

    with jax.named_scope("inverse_and_gate"):
        long_out = jnp.einsum(
            "idf,fa->ida", mixture, forward_in, preferred_element_type=jnp.float32
        ) * (1.0 / double_len)
        gain = lax.dynamic_slice_in_dim(skip_gain, start, own)
        long_out = long_out + gain[None, :, None] * gated_in.astype(jnp.float32)
        gated_out = (gate_out.astype(jnp.float32) * long_out).astype(jnp.bfloat16)

    with jax.named_scope("gated_back_to_rows"):
        gated_out = ctx_exchange(gated_out, 4)
        w_cols, gated_out = lax.optimization_barrier((w_cols, gated_out))
        gated_out = gated_out.reshape(width_dev, span_len)

    with jax.named_scope("output_projection"):
        gathered = half_gather(gated_out, 1)
        partial = lax.dot_general(
            gathered, w_cols, (((0,), (0,)), ((), ())), preferred_element_type=jnp.float32
        )
        core = lax.axis_index("chan") % 2
        mine = lax.dynamic_slice_in_dim(partial, core * width_dev, width_dev, axis=1)
        other = lax.dynamic_slice_in_dim(partial, (1 - core) * width_dev, width_dev, axis=1)
        pairs = [(h, h + 1 - 2 * (h % 2)) for h in range(lax.axis_size("chan"))]
        result = (mine + lax.ppermute(other, "chan", pairs)).astype(jnp.bfloat16)
    return result


def solution(mesh):
    return jax.shard_map(
        body,
        mesh=mesh,
        in_specs=(
            P("ctx", "chan"),
            P(None, None, "chan"),
            P(None, None, "chan"),
            P("chan"),
            P("ctx", "chan"),
            P("chan", None),
        ),
        out_specs=P("ctx", "chan"),
        check_vma=False,
    )
```

```python
import math

import functools

import jax
import jax.numpy as jnp
from jax import lax
from jax.experimental import pallas as pl
from jax.experimental.pallas import tpu as pltpu
from jax.sharding import PartitionSpec as P

KERNEL = 3
MESH = pl.DeviceIdType.MESH
PER_Z = 4


def gather_kernel(chips, groups, *refs):
    if groups:
        (x_ref, t_ref, out_ref, t_out_ref, local_sem, cross_send, cross_recv, ring_send, ring_recv,
         sib_send, sib_recv, t_local_sem, t_send, t_recv) = refs
    else:
        (x_ref, out_ref, local_sem, cross_send, cross_recv, ring_send, ring_recv,
         sib_send, sib_recv) = refs
    row = lax.axis_index("ctx")
    me = lax.axis_index("chan")
    z = me // PER_Z
    y_lo = (me // 2) % 2
    core = me % 2
    way = 1 - 2 * core
    after = ((z + way + chips) % chips) * PER_Z + y_lo * 2 + core
    before = ((z - way + chips) % chips) * PER_Z + y_lo * 2 + core
    sibling = me + 1 - 2 * core
    across = me + 2 - 4 * y_lo
    diagonal = across + 1 - 2 * core
    partners = (sibling, across, diagonal)

    barrier = pltpu.get_barrier_semaphore()
    for peer in partners + (after, before):
        pl.semaphore_signal(barrier, inc=1, device_id=(row, peer), device_id_type=MESH)
    for peer in ctx_peers(groups) if groups else ():
        pl.semaphore_signal(barrier, inc=1, device_id=(peer, me), device_id_type=MESH)
    pl.semaphore_wait(barrier, 5 + max(groups - 1, 0))

    if groups:
        t_local, t_sends, t_receipts = exchange_copies(
            groups, t_ref, t_out_ref, t_local_sem, t_send, t_recv)
        t_local.start()
        for copy in t_sends:
            copy.start()

    local = pltpu.make_async_copy(x_ref, out_ref.at[me], local_sem)
    local.start()

    def cross(k, peer, slot):
        return pltpu.make_async_remote_copy(
            src_ref=x_ref, dst_ref=out_ref.at[slot], send_sem=cross_send.at[k],
            recv_sem=cross_recv.at[k], device_id=(row, peer), device_id_type=MESH)

    for k, peer in enumerate(partners):
        cross(k, peer, me).start()
    local.wait()
    for k, peer in enumerate(partners):
        cross(k, peer, me).wait_send()
        cross(k, peer, peer).wait_recv()

    last = chips // 2 - 1

    def part(chip, s, half):
        if s < last:
            return out_ref.at[pl.ds(pl.multiple_of(chip * PER_Z, PER_Z), PER_Z)]
        start = pl.multiple_of(chip * PER_Z + half * (PER_Z // 2), PER_Z // 2)
        return out_ref.at[pl.ds(start, PER_Z // 2)]

    def ring(s, chip):
        return pltpu.make_async_remote_copy(
            src_ref=part(chip, s, core), dst_ref=part(chip, s, core), send_sem=ring_send.at[s],
            recv_sem=ring_recv.at[s], device_id=(row, after), device_id_type=MESH)

    def sib(s, chip, half):
        return pltpu.make_async_remote_copy(
            src_ref=part(chip, s, half), dst_ref=part(chip, s, half), send_sem=sib_send.at[s],
            recv_sem=sib_recv.at[s], device_id=(row, sibling), device_id_type=MESH)

    for s in range(last + 1):
        sent = (z - way * s + chips) % chips
        got = (z - way * (s + 1) + chips) % chips
        ring(s, sent).start()
        ring(s, got).wait_recv()
        sib(s, got, core).start()

    for s in range(last + 1):
        sent = (z - way * s + chips) % chips
        got = (z - way * (s + 1) + chips) % chips
        theirs = (z + way * (s + 1) + chips) % chips
        ring(s, sent).wait_send()
        sib(s, got, core).wait_send()
        sib(s, theirs, 1 - core).wait_recv()

    if groups:
        t_local.wait()
        for copy, receipt in zip(t_sends, t_receipts):
            copy.wait_send()
            receipt.wait_recv()


def exchange_copies(groups, x_ref, out_ref, local_sem, send_sem, recv_sem):
    me = lax.axis_index("ctx")
    col = lax.axis_index("chan")
    local = pltpu.make_async_copy(x_ref.at[me], out_ref.at[me], local_sem)

    def send(k, peer, slot):
        return pltpu.make_async_remote_copy(
            src_ref=x_ref.at[peer], dst_ref=out_ref.at[slot], send_sem=send_sem.at[k - 1],
            recv_sem=recv_sem.at[k - 1], device_id=(peer, col), device_id_type=MESH)

    sends = [send(k, (me + k) % groups, me) for k in range(1, groups)]
    sources = [(me - k + groups) % groups for k in range(1, groups)]
    receipts = [send(k, source, source) for k, source in zip(range(1, groups), sources)]
    return local, sends, receipts


def ctx_peers(groups):
    me = lax.axis_index("ctx")
    return [(me + k) % groups for k in range(1, groups)]


def exchange_kernel(groups, x_ref, out_ref, local_sem, send_sem, recv_sem):
    col = lax.axis_index("chan")
    barrier = pltpu.get_barrier_semaphore()
    for peer in ctx_peers(groups):
        pl.semaphore_signal(barrier, inc=1, device_id=(peer, col), device_id_type=MESH)
    pl.semaphore_wait(barrier, groups - 1)
    local, sends, receipts = exchange_copies(groups, x_ref, out_ref, local_sem, send_sem, recv_sem)
    local.start()
    for copy in sends:
        copy.start()
    local.wait()
    for copy, receipt in zip(sends, receipts):
        copy.wait_send()
        receipt.wait_recv()


def ctx_exchange(x, collective_id):
    groups = lax.axis_size("ctx")
    return pl.pallas_call(
        functools.partial(exchange_kernel, groups),
        out_shape=jax.ShapeDtypeStruct(x.shape, x.dtype),
        in_specs=[pl.BlockSpec(memory_space=pltpu.VMEM)],
        out_specs=pl.BlockSpec(memory_space=pltpu.VMEM),
        scratch_shapes=[
            pltpu.SemaphoreType.DMA(()),
            pltpu.SemaphoreType.DMA((groups - 1,)),
            pltpu.SemaphoreType.DMA((groups - 1,)),
        ],
        compiler_params=pltpu.CompilerParams(collective_id=collective_id, has_side_effects=True),
    )(x)


def chan_gather(x, t, collective_id):
    size = lax.axis_size("chan")
    groups = lax.axis_size("ctx") if t is not None else 0
    chips = size // PER_Z
    longest = chips // 2
    assert chips % 2 == 0
    operands = (x,) if t is None else (x, t)
    out_shape = [jax.ShapeDtypeStruct((size,) + x.shape, x.dtype)]
    scratch = [
        pltpu.SemaphoreType.DMA(()),
        pltpu.SemaphoreType.DMA((3,)),
        pltpu.SemaphoreType.DMA((3,)),
        pltpu.SemaphoreType.DMA((longest,)),
        pltpu.SemaphoreType.DMA((longest,)),
        pltpu.SemaphoreType.DMA((longest,)),
        pltpu.SemaphoreType.DMA((longest,)),
    ]
    if t is not None:
        out_shape.append(jax.ShapeDtypeStruct(t.shape, t.dtype))
        scratch += [
            pltpu.SemaphoreType.DMA(()),
            pltpu.SemaphoreType.DMA((groups - 1,)),
            pltpu.SemaphoreType.DMA((groups - 1,)),
        ]
    outs = pl.pallas_call(
        functools.partial(gather_kernel, chips, groups),
        out_shape=tuple(out_shape),
        in_specs=[pl.BlockSpec(memory_space=pltpu.VMEM)] * len(operands),
        out_specs=[pl.BlockSpec(memory_space=pltpu.VMEM)] * len(out_shape),
        scratch_shapes=scratch,
        compiler_params=pltpu.CompilerParams(collective_id=collective_id, has_side_effects=True),
    )(*operands)
    gathered = outs[0].reshape(size * x.shape[0], x.shape[1])
    return gathered if t is None else (gathered, outs[1])


def half_gather_kernel(chips, groups, t_ref, out_ref, x_ref, local_sem, cross_send, cross_recv,
                       up_send, up_recv, down_send, down_recv, t_local_sem, t_send, t_recv):
    row = lax.axis_index("ctx")
    me = lax.axis_index("chan")
    z = me // PER_Z
    y_lo = (me // 2) % 2
    core = me % 2
    across = me + 2 - 4 * y_lo
    ahead = ((z + 1) % chips) * PER_Z + y_lo * 2 + core
    behind = ((z + chips - 1) % chips) * PER_Z + y_lo * 2 + core
    mine = me // 2
    theirs = across // 2

    barrier = pltpu.get_barrier_semaphore()
    for peer in (across, ahead, behind):
        pl.semaphore_signal(barrier, inc=1, device_id=(row, peer), device_id_type=MESH)
    for peer in ctx_peers(groups):
        pl.semaphore_signal(barrier, inc=1, device_id=(peer, me), device_id_type=MESH)
    pl.semaphore_wait(barrier, 3 + groups - 1)

    slab = t_ref.shape[1]

    def slot(g):
        return x_ref.at[pl.ds(pl.multiple_of(g * slab, slab), slab)]

    def give(k, peer, g):
        return pltpu.make_async_remote_copy(
            src_ref=t_ref.at[peer], dst_ref=slot(g), send_sem=t_send.at[k - 1],
            recv_sem=t_recv.at[k - 1], device_id=(peer, me), device_id_type=MESH)

    t_local = pltpu.make_async_copy(t_ref.at[row], slot(row), t_local_sem)
    t_local.start()
    for k in range(1, groups):
        give(k, (row + k) % groups, row).start()
    t_local.wait()
    for k in range(1, groups):
        give(k, (row + k) % groups, row).wait_send()
        source = (row - k + groups) % groups
        give(k, source, source).wait_recv()

    local = pltpu.make_async_copy(x_ref, out_ref.at[mine], local_sem)
    local.start()

    def cross(slot):
        return pltpu.make_async_remote_copy(
            src_ref=x_ref, dst_ref=out_ref.at[slot], send_sem=cross_send,
            recv_sem=cross_recv, device_id=(row, across), device_id_type=MESH)

    cross(mine).start()
    local.wait()
    cross(mine).wait_send()
    cross(theirs).wait_recv()

    def pair(chip):
        return out_ref.at[pl.ds(pl.multiple_of(chip * 2, 2), 2)]

    steps = chips // 2

    def piece(chip, s, half):
        if s < steps - 1:
            return pair(chip)
        return out_ref.at[pl.ds(chip * 2 + half, 1)]

    def up(s, chip):
        return pltpu.make_async_remote_copy(
            src_ref=piece(chip, s, 0), dst_ref=piece(chip, s, 0), send_sem=up_send.at[s],
            recv_sem=up_recv.at[s], device_id=(row, ahead), device_id_type=MESH)

    def down(s, chip):
        return pltpu.make_async_remote_copy(
            src_ref=piece(chip, s, 1), dst_ref=piece(chip, s, 1), send_sem=down_send.at[s],
            recv_sem=down_recv.at[s], device_id=(row, behind), device_id_type=MESH)

    for s in range(steps):
        if s > 0:
            up(s - 1, (z - s + chips) % chips).wait_recv()
        up(s, (z - s + chips) % chips).start()
        if s > 0:
            down(s - 1, (z + s) % chips).wait_recv()
        down(s, (z + s) % chips).start()
    up(steps - 1, (z - steps + chips) % chips).wait_recv()
    down(steps - 1, (z + steps) % chips).wait_recv()
    for s in range(steps):
        up(s, (z - s + chips) % chips).wait_send()
        down(s, (z + s) % chips).wait_send()


def half_gather(t, collective_id):
    size = lax.axis_size("chan")
    groups = lax.axis_size("ctx")
    chips = size // PER_Z
    assert chips % 2 == 0
    ups = downs = chips // 2
    block = (t.shape[0] * t.shape[1], t.shape[2])
    out = pl.pallas_call(
        functools.partial(half_gather_kernel, chips, groups),
        out_shape=jax.ShapeDtypeStruct((size // 2,) + block, t.dtype),
        in_specs=[pl.BlockSpec(memory_space=pltpu.VMEM)],
        out_specs=pl.BlockSpec(memory_space=pltpu.VMEM),
        scratch_shapes=[
            pltpu.VMEM(block, t.dtype),
            pltpu.SemaphoreType.DMA(()),
            pltpu.SemaphoreType.DMA(()),
            pltpu.SemaphoreType.DMA(()),
            pltpu.SemaphoreType.DMA((ups,)),
            pltpu.SemaphoreType.DMA((ups,)),
            pltpu.SemaphoreType.DMA((downs,)),
            pltpu.SemaphoreType.DMA((downs,)),
            pltpu.SemaphoreType.DMA(()),
            pltpu.SemaphoreType.DMA((groups - 1,)),
            pltpu.SemaphoreType.DMA((groups - 1,)),
        ],
        compiler_params=pltpu.CompilerParams(collective_id=collective_id, has_side_effects=True),
    )(t)
    return out.reshape(size // 2 * block[0], block[1])


def dft_table(double_len):
    step = 32
    hi_ids = jnp.arange(double_len // step, dtype=jnp.int32)[:, None]
    lo_ids = jnp.arange(step, dtype=jnp.int32)[:, None]
    cols = jnp.arange(double_len, dtype=jnp.int32)[None, :]
    scale = 2.0 * math.pi / double_len
    hi_angle = scale * (hi_ids * step * cols % double_len).astype(jnp.float32)
    lo_angle = scale * (lo_ids * cols % double_len).astype(jnp.float32)
    hc, hs = jnp.cos(hi_angle)[:, None], jnp.sin(hi_angle)[:, None]
    lc, ls = jnp.cos(lo_angle)[None], jnp.sin(lo_angle)[None]
    cos = (hc * lc - hs * ls).reshape(double_len, double_len)
    sin = (hs * lc + hc * ls).reshape(double_len, double_len)
    return jnp.concatenate([cos, -sin], 0).astype(jnp.bfloat16)


def body(inputs, w_in, conv_taps, skip_gain, filter_taps, w_out):
    span_len, width_dev = inputs.shape
    double_len = 2 * span_len
    groups = lax.axis_size("ctx")
    position = lax.axis_index("ctx")
    own = width_dev // groups

    with jax.named_scope("input_gather_and_filter_to_owner"):
        taps_t = filter_taps.T.reshape(groups, own, span_len)
        inputs_t, taps_t = chan_gather(inputs.T, taps_t, 0)

    with jax.named_scope("input_projection"):
        w_flat = w_in.reshape(w_in.shape[0], 3 * width_dev)
        proj_t = lax.dot_general(
            w_flat, inputs_t, (((0,), (0,)), ((), ())), preferred_element_type=jnp.float32
        ).astype(jnp.bfloat16)

    with jax.named_scope("projection_to_owner"):
        proj_t = proj_t.reshape(3, groups, own, span_len).transpose(1, 0, 2, 3)
        proj_t = ctx_exchange(proj_t, 3)

    with jax.named_scope("out_weight_columns"):
        w_late, proj_t = lax.optimization_barrier((w_out, proj_t))
        size = lax.axis_size("chan")
        same_core = [list(range(c, size, 2)) for c in range(2)]
        w_cols = lax.all_to_all(w_late, "chan", 1, 0, tiled=True, axis_index_groups=same_core)

    with jax.named_scope("short_conv"):
        start = position * own
        taps = lax.dynamic_slice_in_dim(conv_taps, start, own, axis=2)
        rim = jnp.pad(proj_t[:-1, :, :, span_len - (KERNEL - 1) :], ((1, 0), (0, 0), (0, 0), (0, 0)))
        padded = jnp.concatenate([rim, proj_t], 3)
        filtered = jnp.zeros(proj_t.shape, jnp.float32)
        for lag in range(KERNEL):
            start_row = KERNEL - 1 - lag
            filtered = filtered + taps[lag].astype(jnp.float32)[None, :, :, None] * padded[
                ..., start_row : start_row + span_len
            ].astype(jnp.float32)
        streams = filtered.astype(jnp.bfloat16)
        gate_out = streams[:, 0]
        gated_in = (streams[:, 1].astype(jnp.float32) * streams[:, 2].astype(jnp.float32)).astype(
            jnp.bfloat16
        )

    with jax.named_scope("spectra"):
        table = dft_table(double_len)
        forward_in = table[:, :span_len]
        spectra_in = jnp.einsum(
            "jdb,fb->jdf", gated_in, forward_in, preferred_element_type=jnp.float32
        ).astype(jnp.bfloat16)
        previous = jnp.pad(taps_t[:-1, :, 1:], ((1, 0), (0, 0), (0, 0)))
        padded_taps = jnp.concatenate(
            [taps_t, jnp.zeros((groups, own, 1), jnp.bfloat16), previous], 2
        )
        spectra_taps = jnp.einsum(
            "kdm,fm->kdf", padded_taps, table, preferred_element_type=jnp.float32
        ).astype(jnp.bfloat16)

    with jax.named_scope("mixture"):
        real_g = spectra_taps[:, :, :double_len].astype(jnp.float32)
        imag_g = spectra_taps[:, :, double_len:].astype(jnp.float32)
        real_u = spectra_in[:, :, :double_len].astype(jnp.float32)
        imag_u = spectra_in[:, :, double_len:].astype(jnp.float32)
        mixed = []
        for target in range(groups):
            acc_r = jnp.zeros((own, double_len), jnp.float32)
            acc_i = jnp.zeros((own, double_len), jnp.float32)
            for source in range(target + 1):
                lag = target - source
                acc_r = acc_r + (real_g[lag] * real_u[source] - imag_g[lag] * imag_u[source])
                acc_i = acc_i + (real_g[lag] * imag_u[source] + imag_g[lag] * real_u[source])
            mixed.append(jnp.concatenate([acc_r, acc_i], 1))
        mixture = jnp.stack(mixed, 0).astype(jnp.bfloat16)

    with jax.named_scope("inverse_and_gate"):
        long_out = jnp.einsum(
            "idf,fa->ida", mixture, forward_in, preferred_element_type=jnp.float32
        ) * (1.0 / double_len)
        gain = lax.dynamic_slice_in_dim(skip_gain, start, own)
        long_out = long_out + gain[None, :, None] * gated_in.astype(jnp.float32)
        gated_out = (gate_out.astype(jnp.float32) * long_out).astype(jnp.bfloat16)

    with jax.named_scope("output_projection"):
        w_cols, gated_out = lax.optimization_barrier((w_cols, gated_out))
        gathered = half_gather(gated_out, 1)
        partial = lax.dot_general(
            gathered, w_cols, (((0,), (0,)), ((), ())), preferred_element_type=jnp.float32
        )
        core = lax.axis_index("chan") % 2
        mine = lax.dynamic_slice_in_dim(partial, core * width_dev, width_dev, axis=1)
        other = lax.dynamic_slice_in_dim(partial, (1 - core) * width_dev, width_dev, axis=1)
        pairs = [(h, h + 1 - 2 * (h % 2)) for h in range(lax.axis_size("chan"))]
        result = (mine + lax.ppermute(other, "chan", pairs)).astype(jnp.bfloat16)
    return result


def solution(mesh):
    return jax.shard_map(
        body,
        mesh=mesh,
        in_specs=(
            P("ctx", "chan"),
            P(None, None, "chan"),
            P(None, None, "chan"),
            P("chan"),
            P("ctx", "chan"),
            P("chan", None),
        ),
        out_specs=P("ctx", "chan"),
        check_vma=False,
    )
```

```python
import math

import functools

import jax
import jax.numpy as jnp
from jax import lax
from jax.experimental import pallas as pl
from jax.experimental.pallas import tpu as pltpu
from jax.sharding import PartitionSpec as P

KERNEL = 3
MESH = pl.DeviceIdType.MESH
PER_Z = 4


def gather_kernel(chips, groups, *refs):
    if groups:
        (x_ref, t_ref, out_ref, t_out_ref, local_sem, cross_send, cross_recv, ring_send, ring_recv,
         sib_send, sib_recv, t_local_sem, t_send, t_recv) = refs
    else:
        (x_ref, out_ref, local_sem, cross_send, cross_recv, ring_send, ring_recv,
         sib_send, sib_recv) = refs
    row = lax.axis_index("ctx")
    me = lax.axis_index("chan")
    z = me // PER_Z
    y_lo = (me // 2) % 2
    core = me % 2
    way = 1 - 2 * core
    after = ((z + way + chips) % chips) * PER_Z + y_lo * 2 + core
    before = ((z - way + chips) % chips) * PER_Z + y_lo * 2 + core
    sibling = me + 1 - 2 * core
    across = me + 2 - 4 * y_lo
    diagonal = across + 1 - 2 * core
    partners = (sibling, across, diagonal)

    barrier = pltpu.get_barrier_semaphore()
    for peer in partners + (after, before):
        pl.semaphore_signal(barrier, inc=1, device_id=(row, peer), device_id_type=MESH)
    for peer in ctx_peers(groups) if groups else ():
        pl.semaphore_signal(barrier, inc=1, device_id=(peer, me), device_id_type=MESH)
    pl.semaphore_wait(barrier, 5 + max(groups - 1, 0))

    if groups:
        t_local, t_sends, t_receipts = exchange_copies(
            groups, t_ref, t_out_ref, t_local_sem, t_send, t_recv)
        t_local.start()
        for copy in t_sends:
            copy.start()

    local = pltpu.make_async_copy(x_ref, out_ref.at[me], local_sem)
    local.start()

    def cross(k, peer, slot):
        return pltpu.make_async_remote_copy(
            src_ref=x_ref, dst_ref=out_ref.at[slot], send_sem=cross_send.at[k],
            recv_sem=cross_recv.at[k], device_id=(row, peer), device_id_type=MESH)

    for k, peer in enumerate(partners):
        cross(k, peer, me).start()
    local.wait()
    for k, peer in enumerate(partners):
        cross(k, peer, me).wait_send()
        cross(k, peer, peer).wait_recv()

    last = chips // 2 - 1

    def part(chip, s, half):
        if s < last:
            return out_ref.at[pl.ds(pl.multiple_of(chip * PER_Z, PER_Z), PER_Z)]
        start = pl.multiple_of(chip * PER_Z + half * (PER_Z // 2), PER_Z // 2)
        return out_ref.at[pl.ds(start, PER_Z // 2)]

    def ring(s, chip):
        return pltpu.make_async_remote_copy(
            src_ref=part(chip, s, core), dst_ref=part(chip, s, core), send_sem=ring_send.at[s],
            recv_sem=ring_recv.at[s], device_id=(row, after), device_id_type=MESH)

    def sib(s, chip, half):
        return pltpu.make_async_remote_copy(
            src_ref=part(chip, s, half), dst_ref=part(chip, s, half), send_sem=sib_send.at[s],
            recv_sem=sib_recv.at[s], device_id=(row, sibling), device_id_type=MESH)

    for s in range(last + 1):
        sent = (z - way * s + chips) % chips
        got = (z - way * (s + 1) + chips) % chips
        ring(s, sent).start()
        ring(s, got).wait_recv()
        sib(s, got, core).start()

    for s in range(last + 1):
        sent = (z - way * s + chips) % chips
        got = (z - way * (s + 1) + chips) % chips
        theirs = (z + way * (s + 1) + chips) % chips
        ring(s, sent).wait_send()
        sib(s, got, core).wait_send()
        sib(s, theirs, 1 - core).wait_recv()

    if groups:
        t_local.wait()
        for copy, receipt in zip(t_sends, t_receipts):
            copy.wait_send()
            receipt.wait_recv()


def exchange_copies(groups, x_ref, out_ref, local_sem, send_sem, recv_sem):
    me = lax.axis_index("ctx")
    col = lax.axis_index("chan")
    local = pltpu.make_async_copy(x_ref.at[me], out_ref.at[me], local_sem)

    def send(k, peer, slot):
        return pltpu.make_async_remote_copy(
            src_ref=x_ref.at[peer], dst_ref=out_ref.at[slot], send_sem=send_sem.at[k - 1],
            recv_sem=recv_sem.at[k - 1], device_id=(peer, col), device_id_type=MESH)

    sends = [send(k, (me + k) % groups, me) for k in range(1, groups)]
    sources = [(me - k + groups) % groups for k in range(1, groups)]
    receipts = [send(k, source, source) for k, source in zip(range(1, groups), sources)]
    return local, sends, receipts


def ctx_peers(groups):
    me = lax.axis_index("ctx")
    return [(me + k) % groups for k in range(1, groups)]


def exchange_kernel(groups, x_ref, out_ref, local_sem, send_sem, recv_sem):
    col = lax.axis_index("chan")
    barrier = pltpu.get_barrier_semaphore()
    for peer in ctx_peers(groups):
        pl.semaphore_signal(barrier, inc=1, device_id=(peer, col), device_id_type=MESH)
    pl.semaphore_wait(barrier, groups - 1)
    local, sends, receipts = exchange_copies(groups, x_ref, out_ref, local_sem, send_sem, recv_sem)
    local.start()
    for copy in sends:
        copy.start()
    local.wait()
    for copy, receipt in zip(sends, receipts):
        copy.wait_send()
        receipt.wait_recv()


def ctx_exchange(x, collective_id):
    groups = lax.axis_size("ctx")
    return pl.pallas_call(
        functools.partial(exchange_kernel, groups),
        out_shape=jax.ShapeDtypeStruct(x.shape, x.dtype),
        in_specs=[pl.BlockSpec(memory_space=pltpu.VMEM)],
        out_specs=pl.BlockSpec(memory_space=pltpu.VMEM),
        scratch_shapes=[
            pltpu.SemaphoreType.DMA(()),
            pltpu.SemaphoreType.DMA((groups - 1,)),
            pltpu.SemaphoreType.DMA((groups - 1,)),
        ],
        compiler_params=pltpu.CompilerParams(collective_id=collective_id, has_side_effects=True),
    )(x)


def chan_gather(x, t, collective_id):
    size = lax.axis_size("chan")
    groups = lax.axis_size("ctx") if t is not None else 0
    chips = size // PER_Z
    longest = chips // 2
    assert chips % 2 == 0
    operands = (x,) if t is None else (x, t)
    out_shape = [jax.ShapeDtypeStruct((size,) + x.shape, x.dtype)]
    scratch = [
        pltpu.SemaphoreType.DMA(()),
        pltpu.SemaphoreType.DMA((3,)),
        pltpu.SemaphoreType.DMA((3,)),
        pltpu.SemaphoreType.DMA((longest,)),
        pltpu.SemaphoreType.DMA((longest,)),
        pltpu.SemaphoreType.DMA((longest,)),
        pltpu.SemaphoreType.DMA((longest,)),
    ]
    if t is not None:
        out_shape.append(jax.ShapeDtypeStruct(t.shape, t.dtype))
        scratch += [
            pltpu.SemaphoreType.DMA(()),
            pltpu.SemaphoreType.DMA((groups - 1,)),
            pltpu.SemaphoreType.DMA((groups - 1,)),
        ]
    outs = pl.pallas_call(
        functools.partial(gather_kernel, chips, groups),
        out_shape=tuple(out_shape),
        in_specs=[pl.BlockSpec(memory_space=pltpu.VMEM)] * len(operands),
        out_specs=[pl.BlockSpec(memory_space=pltpu.VMEM)] * len(out_shape),
        scratch_shapes=scratch,
        compiler_params=pltpu.CompilerParams(collective_id=collective_id, has_side_effects=True),
    )(*operands)
    gathered = outs[0].reshape(size * x.shape[0], x.shape[1])
    return gathered if t is None else (gathered, outs[1])


def half_gather_kernel(chips, groups, t_ref, out_ref, x_ref, local_sem, cross_send, cross_recv,
                       up_send, up_recv, down_send, down_recv, t_local_sem, t_send, t_recv):
    row = lax.axis_index("ctx")
    me = lax.axis_index("chan")
    z = me // PER_Z
    y_lo = (me // 2) % 2
    core = me % 2
    across = me + 2 - 4 * y_lo
    ahead = ((z + 1) % chips) * PER_Z + y_lo * 2 + core
    behind = ((z + chips - 1) % chips) * PER_Z + y_lo * 2 + core
    mine = me // 2
    theirs = across // 2

    barrier = pltpu.get_barrier_semaphore()
    for peer in (across, ahead, behind):
        pl.semaphore_signal(barrier, inc=1, device_id=(row, peer), device_id_type=MESH)
    for peer in ctx_peers(groups):
        pl.semaphore_signal(barrier, inc=1, device_id=(peer, me), device_id_type=MESH)
    pl.semaphore_wait(barrier, 3 + groups - 1)

    slab = t_ref.shape[1]

    def slot(g):
        return x_ref.at[pl.ds(pl.multiple_of(g * slab, slab), slab)]

    def give(k, peer, g):
        return pltpu.make_async_remote_copy(
            src_ref=t_ref.at[peer], dst_ref=slot(g), send_sem=t_send.at[k - 1],
            recv_sem=t_recv.at[k - 1], device_id=(peer, me), device_id_type=MESH)

    t_local = pltpu.make_async_copy(t_ref.at[row], slot(row), t_local_sem)
    t_local.start()
    for k in range(1, groups):
        give(k, (row + k) % groups, row).start()
    t_local.wait()
    for k in range(1, groups):
        give(k, (row + k) % groups, row).wait_send()
        source = (row - k + groups) % groups
        give(k, source, source).wait_recv()

    local = pltpu.make_async_copy(x_ref, out_ref.at[mine], local_sem)
    local.start()

    def cross(slot):
        return pltpu.make_async_remote_copy(
            src_ref=x_ref, dst_ref=out_ref.at[slot], send_sem=cross_send,
            recv_sem=cross_recv, device_id=(row, across), device_id_type=MESH)

    cross(mine).start()
    local.wait()
    cross(mine).wait_send()
    cross(theirs).wait_recv()

    def pair(chip):
        return out_ref.at[pl.ds(pl.multiple_of(chip * 2, 2), 2)]

    steps = chips // 2

    def piece(chip, s, half):
        if s < steps - 1:
            return pair(chip)
        return out_ref.at[pl.ds(chip * 2 + half, 1)]

    def up(s, chip):
        return pltpu.make_async_remote_copy(
            src_ref=piece(chip, s, 0), dst_ref=piece(chip, s, 0), send_sem=up_send.at[s],
            recv_sem=up_recv.at[s], device_id=(row, ahead), device_id_type=MESH)

    def down(s, chip):
        return pltpu.make_async_remote_copy(
            src_ref=piece(chip, s, 1), dst_ref=piece(chip, s, 1), send_sem=down_send.at[s],
            recv_sem=down_recv.at[s], device_id=(row, behind), device_id_type=MESH)

    for s in range(steps):
        if s > 0:
            up(s - 1, (z - s + chips) % chips).wait_recv()
        up(s, (z - s + chips) % chips).start()
        if s > 0:
            down(s - 1, (z + s) % chips).wait_recv()
        down(s, (z + s) % chips).start()
    up(steps - 1, (z - steps + chips) % chips).wait_recv()
    down(steps - 1, (z + steps) % chips).wait_recv()
    for s in range(steps):
        up(s, (z - s + chips) % chips).wait_send()
        down(s, (z + s) % chips).wait_send()


def half_gather(t, collective_id):
    size = lax.axis_size("chan")
    groups = lax.axis_size("ctx")
    chips = size // PER_Z
    assert chips % 2 == 0
    ups = downs = chips // 2
    block = (t.shape[0] * t.shape[1], t.shape[2])
    out = pl.pallas_call(
        functools.partial(half_gather_kernel, chips, groups),
        out_shape=jax.ShapeDtypeStruct((size // 2,) + block, t.dtype),
        in_specs=[pl.BlockSpec(memory_space=pltpu.VMEM)],
        out_specs=pl.BlockSpec(memory_space=pltpu.VMEM),
        scratch_shapes=[
            pltpu.VMEM(block, t.dtype),
            pltpu.SemaphoreType.DMA(()),
            pltpu.SemaphoreType.DMA(()),
            pltpu.SemaphoreType.DMA(()),
            pltpu.SemaphoreType.DMA((ups,)),
            pltpu.SemaphoreType.DMA((ups,)),
            pltpu.SemaphoreType.DMA((downs,)),
            pltpu.SemaphoreType.DMA((downs,)),
            pltpu.SemaphoreType.DMA(()),
            pltpu.SemaphoreType.DMA((groups - 1,)),
            pltpu.SemaphoreType.DMA((groups - 1,)),
        ],
        compiler_params=pltpu.CompilerParams(collective_id=collective_id, has_side_effects=True),
    )(t)
    return out.reshape(size // 2 * block[0], block[1])


def dft_table(double_len):
    step = 32
    hi_ids = jnp.arange(double_len // step, dtype=jnp.int32)[:, None]
    lo_ids = jnp.arange(step, dtype=jnp.int32)[:, None]
    cols = jnp.arange(double_len, dtype=jnp.int32)[None, :]
    scale = 2.0 * math.pi / double_len
    hi_angle = scale * (hi_ids * step * cols % double_len).astype(jnp.float32)
    lo_angle = scale * (lo_ids * cols % double_len).astype(jnp.float32)
    hc, hs = jnp.cos(hi_angle)[:, None], jnp.sin(hi_angle)[:, None]
    lc, ls = jnp.cos(lo_angle)[None], jnp.sin(lo_angle)[None]
    cos = (hc * lc - hs * ls).reshape(double_len, double_len)
    sin = (hs * lc + hc * ls).reshape(double_len, double_len)
    return jnp.concatenate([cos, -sin], 0).astype(jnp.bfloat16)


def body(inputs, w_in, conv_taps, skip_gain, filter_taps, w_out):
    span_len, width_dev = inputs.shape
    double_len = 2 * span_len
    groups = lax.axis_size("ctx")
    position = lax.axis_index("ctx")
    own = width_dev // groups

    with jax.named_scope("input_gather_and_filter_to_owner"):
        taps_t = filter_taps.T.reshape(groups, own, span_len)
        inputs_t, taps_t = chan_gather(inputs.T, taps_t, 0)

    with jax.named_scope("input_projection"):
        w_flat = w_in.reshape(w_in.shape[0], 3 * width_dev)
        proj_t = lax.dot_general(
            w_flat, inputs_t, (((0,), (0,)), ((), ())), preferred_element_type=jnp.float32
        ).astype(jnp.bfloat16)

    with jax.named_scope("projection_to_owner"):
        proj_t = proj_t.reshape(3, groups, own, span_len).transpose(1, 0, 2, 3)
        proj_t = ctx_exchange(proj_t, 3)

    with jax.named_scope("out_weight_columns"):
        w_late, proj_t = lax.optimization_barrier((w_out, proj_t))
        size = lax.axis_size("chan")
        same_core = [list(range(c, size, 2)) for c in range(2)]
        w_cols = lax.all_to_all(w_late, "chan", 1, 0, tiled=True, axis_index_groups=same_core)

    with jax.named_scope("short_conv"):
        start = position * own
        taps = lax.dynamic_slice_in_dim(conv_taps, start, own, axis=2)
        rim = jnp.pad(proj_t[:-1, :, :, span_len - (KERNEL - 1) :], ((1, 0), (0, 0), (0, 0), (0, 0)))
        padded = jnp.concatenate([rim, proj_t], 3)
        filtered = jnp.zeros(proj_t.shape, jnp.float32)
        for lag in range(KERNEL):
            start_row = KERNEL - 1 - lag
            filtered = filtered + taps[lag].astype(jnp.float32)[None, :, :, None] * padded[
                ..., start_row : start_row + span_len
            ].astype(jnp.float32)
        streams = filtered.astype(jnp.bfloat16)
        gate_out = streams[:, 0]
        gated_in = (streams[:, 1].astype(jnp.float32) * streams[:, 2].astype(jnp.float32)).astype(
            jnp.bfloat16
        )

    with jax.named_scope("spectra"):
        table = dft_table(double_len)
        forward_in = table[:, :span_len]
        spectra_in = jnp.einsum(
            "jdb,fb->jdf", gated_in, forward_in, preferred_element_type=jnp.float32
        ).astype(jnp.bfloat16)
        previous = jnp.pad(taps_t[:-1, :, 1:], ((1, 0), (0, 0), (0, 0)))
        padded_taps = jnp.concatenate(
            [taps_t, jnp.zeros((groups, own, 1), jnp.bfloat16), previous], 2
        )
        spectra_taps = jnp.einsum(
            "kdm,fm->kdf", padded_taps, table, preferred_element_type=jnp.float32
        ).astype(jnp.bfloat16)

    with jax.named_scope("mixture"):
        real_g = spectra_taps[:, :, :double_len].astype(jnp.float32)
        imag_g = spectra_taps[:, :, double_len:].astype(jnp.float32)
        real_u = spectra_in[:, :, :double_len].astype(jnp.float32)
        imag_u = spectra_in[:, :, double_len:].astype(jnp.float32)
        mixed = []
        for target in range(groups):
            acc_r = jnp.zeros((own, double_len), jnp.float32)
            acc_i = jnp.zeros((own, double_len), jnp.float32)
            for source in range(target + 1):
                lag = target - source
                acc_r = acc_r + (real_g[lag] * real_u[source] - imag_g[lag] * imag_u[source])
                acc_i = acc_i + (real_g[lag] * imag_u[source] + imag_g[lag] * real_u[source])
            mixed.append(jnp.concatenate([acc_r, acc_i], 1))
        mixture = jnp.stack(mixed, 0).astype(jnp.bfloat16)

    with jax.named_scope("inverse_and_gate"):
        long_out = jnp.einsum(
            "idf,fa->ida", mixture, forward_in, preferred_element_type=jnp.float32
        ) * (1.0 / double_len)
        gain = lax.dynamic_slice_in_dim(skip_gain, start, own)
        long_out = long_out + gain[None, :, None] * gated_in.astype(jnp.float32)
        gated_out = (gate_out.astype(jnp.float32) * long_out).astype(jnp.bfloat16)

    with jax.named_scope("output_projection"):
        gathered = half_gather(gated_out, 1)
        partial = lax.dot_general(
            gathered, w_cols, (((0,), (0,)), ((), ())), preferred_element_type=jnp.float32
        )
        core = lax.axis_index("chan") % 2
        mine = lax.dynamic_slice_in_dim(partial, core * width_dev, width_dev, axis=1)
        other = lax.dynamic_slice_in_dim(partial, (1 - core) * width_dev, width_dev, axis=1)
        pairs = [(h, h + 1 - 2 * (h % 2)) for h in range(lax.axis_size("chan"))]
        result = (mine + lax.ppermute(other, "chan", pairs)).astype(jnp.bfloat16)
    return result


def solution(mesh):
    return jax.shard_map(
        body,
        mesh=mesh,
        in_specs=(
            P("ctx", "chan"),
            P(None, None, "chan"),
            P(None, None, "chan"),
            P("chan"),
            P("ctx", "chan"),
            P("chan", None),
        ),
        out_specs=P("ctx", "chan"),
        check_vma=False,
    )
```

```python
import math

import functools

import jax
import jax.numpy as jnp
from jax import lax
from jax.experimental import pallas as pl
from jax.experimental.pallas import tpu as pltpu
from jax.sharding import PartitionSpec as P

KERNEL = 3
MESH = pl.DeviceIdType.MESH
PER_Z = 4


def gather_kernel(chips, groups, *refs):
    if groups:
        (x_ref, t_ref, out_ref, t_out_ref, local_sem, cross_send, cross_recv, ring_send, ring_recv,
         sib_send, sib_recv, t_local_sem, t_send, t_recv) = refs
    else:
        (x_ref, out_ref, local_sem, cross_send, cross_recv, ring_send, ring_recv,
         sib_send, sib_recv) = refs
    row = lax.axis_index("ctx")
    me = lax.axis_index("chan")
    z = me // PER_Z
    y_lo = (me // 2) % 2
    core = me % 2
    way = 1 - 2 * core
    after = ((z + way + chips) % chips) * PER_Z + y_lo * 2 + core
    before = ((z - way + chips) % chips) * PER_Z + y_lo * 2 + core
    sibling = me + 1 - 2 * core
    across = me + 2 - 4 * y_lo
    diagonal = across + 1 - 2 * core
    partners = (sibling, across, diagonal)

    barrier = pltpu.get_barrier_semaphore()
    for peer in partners + (after, before):
        pl.semaphore_signal(barrier, inc=1, device_id=(row, peer), device_id_type=MESH)
    for peer in ctx_peers(groups) if groups else ():
        pl.semaphore_signal(barrier, inc=1, device_id=(peer, me), device_id_type=MESH)
    pl.semaphore_wait(barrier, 5 + max(groups - 1, 0))

    if groups:
        t_local, t_sends, t_receipts = exchange_copies(
            groups, t_ref, t_out_ref, t_local_sem, t_send, t_recv)
        t_local.start()
        for copy in t_sends:
            copy.start()

    local = pltpu.make_async_copy(x_ref, out_ref.at[me], local_sem)
    local.start()

    def cross(k, peer, slot):
        return pltpu.make_async_remote_copy(
            src_ref=x_ref, dst_ref=out_ref.at[slot], send_sem=cross_send.at[k],
            recv_sem=cross_recv.at[k], device_id=(row, peer), device_id_type=MESH)

    for k, peer in enumerate(partners):
        cross(k, peer, me).start()
    local.wait()
    for k, peer in enumerate(partners):
        cross(k, peer, me).wait_send()
        cross(k, peer, peer).wait_recv()

    last = chips // 2 - 1

    def part(chip, s, half):
        if s < last:
            return out_ref.at[pl.ds(pl.multiple_of(chip * PER_Z, PER_Z), PER_Z)]
        start = pl.multiple_of(chip * PER_Z + half * (PER_Z // 2), PER_Z // 2)
        return out_ref.at[pl.ds(start, PER_Z // 2)]

    def ring(s, chip):
        return pltpu.make_async_remote_copy(
            src_ref=part(chip, s, core), dst_ref=part(chip, s, core), send_sem=ring_send.at[s],
            recv_sem=ring_recv.at[s], device_id=(row, after), device_id_type=MESH)

    def sib(s, chip, half):
        return pltpu.make_async_remote_copy(
            src_ref=part(chip, s, half), dst_ref=part(chip, s, half), send_sem=sib_send.at[s],
            recv_sem=sib_recv.at[s], device_id=(row, sibling), device_id_type=MESH)

    for s in range(last + 1):
        sent = (z - way * s + chips) % chips
        got = (z - way * (s + 1) + chips) % chips
        ring(s, sent).start()
        ring(s, got).wait_recv()
        sib(s, got, core).start()

    for s in range(last + 1):
        sent = (z - way * s + chips) % chips
        got = (z - way * (s + 1) + chips) % chips
        theirs = (z + way * (s + 1) + chips) % chips
        ring(s, sent).wait_send()
        sib(s, got, core).wait_send()
        sib(s, theirs, 1 - core).wait_recv()

    if groups:
        t_local.wait()
        for copy, receipt in zip(t_sends, t_receipts):
            copy.wait_send()
            receipt.wait_recv()


def exchange_copies(groups, x_ref, out_ref, local_sem, send_sem, recv_sem):
    me = lax.axis_index("ctx")
    col = lax.axis_index("chan")
    local = pltpu.make_async_copy(x_ref.at[me], out_ref.at[me], local_sem)

    def send(k, peer, slot):
        return pltpu.make_async_remote_copy(
            src_ref=x_ref.at[peer], dst_ref=out_ref.at[slot], send_sem=send_sem.at[k - 1],
            recv_sem=recv_sem.at[k - 1], device_id=(peer, col), device_id_type=MESH)

    sends = [send(k, (me + k) % groups, me) for k in range(1, groups)]
    sources = [(me - k + groups) % groups for k in range(1, groups)]
    receipts = [send(k, source, source) for k, source in zip(range(1, groups), sources)]
    return local, sends, receipts


def ctx_peers(groups):
    me = lax.axis_index("ctx")
    return [(me + k) % groups for k in range(1, groups)]


def exchange_kernel(groups, x_ref, out_ref, local_sem, send_sem, recv_sem):
    col = lax.axis_index("chan")
    barrier = pltpu.get_barrier_semaphore()
    for peer in ctx_peers(groups):
        pl.semaphore_signal(barrier, inc=1, device_id=(peer, col), device_id_type=MESH)
    pl.semaphore_wait(barrier, groups - 1)
    local, sends, receipts = exchange_copies(groups, x_ref, out_ref, local_sem, send_sem, recv_sem)
    local.start()
    for copy in sends:
        copy.start()
    local.wait()
    for copy, receipt in zip(sends, receipts):
        copy.wait_send()
        receipt.wait_recv()


def ctx_exchange(x, collective_id):
    groups = lax.axis_size("ctx")
    return pl.pallas_call(
        functools.partial(exchange_kernel, groups),
        out_shape=jax.ShapeDtypeStruct(x.shape, x.dtype),
        in_specs=[pl.BlockSpec(memory_space=pltpu.VMEM)],
        out_specs=pl.BlockSpec(memory_space=pltpu.VMEM),
        scratch_shapes=[
            pltpu.SemaphoreType.DMA(()),
            pltpu.SemaphoreType.DMA((groups - 1,)),
            pltpu.SemaphoreType.DMA((groups - 1,)),
        ],
        compiler_params=pltpu.CompilerParams(collective_id=collective_id, has_side_effects=True),
    )(x)


def chan_gather(x, t, collective_id):
    size = lax.axis_size("chan")
    groups = lax.axis_size("ctx") if t is not None else 0
    chips = size // PER_Z
    longest = chips // 2
    assert chips % 2 == 0
    operands = (x,) if t is None else (x, t)
    out_shape = [jax.ShapeDtypeStruct((size,) + x.shape, x.dtype)]
    scratch = [
        pltpu.SemaphoreType.DMA(()),
        pltpu.SemaphoreType.DMA((3,)),
        pltpu.SemaphoreType.DMA((3,)),
        pltpu.SemaphoreType.DMA((longest,)),
        pltpu.SemaphoreType.DMA((longest,)),
        pltpu.SemaphoreType.DMA((longest,)),
        pltpu.SemaphoreType.DMA((longest,)),
    ]
    if t is not None:
        out_shape.append(jax.ShapeDtypeStruct(t.shape, t.dtype))
        scratch += [
            pltpu.SemaphoreType.DMA(()),
            pltpu.SemaphoreType.DMA((groups - 1,)),
            pltpu.SemaphoreType.DMA((groups - 1,)),
        ]
    outs = pl.pallas_call(
        functools.partial(gather_kernel, chips, groups),
        out_shape=tuple(out_shape),
        in_specs=[pl.BlockSpec(memory_space=pltpu.VMEM)] * len(operands),
        out_specs=[pl.BlockSpec(memory_space=pltpu.VMEM)] * len(out_shape),
        scratch_shapes=scratch,
        compiler_params=pltpu.CompilerParams(collective_id=collective_id, has_side_effects=True),
    )(*operands)
    gathered = outs[0].reshape(size * x.shape[0], x.shape[1])
    return gathered if t is None else (gathered, outs[1])


def half_gather_kernel(chips, groups, t_ref, out_ref, x_ref, local_sem, cross_send, cross_recv,
                       up_send, up_recv, down_send, down_recv, t_local_sem, t_send, t_recv):
    row = lax.axis_index("ctx")
    me = lax.axis_index("chan")
    z = me // PER_Z
    y_lo = (me // 2) % 2
    core = me % 2
    across = me + 2 - 4 * y_lo
    ahead = ((z + 1) % chips) * PER_Z + y_lo * 2 + core
    behind = ((z + chips - 1) % chips) * PER_Z + y_lo * 2 + core
    mine = me // 2
    theirs = across // 2

    barrier = pltpu.get_barrier_semaphore()
    for peer in (across, ahead, behind):
        pl.semaphore_signal(barrier, inc=1, device_id=(row, peer), device_id_type=MESH)
    for peer in ctx_peers(groups):
        pl.semaphore_signal(barrier, inc=1, device_id=(peer, me), device_id_type=MESH)
    pl.semaphore_wait(barrier, 3 + groups - 1)

    slab = t_ref.shape[1]

    def slot(g):
        return x_ref.at[pl.ds(pl.multiple_of(g * slab, slab), slab)]

    def give(k, peer, g):
        return pltpu.make_async_remote_copy(
            src_ref=t_ref.at[peer], dst_ref=slot(g), send_sem=t_send.at[k - 1],
            recv_sem=t_recv.at[k - 1], device_id=(peer, me), device_id_type=MESH)

    t_local = pltpu.make_async_copy(t_ref.at[row], slot(row), t_local_sem)
    t_local.start()
    for k in range(1, groups):
        give(k, (row + k) % groups, row).start()
    t_local.wait()
    for k in range(1, groups):
        give(k, (row + k) % groups, row).wait_send()
        source = (row - k + groups) % groups
        give(k, source, source).wait_recv()

    local = pltpu.make_async_copy(x_ref, out_ref.at[mine], local_sem)
    local.start()

    def cross(slot):
        return pltpu.make_async_remote_copy(
            src_ref=x_ref, dst_ref=out_ref.at[slot], send_sem=cross_send,
            recv_sem=cross_recv, device_id=(row, across), device_id_type=MESH)

    cross(mine).start()
    local.wait()
    cross(mine).wait_send()
    cross(theirs).wait_recv()

    def pair(chip):
        return out_ref.at[pl.ds(pl.multiple_of(chip * 2, 2), 2)]

    steps = chips // 2

    def piece(chip, s, half):
        if s < steps - 1:
            return pair(chip)
        return out_ref.at[pl.ds(chip * 2 + half, 1)]

    def up(s, chip):
        return pltpu.make_async_remote_copy(
            src_ref=piece(chip, s, 0), dst_ref=piece(chip, s, 0), send_sem=up_send.at[s],
            recv_sem=up_recv.at[s], device_id=(row, ahead), device_id_type=MESH)

    def down(s, chip):
        return pltpu.make_async_remote_copy(
            src_ref=piece(chip, s, 1), dst_ref=piece(chip, s, 1), send_sem=down_send.at[s],
            recv_sem=down_recv.at[s], device_id=(row, behind), device_id_type=MESH)

    for s in range(steps):
        if s > 0:
            up(s - 1, (z - s + chips) % chips).wait_recv()
        up(s, (z - s + chips) % chips).start()
        if s > 0:
            down(s - 1, (z + s) % chips).wait_recv()
        down(s, (z + s) % chips).start()
    up(steps - 1, (z - steps + chips) % chips).wait_recv()
    down(steps - 1, (z + steps) % chips).wait_recv()
    for s in range(steps):
        up(s, (z - s + chips) % chips).wait_send()
        down(s, (z + s) % chips).wait_send()


def half_gather(t, collective_id):
    size = lax.axis_size("chan")
    groups = lax.axis_size("ctx")
    chips = size // PER_Z
    assert chips % 2 == 0
    ups = downs = chips // 2
    block = (t.shape[0] * t.shape[1], t.shape[2])
    out = pl.pallas_call(
        functools.partial(half_gather_kernel, chips, groups),
        out_shape=jax.ShapeDtypeStruct((size // 2,) + block, t.dtype),
        in_specs=[pl.BlockSpec(memory_space=pltpu.VMEM)],
        out_specs=pl.BlockSpec(memory_space=pltpu.VMEM),
        scratch_shapes=[
            pltpu.VMEM(block, t.dtype),
            pltpu.SemaphoreType.DMA(()),
            pltpu.SemaphoreType.DMA(()),
            pltpu.SemaphoreType.DMA(()),
            pltpu.SemaphoreType.DMA((ups,)),
            pltpu.SemaphoreType.DMA((ups,)),
            pltpu.SemaphoreType.DMA((downs,)),
            pltpu.SemaphoreType.DMA((downs,)),
            pltpu.SemaphoreType.DMA(()),
            pltpu.SemaphoreType.DMA((groups - 1,)),
            pltpu.SemaphoreType.DMA((groups - 1,)),
        ],
        compiler_params=pltpu.CompilerParams(collective_id=collective_id, has_side_effects=True),
    )(t)
    return out.reshape(size // 2 * block[0], block[1])


def dft_table(double_len):
    step = 32
    hi_ids = jnp.arange(double_len // step, dtype=jnp.int32)[:, None]
    lo_ids = jnp.arange(step, dtype=jnp.int32)[:, None]
    cols = jnp.arange(double_len, dtype=jnp.int32)[None, :]
    scale = 2.0 * math.pi / double_len
    hi_angle = scale * (hi_ids * step * cols % double_len).astype(jnp.float32)
    lo_angle = scale * (lo_ids * cols % double_len).astype(jnp.float32)
    hc, hs = jnp.cos(hi_angle)[:, None], jnp.sin(hi_angle)[:, None]
    lc, ls = jnp.cos(lo_angle)[None], jnp.sin(lo_angle)[None]
    cos = (hc * lc - hs * ls).reshape(double_len, double_len)
    sin = (hs * lc + hc * ls).reshape(double_len, double_len)
    return jnp.concatenate([cos, -sin], 0).astype(jnp.bfloat16)


def body(inputs, w_in, conv_taps, skip_gain, filter_taps, w_out):
    span_len, width_dev = inputs.shape
    double_len = 2 * span_len
    groups = lax.axis_size("ctx")
    position = lax.axis_index("ctx")
    own = width_dev // groups

    with jax.named_scope("input_gather_and_filter_to_owner"):
        taps_t = filter_taps.T.reshape(groups, own, span_len)
        inputs_t, taps_t = chan_gather(inputs.T, taps_t, 0)

    with jax.named_scope("input_projection"):
        w_flat = w_in.reshape(w_in.shape[0], 3 * width_dev)
        proj_t = lax.dot_general(
            w_flat, inputs_t, (((0,), (0,)), ((), ())), preferred_element_type=jnp.float32
        ).astype(jnp.bfloat16)

    with jax.named_scope("projection_to_owner"):
        proj_t = proj_t.reshape(3, groups, own, span_len).transpose(1, 0, 2, 3)
        proj_t = ctx_exchange(proj_t, 3)

    with jax.named_scope("out_weight_columns"):
        w_late, proj_t = lax.optimization_barrier((w_out, proj_t))
        size = lax.axis_size("chan")
        same_core = [list(range(c, size, 2)) for c in range(2)]
        w_cols = lax.all_to_all(w_late, "chan", 1, 0, tiled=True, axis_index_groups=same_core)

    with jax.named_scope("short_conv"):
        start = position * own
        taps = lax.dynamic_slice_in_dim(conv_taps, start, own, axis=2)
        rim = jnp.pad(proj_t[:-1, :, :, span_len - (KERNEL - 1) :], ((1, 0), (0, 0), (0, 0), (0, 0)))
        padded = jnp.concatenate([rim, proj_t], 3)
        filtered = jnp.zeros(proj_t.shape, jnp.float32)
        for lag in range(KERNEL):
            start_row = KERNEL - 1 - lag
            filtered = filtered + taps[lag].astype(jnp.float32)[None, :, :, None] * padded[
                ..., start_row : start_row + span_len
            ].astype(jnp.float32)
        streams = filtered.astype(jnp.bfloat16)
        gate_out = streams[:, 0]
        gated_in = (streams[:, 1].astype(jnp.float32) * streams[:, 2].astype(jnp.float32)).astype(
            jnp.bfloat16
        )

    with jax.named_scope("spectra"):
        table = dft_table(double_len)
        forward_in = table[:, :span_len]
        spectra_in = jnp.einsum(
            "jdb,fb->jdf", gated_in, forward_in, preferred_element_type=jnp.float32
        ).astype(jnp.bfloat16)
        previous = jnp.pad(taps_t[:-1, :, 1:], ((1, 0), (0, 0), (0, 0)))
        padded_taps = jnp.concatenate(
            [taps_t, jnp.zeros((groups, own, 1), jnp.bfloat16), previous], 2
        )
        spectra_taps = jnp.einsum(
            "kdm,fm->kdf", padded_taps, table, preferred_element_type=jnp.float32
        ).astype(jnp.bfloat16)

    with jax.named_scope("mixture"):
        real_g = spectra_taps[:, :, :double_len].astype(jnp.float32)
        imag_g = spectra_taps[:, :, double_len:].astype(jnp.float32)
        real_u = spectra_in[:, :, :double_len].astype(jnp.float32)
        imag_u = spectra_in[:, :, double_len:].astype(jnp.float32)
        acc_r = jnp.zeros(real_u.shape, jnp.float32)
        acc_i = jnp.zeros(real_u.shape, jnp.float32)
        for lag in range(groups):
            keep = groups - lag
            shift = ((lag, 0), (0, 0), (0, 0))
            acc_r = acc_r + jnp.pad(
                real_g[lag] * real_u[:keep] - imag_g[lag] * imag_u[:keep], shift)
            acc_i = acc_i + jnp.pad(
                real_g[lag] * imag_u[:keep] + imag_g[lag] * real_u[:keep], shift)
        mixture = jnp.concatenate([acc_r, acc_i], 2).astype(jnp.bfloat16)

    with jax.named_scope("inverse_and_gate"):
        long_out = jnp.einsum(
            "idf,fa->ida", mixture, forward_in, preferred_element_type=jnp.float32
        ) * (1.0 / double_len)
        gain = lax.dynamic_slice_in_dim(skip_gain, start, own)
        long_out = long_out + gain[None, :, None] * gated_in.astype(jnp.float32)
        gated_out = (gate_out.astype(jnp.float32) * long_out).astype(jnp.bfloat16)

    with jax.named_scope("output_projection"):
        gathered = half_gather(gated_out, 1)
        partial = lax.dot_general(
            gathered, w_cols, (((0,), (0,)), ((), ())), preferred_element_type=jnp.float32
        )
        core = lax.axis_index("chan") % 2
        mine = lax.dynamic_slice_in_dim(partial, core * width_dev, width_dev, axis=1)
        other = lax.dynamic_slice_in_dim(partial, (1 - core) * width_dev, width_dev, axis=1)
        pairs = [(h, h + 1 - 2 * (h % 2)) for h in range(lax.axis_size("chan"))]
        result = (mine + lax.ppermute(other, "chan", pairs)).astype(jnp.bfloat16)
    return result


def solution(mesh):
    return jax.shard_map(
        body,
        mesh=mesh,
        in_specs=(
            P("ctx", "chan"),
            P(None, None, "chan"),
            P(None, None, "chan"),
            P("chan"),
            P("ctx", "chan"),
            P("chan", None),
        ),
        out_specs=P("ctx", "chan"),
        check_vma=False,
    )
```

```python
import math

import functools

import jax
import jax.numpy as jnp
from jax import lax
from jax.experimental import pallas as pl
from jax.experimental.pallas import tpu as pltpu
from jax.sharding import PartitionSpec as P

KERNEL = 3
MESH = pl.DeviceIdType.MESH
PER_Z = 4


def gather_kernel(chips, groups, *refs):
    if groups:
        (x_ref, t_ref, out_ref, t_out_ref, local_sem, cross_send, cross_recv, ring_send, ring_recv,
         sib_send, sib_recv, t_local_sem, t_send, t_recv) = refs
    else:
        (x_ref, out_ref, local_sem, cross_send, cross_recv, ring_send, ring_recv,
         sib_send, sib_recv) = refs
    row = lax.axis_index("ctx")
    me = lax.axis_index("chan")
    z = me // PER_Z
    y_lo = (me // 2) % 2
    core = me % 2
    way = 1 - 2 * core
    after = ((z + way + chips) % chips) * PER_Z + y_lo * 2 + core
    before = ((z - way + chips) % chips) * PER_Z + y_lo * 2 + core
    sibling = me + 1 - 2 * core
    across = me + 2 - 4 * y_lo
    diagonal = across + 1 - 2 * core
    partners = (sibling, across, diagonal)

    barrier = pltpu.get_barrier_semaphore()
    for peer in partners + (after, before):
        pl.semaphore_signal(barrier, inc=1, device_id=(row, peer), device_id_type=MESH)
    for peer in ctx_peers(groups) if groups else ():
        pl.semaphore_signal(barrier, inc=1, device_id=(peer, me), device_id_type=MESH)
    pl.semaphore_wait(barrier, 5 + max(groups - 1, 0))

    if groups:
        t_local, t_sends, t_receipts = exchange_copies(
            groups, t_ref, t_out_ref, t_local_sem, t_send, t_recv)
        t_local.start()
        for copy in t_sends:
            copy.start()

    local = pltpu.make_async_copy(x_ref, out_ref.at[me], local_sem)
    local.start()

    def cross(k, peer, slot):
        return pltpu.make_async_remote_copy(
            src_ref=x_ref, dst_ref=out_ref.at[slot], send_sem=cross_send.at[k],
            recv_sem=cross_recv.at[k], device_id=(row, peer), device_id_type=MESH)

    for k, peer in enumerate(partners):
        cross(k, peer, me).start()
    local.wait()
    for k, peer in enumerate(partners):
        cross(k, peer, me).wait_send()
        cross(k, peer, peer).wait_recv()

    last = chips // 2 - 1

    def part(chip, s, half):
        if s < last:
            return out_ref.at[pl.ds(pl.multiple_of(chip * PER_Z, PER_Z), PER_Z)]
        start = pl.multiple_of(chip * PER_Z + half * (PER_Z // 2), PER_Z // 2)
        return out_ref.at[pl.ds(start, PER_Z // 2)]

    def ring(s, chip):
        return pltpu.make_async_remote_copy(
            src_ref=part(chip, s, core), dst_ref=part(chip, s, core), send_sem=ring_send.at[s],
            recv_sem=ring_recv.at[s], device_id=(row, after), device_id_type=MESH)

    def sib(s, chip, half):
        return pltpu.make_async_remote_copy(
            src_ref=part(chip, s, half), dst_ref=part(chip, s, half), send_sem=sib_send.at[s],
            recv_sem=sib_recv.at[s], device_id=(row, sibling), device_id_type=MESH)

    for s in range(last + 1):
        sent = (z - way * s + chips) % chips
        got = (z - way * (s + 1) + chips) % chips
        ring(s, sent).start()
        ring(s, got).wait_recv()
        sib(s, got, core).start()

    for s in range(last + 1):
        sent = (z - way * s + chips) % chips
        got = (z - way * (s + 1) + chips) % chips
        theirs = (z + way * (s + 1) + chips) % chips
        ring(s, sent).wait_send()
        sib(s, got, core).wait_send()
        sib(s, theirs, 1 - core).wait_recv()

    if groups:
        t_local.wait()
        for copy, receipt in zip(t_sends, t_receipts):
            copy.wait_send()
            receipt.wait_recv()


def exchange_copies(groups, x_ref, out_ref, local_sem, send_sem, recv_sem):
    me = lax.axis_index("ctx")
    col = lax.axis_index("chan")
    local = pltpu.make_async_copy(x_ref.at[me], out_ref.at[me], local_sem)

    def send(k, peer, slot):
        return pltpu.make_async_remote_copy(
            src_ref=x_ref.at[peer], dst_ref=out_ref.at[slot], send_sem=send_sem.at[k - 1],
            recv_sem=recv_sem.at[k - 1], device_id=(peer, col), device_id_type=MESH)

    sends = [send(k, (me + k) % groups, me) for k in range(1, groups)]
    sources = [(me - k + groups) % groups for k in range(1, groups)]
    receipts = [send(k, source, source) for k, source in zip(range(1, groups), sources)]
    return local, sends, receipts


def ctx_peers(groups):
    me = lax.axis_index("ctx")
    return [(me + k) % groups for k in range(1, groups)]


def exchange_kernel(groups, x_ref, out_ref, local_sem, send_sem, recv_sem):
    col = lax.axis_index("chan")
    barrier = pltpu.get_barrier_semaphore()
    for peer in ctx_peers(groups):
        pl.semaphore_signal(barrier, inc=1, device_id=(peer, col), device_id_type=MESH)
    pl.semaphore_wait(barrier, groups - 1)
    local, sends, receipts = exchange_copies(groups, x_ref, out_ref, local_sem, send_sem, recv_sem)
    local.start()
    for copy in sends:
        copy.start()
    local.wait()
    for copy, receipt in zip(sends, receipts):
        copy.wait_send()
        receipt.wait_recv()


def ctx_exchange(x, collective_id):
    groups = lax.axis_size("ctx")
    return pl.pallas_call(
        functools.partial(exchange_kernel, groups),
        out_shape=jax.ShapeDtypeStruct(x.shape, x.dtype),
        in_specs=[pl.BlockSpec(memory_space=pltpu.VMEM)],
        out_specs=pl.BlockSpec(memory_space=pltpu.VMEM),
        scratch_shapes=[
            pltpu.SemaphoreType.DMA(()),
            pltpu.SemaphoreType.DMA((groups - 1,)),
            pltpu.SemaphoreType.DMA((groups - 1,)),
        ],
        compiler_params=pltpu.CompilerParams(collective_id=collective_id, has_side_effects=True),
    )(x)


def chan_gather(x, t, collective_id):
    size = lax.axis_size("chan")
    groups = lax.axis_size("ctx") if t is not None else 0
    chips = size // PER_Z
    longest = chips // 2
    assert chips % 2 == 0
    operands = (x,) if t is None else (x, t)
    out_shape = [jax.ShapeDtypeStruct((size,) + x.shape, x.dtype)]
    scratch = [
        pltpu.SemaphoreType.DMA(()),
        pltpu.SemaphoreType.DMA((3,)),
        pltpu.SemaphoreType.DMA((3,)),
        pltpu.SemaphoreType.DMA((longest,)),
        pltpu.SemaphoreType.DMA((longest,)),
        pltpu.SemaphoreType.DMA((longest,)),
        pltpu.SemaphoreType.DMA((longest,)),
    ]
    if t is not None:
        out_shape.append(jax.ShapeDtypeStruct(t.shape, t.dtype))
        scratch += [
            pltpu.SemaphoreType.DMA(()),
            pltpu.SemaphoreType.DMA((groups - 1,)),
            pltpu.SemaphoreType.DMA((groups - 1,)),
        ]
    outs = pl.pallas_call(
        functools.partial(gather_kernel, chips, groups),
        out_shape=tuple(out_shape),
        in_specs=[pl.BlockSpec(memory_space=pltpu.VMEM)] * len(operands),
        out_specs=[pl.BlockSpec(memory_space=pltpu.VMEM)] * len(out_shape),
        scratch_shapes=scratch,
        compiler_params=pltpu.CompilerParams(collective_id=collective_id, has_side_effects=True),
    )(*operands)
    gathered = outs[0].reshape(size * x.shape[0], x.shape[1])
    return gathered if t is None else (gathered, outs[1])


def half_gather_kernel(chips, groups, t_ref, out_ref, x_ref, local_sem, cross_send, cross_recv,
                       up_send, up_recv, down_send, down_recv, t_local_sem, t_send, t_recv):
    row = lax.axis_index("ctx")
    me = lax.axis_index("chan")
    z = me // PER_Z
    y_lo = (me // 2) % 2
    core = me % 2
    across = me + 2 - 4 * y_lo
    ahead = ((z + 1) % chips) * PER_Z + y_lo * 2 + core
    behind = ((z + chips - 1) % chips) * PER_Z + y_lo * 2 + core
    mine = me // 2
    theirs = across // 2

    barrier = pltpu.get_barrier_semaphore()
    for peer in (across, ahead, behind):
        pl.semaphore_signal(barrier, inc=1, device_id=(row, peer), device_id_type=MESH)
    for peer in ctx_peers(groups):
        pl.semaphore_signal(barrier, inc=1, device_id=(peer, me), device_id_type=MESH)
    pl.semaphore_wait(barrier, 3 + groups - 1)

    slab = t_ref.shape[1]

    def slot(g):
        return x_ref.at[pl.ds(pl.multiple_of(g * slab, slab), slab)]

    def give(k, peer, g):
        return pltpu.make_async_remote_copy(
            src_ref=t_ref.at[peer], dst_ref=slot(g), send_sem=t_send.at[k - 1],
            recv_sem=t_recv.at[k - 1], device_id=(peer, me), device_id_type=MESH)

    t_local = pltpu.make_async_copy(t_ref.at[row], slot(row), t_local_sem)
    t_local.start()
    for k in range(1, groups):
        give(k, (row + k) % groups, row).start()
    t_local.wait()
    for k in range(1, groups):
        give(k, (row + k) % groups, row).wait_send()
        source = (row - k + groups) % groups
        give(k, source, source).wait_recv()

    local = pltpu.make_async_copy(x_ref, out_ref.at[mine], local_sem)
    local.start()

    def cross(slot):
        return pltpu.make_async_remote_copy(
            src_ref=x_ref, dst_ref=out_ref.at[slot], send_sem=cross_send,
            recv_sem=cross_recv, device_id=(row, across), device_id_type=MESH)

    cross(mine).start()
    local.wait()
    cross(mine).wait_send()
    cross(theirs).wait_recv()

    def pair(chip):
        return out_ref.at[pl.ds(pl.multiple_of(chip * 2, 2), 2)]

    steps = chips // 2

    def piece(chip, s, half):
        if s < steps - 1:
            return pair(chip)
        return out_ref.at[pl.ds(chip * 2 + half, 1)]

    def up(s, chip):
        return pltpu.make_async_remote_copy(
            src_ref=piece(chip, s, 0), dst_ref=piece(chip, s, 0), send_sem=up_send.at[s],
            recv_sem=up_recv.at[s], device_id=(row, ahead), device_id_type=MESH)

    def down(s, chip):
        return pltpu.make_async_remote_copy(
            src_ref=piece(chip, s, 1), dst_ref=piece(chip, s, 1), send_sem=down_send.at[s],
            recv_sem=down_recv.at[s], device_id=(row, behind), device_id_type=MESH)

    for s in range(steps):
        if s > 0:
            up(s - 1, (z - s + chips) % chips).wait_recv()
        up(s, (z - s + chips) % chips).start()
        if s > 0:
            down(s - 1, (z + s) % chips).wait_recv()
        down(s, (z + s) % chips).start()
    up(steps - 1, (z - steps + chips) % chips).wait_recv()
    down(steps - 1, (z + steps) % chips).wait_recv()
    for s in range(steps):
        up(s, (z - s + chips) % chips).wait_send()
        down(s, (z + s) % chips).wait_send()


def half_gather(t, collective_id):
    size = lax.axis_size("chan")
    groups = lax.axis_size("ctx")
    chips = size // PER_Z
    assert chips % 2 == 0
    ups = downs = chips // 2
    block = (t.shape[0] * t.shape[1], t.shape[2])
    out = pl.pallas_call(
        functools.partial(half_gather_kernel, chips, groups),
        out_shape=jax.ShapeDtypeStruct((size // 2,) + block, t.dtype),
        in_specs=[pl.BlockSpec(memory_space=pltpu.VMEM)],
        out_specs=pl.BlockSpec(memory_space=pltpu.VMEM),
        scratch_shapes=[
            pltpu.VMEM(block, t.dtype),
            pltpu.SemaphoreType.DMA(()),
            pltpu.SemaphoreType.DMA(()),
            pltpu.SemaphoreType.DMA(()),
            pltpu.SemaphoreType.DMA((ups,)),
            pltpu.SemaphoreType.DMA((ups,)),
            pltpu.SemaphoreType.DMA((downs,)),
            pltpu.SemaphoreType.DMA((downs,)),
            pltpu.SemaphoreType.DMA(()),
            pltpu.SemaphoreType.DMA((groups - 1,)),
            pltpu.SemaphoreType.DMA((groups - 1,)),
        ],
        compiler_params=pltpu.CompilerParams(collective_id=collective_id, has_side_effects=True),
    )(t)
    return out.reshape(size // 2 * block[0], block[1])


def dft_table(double_len):
    step = 32
    hi_ids = jnp.arange(double_len // step, dtype=jnp.int32)[:, None]
    lo_ids = jnp.arange(step, dtype=jnp.int32)[:, None]
    cols = jnp.arange(double_len, dtype=jnp.int32)[None, :]
    scale = 2.0 * math.pi / double_len
    hi_angle = scale * (hi_ids * step * cols % double_len).astype(jnp.float32)
    lo_angle = scale * (lo_ids * cols % double_len).astype(jnp.float32)
    hc, hs = jnp.cos(hi_angle)[:, None], jnp.sin(hi_angle)[:, None]
    lc, ls = jnp.cos(lo_angle)[None], jnp.sin(lo_angle)[None]
    cos = (hc * lc - hs * ls).reshape(double_len, double_len)
    sin = (hs * lc + hc * ls).reshape(double_len, double_len)
    return jnp.concatenate([cos, -sin], 0).astype(jnp.bfloat16)


def body(inputs, w_in, conv_taps, skip_gain, filter_taps, w_out):
    span_len, width_dev = inputs.shape
    double_len = 2 * span_len
    groups = lax.axis_size("ctx")
    position = lax.axis_index("ctx")
    own = width_dev // groups

    with jax.named_scope("input_gather_and_filter_to_owner"):
        taps_t = filter_taps.T.reshape(groups, own, span_len)
        inputs_t, taps_t = chan_gather(inputs.T, taps_t, 0)

    with jax.named_scope("out_weight_columns"):
        w_late, inputs_t = lax.optimization_barrier((w_out, inputs_t))
        size = lax.axis_size("chan")
        same_core = [list(range(c, size, 2)) for c in range(2)]
        w_cols = lax.all_to_all(w_late, "chan", 1, 0, tiled=True, axis_index_groups=same_core)

    with jax.named_scope("input_projection"):
        w_flat = w_in.reshape(w_in.shape[0], 3 * width_dev)
        proj_t = lax.dot_general(
            w_flat, inputs_t, (((0,), (0,)), ((), ())), preferred_element_type=jnp.float32
        ).astype(jnp.bfloat16)

    with jax.named_scope("projection_to_owner"):
        proj_t = proj_t.reshape(3, groups, own, span_len).transpose(1, 0, 2, 3)
        proj_t = ctx_exchange(proj_t, 3)

    with jax.named_scope("short_conv"):
        start = position * own
        taps = lax.dynamic_slice_in_dim(conv_taps, start, own, axis=2)
        rim = jnp.pad(proj_t[:-1, :, :, span_len - (KERNEL - 1) :], ((1, 0), (0, 0), (0, 0), (0, 0)))
        padded = jnp.concatenate([rim, proj_t], 3)
        filtered = jnp.zeros(proj_t.shape, jnp.float32)
        for lag in range(KERNEL):
            start_row = KERNEL - 1 - lag
            filtered = filtered + taps[lag].astype(jnp.float32)[None, :, :, None] * padded[
                ..., start_row : start_row + span_len
            ].astype(jnp.float32)
        streams = filtered.astype(jnp.bfloat16)
        gate_out = streams[:, 0]
        gated_in = (streams[:, 1].astype(jnp.float32) * streams[:, 2].astype(jnp.float32)).astype(
            jnp.bfloat16
        )

    with jax.named_scope("spectra"):
        table = dft_table(double_len)
        forward_in = table[:, :span_len]
        spectra_in = jnp.einsum(
            "jdb,fb->jdf", gated_in, forward_in, preferred_element_type=jnp.float32
        ).astype(jnp.bfloat16)
        previous = jnp.pad(taps_t[:-1, :, 1:], ((1, 0), (0, 0), (0, 0)))
        padded_taps = jnp.concatenate(
            [taps_t, jnp.zeros((groups, own, 1), jnp.bfloat16), previous], 2
        )
        spectra_taps = jnp.einsum(
            "kdm,fm->kdf", padded_taps, table, preferred_element_type=jnp.float32
        ).astype(jnp.bfloat16)

    with jax.named_scope("mixture"):
        real_g = spectra_taps[:, :, :double_len].astype(jnp.float32)
        imag_g = spectra_taps[:, :, double_len:].astype(jnp.float32)
        real_u = spectra_in[:, :, :double_len].astype(jnp.float32)
        imag_u = spectra_in[:, :, double_len:].astype(jnp.float32)
        acc_r = jnp.zeros(real_u.shape, jnp.float32)
        acc_i = jnp.zeros(real_u.shape, jnp.float32)
        for lag in range(groups):
            keep = groups - lag
            shift = ((lag, 0), (0, 0), (0, 0))
            acc_r = acc_r + jnp.pad(
                real_g[lag] * real_u[:keep] - imag_g[lag] * imag_u[:keep], shift)
            acc_i = acc_i + jnp.pad(
                real_g[lag] * imag_u[:keep] + imag_g[lag] * real_u[:keep], shift)
        mixture = jnp.concatenate([acc_r, acc_i], 2).astype(jnp.bfloat16)

    with jax.named_scope("inverse_and_gate"):
        long_out = jnp.einsum(
            "idf,fa->ida", mixture, forward_in, preferred_element_type=jnp.float32
        ) * (1.0 / double_len)
        gain = lax.dynamic_slice_in_dim(skip_gain, start, own)
        long_out = long_out + gain[None, :, None] * gated_in.astype(jnp.float32)
        gated_out = (gate_out.astype(jnp.float32) * long_out).astype(jnp.bfloat16)

    with jax.named_scope("output_projection"):
        gathered = half_gather(gated_out, 1)
        partial = lax.dot_general(
            gathered, w_cols, (((0,), (0,)), ((), ())), preferred_element_type=jnp.float32
        )
        core = lax.axis_index("chan") % 2
        mine = lax.dynamic_slice_in_dim(partial, core * width_dev, width_dev, axis=1)
        other = lax.dynamic_slice_in_dim(partial, (1 - core) * width_dev, width_dev, axis=1)
        pairs = [(h, h + 1 - 2 * (h % 2)) for h in range(lax.axis_size("chan"))]
        result = (mine + lax.ppermute(other, "chan", pairs)).astype(jnp.bfloat16)
    return result


def solution(mesh):
    return jax.shard_map(
        body,
        mesh=mesh,
        in_specs=(
            P("ctx", "chan"),
            P(None, None, "chan"),
            P(None, None, "chan"),
            P("chan"),
            P("ctx", "chan"),
            P("chan", None),
        ),
        out_specs=P("ctx", "chan"),
        check_vma=False,
    )
```

```python
import math

import functools

import jax
import jax.numpy as jnp
from jax import lax
from jax.experimental import pallas as pl
from jax.experimental.pallas import tpu as pltpu
from jax.sharding import PartitionSpec as P

KERNEL = 3
MESH = pl.DeviceIdType.MESH
PER_Z = 4


def gather_kernel(chips, groups, *refs):
    if groups:
        (x_ref, t_ref, out_ref, t_out_ref, local_sem, cross_send, cross_recv, ring_send, ring_recv,
         sib_send, sib_recv, t_local_sem, t_send, t_recv) = refs
    else:
        (x_ref, out_ref, local_sem, cross_send, cross_recv, ring_send, ring_recv,
         sib_send, sib_recv) = refs
    row = lax.axis_index("ctx")
    me = lax.axis_index("chan")
    z = me // PER_Z
    y_lo = (me // 2) % 2
    core = me % 2
    way = 1 - 2 * core
    after = ((z + way + chips) % chips) * PER_Z + y_lo * 2 + core
    before = ((z - way + chips) % chips) * PER_Z + y_lo * 2 + core
    sibling = me + 1 - 2 * core
    across = me + 2 - 4 * y_lo
    diagonal = across + 1 - 2 * core
    partners = (sibling, across, diagonal)

    barrier = pltpu.get_barrier_semaphore()
    for peer in partners + (after, before):
        pl.semaphore_signal(barrier, inc=1, device_id=(row, peer), device_id_type=MESH)
    for peer in ctx_peers(groups) if groups else ():
        pl.semaphore_signal(barrier, inc=1, device_id=(peer, me), device_id_type=MESH)
    pl.semaphore_wait(barrier, 5 + max(groups - 1, 0))

    if groups:
        t_local, t_sends, t_receipts = exchange_copies(
            groups, t_ref, t_out_ref, t_local_sem, t_send, t_recv)
        t_local.start()
        for copy in t_sends:
            copy.start()

    width = x_ref.shape[1]

    def cols(first, count):
        return out_ref.at[:, pl.ds(pl.multiple_of(first * width, width), count * width)]

    local = pltpu.make_async_copy(x_ref, cols(me, 1), local_sem)
    local.start()

    def cross(k, peer, slot):
        return pltpu.make_async_remote_copy(
            src_ref=x_ref, dst_ref=cols(slot, 1), send_sem=cross_send.at[k],
            recv_sem=cross_recv.at[k], device_id=(row, peer), device_id_type=MESH)

    for k, peer in enumerate(partners):
        cross(k, peer, me).start()
    local.wait()
    for k, peer in enumerate(partners):
        cross(k, peer, me).wait_send()
        cross(k, peer, peer).wait_recv()

    last = chips // 2 - 1

    def part(chip, s, half):
        if s < last:
            return cols(chip * PER_Z, PER_Z)
        return cols(chip * PER_Z + half * (PER_Z // 2), PER_Z // 2)

    def ring(s, chip):
        return pltpu.make_async_remote_copy(
            src_ref=part(chip, s, core), dst_ref=part(chip, s, core), send_sem=ring_send.at[s],
            recv_sem=ring_recv.at[s], device_id=(row, after), device_id_type=MESH)

    def sib(s, chip, half):
        return pltpu.make_async_remote_copy(
            src_ref=part(chip, s, half), dst_ref=part(chip, s, half), send_sem=sib_send.at[s],
            recv_sem=sib_recv.at[s], device_id=(row, sibling), device_id_type=MESH)

    for s in range(last + 1):
        sent = (z - way * s + chips) % chips
        got = (z - way * (s + 1) + chips) % chips
        ring(s, sent).start()
        ring(s, got).wait_recv()
        sib(s, got, core).start()

    for s in range(last + 1):
        sent = (z - way * s + chips) % chips
        got = (z - way * (s + 1) + chips) % chips
        theirs = (z + way * (s + 1) + chips) % chips
        ring(s, sent).wait_send()
        sib(s, got, core).wait_send()
        sib(s, theirs, 1 - core).wait_recv()

    if groups:
        t_local.wait()
        for copy, receipt in zip(t_sends, t_receipts):
            copy.wait_send()
            receipt.wait_recv()


def exchange_copies(groups, x_ref, out_ref, local_sem, send_sem, recv_sem):
    me = lax.axis_index("ctx")
    col = lax.axis_index("chan")
    local = pltpu.make_async_copy(x_ref.at[me], out_ref.at[me], local_sem)

    def send(k, peer, slot):
        return pltpu.make_async_remote_copy(
            src_ref=x_ref.at[peer], dst_ref=out_ref.at[slot], send_sem=send_sem.at[k - 1],
            recv_sem=recv_sem.at[k - 1], device_id=(peer, col), device_id_type=MESH)

    sends = [send(k, (me + k) % groups, me) for k in range(1, groups)]
    sources = [(me - k + groups) % groups for k in range(1, groups)]
    receipts = [send(k, source, source) for k, source in zip(range(1, groups), sources)]
    return local, sends, receipts


def ctx_peers(groups):
    me = lax.axis_index("ctx")
    return [(me + k) % groups for k in range(1, groups)]


def exchange_kernel(groups, x_ref, out_ref, local_sem, send_sem, recv_sem):
    col = lax.axis_index("chan")
    barrier = pltpu.get_barrier_semaphore()
    for peer in ctx_peers(groups):
        pl.semaphore_signal(barrier, inc=1, device_id=(peer, col), device_id_type=MESH)
    pl.semaphore_wait(barrier, groups - 1)
    local, sends, receipts = exchange_copies(groups, x_ref, out_ref, local_sem, send_sem, recv_sem)
    local.start()
    for copy in sends:
        copy.start()
    local.wait()
    for copy, receipt in zip(sends, receipts):
        copy.wait_send()
        receipt.wait_recv()


def ctx_exchange(x, collective_id):
    groups = lax.axis_size("ctx")
    return pl.pallas_call(
        functools.partial(exchange_kernel, groups),
        out_shape=jax.ShapeDtypeStruct(x.shape, x.dtype),
        in_specs=[pl.BlockSpec(memory_space=pltpu.VMEM)],
        out_specs=pl.BlockSpec(memory_space=pltpu.VMEM),
        scratch_shapes=[
            pltpu.SemaphoreType.DMA(()),
            pltpu.SemaphoreType.DMA((groups - 1,)),
            pltpu.SemaphoreType.DMA((groups - 1,)),
        ],
        compiler_params=pltpu.CompilerParams(collective_id=collective_id, has_side_effects=True),
    )(x)


def chan_gather(x, t, collective_id):
    size = lax.axis_size("chan")
    groups = lax.axis_size("ctx") if t is not None else 0
    chips = size // PER_Z
    longest = chips // 2
    assert chips % 2 == 0
    operands = (x,) if t is None else (x, t)
    out_shape = [jax.ShapeDtypeStruct((x.shape[0], size * x.shape[1]), x.dtype)]
    scratch = [
        pltpu.SemaphoreType.DMA(()),
        pltpu.SemaphoreType.DMA((3,)),
        pltpu.SemaphoreType.DMA((3,)),
        pltpu.SemaphoreType.DMA((longest,)),
        pltpu.SemaphoreType.DMA((longest,)),
        pltpu.SemaphoreType.DMA((longest,)),
        pltpu.SemaphoreType.DMA((longest,)),
    ]
    if t is not None:
        out_shape.append(jax.ShapeDtypeStruct(t.shape, t.dtype))
        scratch += [
            pltpu.SemaphoreType.DMA(()),
            pltpu.SemaphoreType.DMA((groups - 1,)),
            pltpu.SemaphoreType.DMA((groups - 1,)),
        ]
    outs = pl.pallas_call(
        functools.partial(gather_kernel, chips, groups),
        out_shape=tuple(out_shape),
        in_specs=[pl.BlockSpec(memory_space=pltpu.VMEM)] * len(operands),
        out_specs=[pl.BlockSpec(memory_space=pltpu.VMEM)] * len(out_shape),
        scratch_shapes=scratch,
        compiler_params=pltpu.CompilerParams(collective_id=collective_id, has_side_effects=True),
    )(*operands)
    gathered = outs[0]
    return gathered if t is None else (gathered, outs[1])


def half_gather_kernel(chips, groups, t_ref, out_ref, x_ref, local_sem, cross_send, cross_recv,
                       up_send, up_recv, down_send, down_recv, t_local_sem, t_send, t_recv):
    row = lax.axis_index("ctx")
    me = lax.axis_index("chan")
    z = me // PER_Z
    y_lo = (me // 2) % 2
    core = me % 2
    across = me + 2 - 4 * y_lo
    ahead = ((z + 1) % chips) * PER_Z + y_lo * 2 + core
    behind = ((z + chips - 1) % chips) * PER_Z + y_lo * 2 + core
    mine = me // 2
    theirs = across // 2

    barrier = pltpu.get_barrier_semaphore()
    for peer in (across, ahead, behind):
        pl.semaphore_signal(barrier, inc=1, device_id=(row, peer), device_id_type=MESH)
    for peer in ctx_peers(groups):
        pl.semaphore_signal(barrier, inc=1, device_id=(peer, me), device_id_type=MESH)
    pl.semaphore_wait(barrier, 3 + groups - 1)

    slab = t_ref.shape[1]

    def slot(g):
        return x_ref.at[pl.ds(pl.multiple_of(g * slab, slab), slab)]

    def give(k, peer, g):
        return pltpu.make_async_remote_copy(
            src_ref=t_ref.at[peer], dst_ref=slot(g), send_sem=t_send.at[k - 1],
            recv_sem=t_recv.at[k - 1], device_id=(peer, me), device_id_type=MESH)

    t_local = pltpu.make_async_copy(t_ref.at[row], slot(row), t_local_sem)
    t_local.start()
    for k in range(1, groups):
        give(k, (row + k) % groups, row).start()
    t_local.wait()
    for k in range(1, groups):
        give(k, (row + k) % groups, row).wait_send()
        source = (row - k + groups) % groups
        give(k, source, source).wait_recv()

    local = pltpu.make_async_copy(x_ref, out_ref.at[mine], local_sem)
    local.start()

    def cross(slot):
        return pltpu.make_async_remote_copy(
            src_ref=x_ref, dst_ref=out_ref.at[slot], send_sem=cross_send,
            recv_sem=cross_recv, device_id=(row, across), device_id_type=MESH)

    cross(mine).start()
    local.wait()
    cross(mine).wait_send()
    cross(theirs).wait_recv()

    def pair(chip):
        return out_ref.at[pl.ds(pl.multiple_of(chip * 2, 2), 2)]

    steps = chips // 2

    def piece(chip, s, half):
        if s < steps - 1:
            return pair(chip)
        return out_ref.at[pl.ds(chip * 2 + half, 1)]

    def up(s, chip):
        return pltpu.make_async_remote_copy(
            src_ref=piece(chip, s, 0), dst_ref=piece(chip, s, 0), send_sem=up_send.at[s],
            recv_sem=up_recv.at[s], device_id=(row, ahead), device_id_type=MESH)

    def down(s, chip):
        return pltpu.make_async_remote_copy(
            src_ref=piece(chip, s, 1), dst_ref=piece(chip, s, 1), send_sem=down_send.at[s],
            recv_sem=down_recv.at[s], device_id=(row, behind), device_id_type=MESH)

    for s in range(steps):
        if s > 0:
            up(s - 1, (z - s + chips) % chips).wait_recv()
        up(s, (z - s + chips) % chips).start()
        if s > 0:
            down(s - 1, (z + s) % chips).wait_recv()
        down(s, (z + s) % chips).start()
    up(steps - 1, (z - steps + chips) % chips).wait_recv()
    down(steps - 1, (z + steps) % chips).wait_recv()
    for s in range(steps):
        up(s, (z - s + chips) % chips).wait_send()
        down(s, (z + s) % chips).wait_send()


def half_gather(t, collective_id):
    size = lax.axis_size("chan")
    groups = lax.axis_size("ctx")
    chips = size // PER_Z
    assert chips % 2 == 0
    ups = downs = chips // 2
    block = (t.shape[0] * t.shape[1], t.shape[2])
    out = pl.pallas_call(
        functools.partial(half_gather_kernel, chips, groups),
        out_shape=jax.ShapeDtypeStruct((size // 2,) + block, t.dtype),
        in_specs=[pl.BlockSpec(memory_space=pltpu.VMEM)],
        out_specs=pl.BlockSpec(memory_space=pltpu.VMEM),
        scratch_shapes=[
            pltpu.VMEM(block, t.dtype),
            pltpu.SemaphoreType.DMA(()),
            pltpu.SemaphoreType.DMA(()),
            pltpu.SemaphoreType.DMA(()),
            pltpu.SemaphoreType.DMA((ups,)),
            pltpu.SemaphoreType.DMA((ups,)),
            pltpu.SemaphoreType.DMA((downs,)),
            pltpu.SemaphoreType.DMA((downs,)),
            pltpu.SemaphoreType.DMA(()),
            pltpu.SemaphoreType.DMA((groups - 1,)),
            pltpu.SemaphoreType.DMA((groups - 1,)),
        ],
        compiler_params=pltpu.CompilerParams(collective_id=collective_id, has_side_effects=True),
    )(t)
    return out.reshape(size // 2 * block[0], block[1])


def matmul_kernel(depth, x_ref, w_ref, out_ref):
    for stream in range(w_ref.shape[0]):
        def step(k, acc):
            rows = pl.ds(pl.multiple_of(k * depth, depth), depth)
            return acc + jnp.dot(x_ref[:, rows], w_ref[stream, rows, :],
                                 preferred_element_type=jnp.float32)

        total = lax.fori_loop(0, x_ref.shape[1] // depth, step,
                              jnp.zeros(out_ref.shape[1:], jnp.float32))
        out_ref[stream] = total.astype(out_ref.dtype)


def project(x, w):
    depth = 512
    return pl.pallas_call(
        functools.partial(matmul_kernel, depth),
        out_shape=jax.ShapeDtypeStruct((w.shape[0], x.shape[0], w.shape[2]), jnp.bfloat16),
        in_specs=[pl.BlockSpec(memory_space=pltpu.VMEM)] * 2,
        out_specs=pl.BlockSpec(memory_space=pltpu.VMEM),
        cost_estimate=pl.CostEstimate(
            flops=2 * x.shape[0] * x.shape[1] * w.shape[0] * w.shape[2], transcendentals=0,
            bytes_accessed=2 * (x.size + w.size + x.shape[0] * w.shape[0] * w.shape[2])),
    )(x, w)


def dft_table(double_len):
    step = 32
    hi_ids = jnp.arange(double_len // step, dtype=jnp.int32)[:, None]
    lo_ids = jnp.arange(step, dtype=jnp.int32)[:, None]
    cols = jnp.arange(double_len, dtype=jnp.int32)[None, :]
    scale = 2.0 * math.pi / double_len
    hi_angle = scale * (hi_ids * step * cols % double_len).astype(jnp.float32)
    lo_angle = scale * (lo_ids * cols % double_len).astype(jnp.float32)
    hc, hs = jnp.cos(hi_angle)[:, None], jnp.sin(hi_angle)[:, None]
    lc, ls = jnp.cos(lo_angle)[None], jnp.sin(lo_angle)[None]
    cos = (hc * lc - hs * ls).reshape(double_len, double_len)
    sin = (hs * lc + hc * ls).reshape(double_len, double_len)
    return jnp.concatenate([cos, -sin], 0).astype(jnp.bfloat16)


def body(inputs, w_in, conv_taps, skip_gain, filter_taps, w_out):
    span_len, width_dev = inputs.shape
    double_len = 2 * span_len
    groups = lax.axis_size("ctx")
    position = lax.axis_index("ctx")
    own = width_dev // groups

    with jax.named_scope("input_gather_and_filter_to_owner"):
        taps_t = filter_taps.T.reshape(groups, own, span_len)
        inputs_all, taps_t = chan_gather(inputs, taps_t, 0)

    with jax.named_scope("input_projection"):
        projected = project(inputs_all, jnp.transpose(w_in, (1, 0, 2)))

    with jax.named_scope("projection_to_owner"):
        proj_t = projected.reshape(3, span_len, groups, own).transpose(2, 0, 3, 1)
        proj_t = ctx_exchange(proj_t, 3)

    with jax.named_scope("out_weight_columns"):
        w_late, proj_t = lax.optimization_barrier((w_out, proj_t))
        size = lax.axis_size("chan")
        same_core = [list(range(c, size, 2)) for c in range(2)]
        w_cols = lax.all_to_all(w_late, "chan", 1, 0, tiled=True, axis_index_groups=same_core)

    with jax.named_scope("short_conv"):
        start = position * own
        taps = lax.dynamic_slice_in_dim(conv_taps, start, own, axis=2)
        rim = jnp.pad(proj_t[:-1, :, :, span_len - (KERNEL - 1) :], ((1, 0), (0, 0), (0, 0), (0, 0)))
        padded = jnp.concatenate([rim, proj_t], 3)
        filtered = jnp.zeros(proj_t.shape, jnp.float32)
        for lag in range(KERNEL):
            start_row = KERNEL - 1 - lag
            filtered = filtered + taps[lag].astype(jnp.float32)[None, :, :, None] * padded[
                ..., start_row : start_row + span_len
            ].astype(jnp.float32)
        streams = filtered.astype(jnp.bfloat16)
        gate_out = streams[:, 0]
        gated_in = (streams[:, 1].astype(jnp.float32) * streams[:, 2].astype(jnp.float32)).astype(
            jnp.bfloat16
        )

    with jax.named_scope("spectra"):
        table = dft_table(double_len)
        forward_in = table[:, :span_len]
        spectra_in = jnp.einsum(
            "jdb,fb->jdf", gated_in, forward_in, preferred_element_type=jnp.float32
        ).astype(jnp.bfloat16)
        previous = jnp.pad(taps_t[:-1, :, 1:], ((1, 0), (0, 0), (0, 0)))
        padded_taps = jnp.concatenate(
            [taps_t, jnp.zeros((groups, own, 1), jnp.bfloat16), previous], 2
        )
        spectra_taps = jnp.einsum(
            "kdm,fm->kdf", padded_taps, table, preferred_element_type=jnp.float32
        ).astype(jnp.bfloat16)

    with jax.named_scope("mixture"):
        real_g = spectra_taps[:, :, :double_len].astype(jnp.float32)
        imag_g = spectra_taps[:, :, double_len:].astype(jnp.float32)
        real_u = spectra_in[:, :, :double_len].astype(jnp.float32)
        imag_u = spectra_in[:, :, double_len:].astype(jnp.float32)
        acc_r = jnp.zeros(real_u.shape, jnp.float32)
        acc_i = jnp.zeros(real_u.shape, jnp.float32)
        for lag in range(groups):
            keep = groups - lag
            shift = ((lag, 0), (0, 0), (0, 0))
            acc_r = acc_r + jnp.pad(
                real_g[lag] * real_u[:keep] - imag_g[lag] * imag_u[:keep], shift)
            acc_i = acc_i + jnp.pad(
                real_g[lag] * imag_u[:keep] + imag_g[lag] * real_u[:keep], shift)
        mixture = jnp.concatenate([acc_r, acc_i], 2).astype(jnp.bfloat16)

    with jax.named_scope("inverse_and_gate"):
        long_out = jnp.einsum(
            "idf,fa->ida", mixture, forward_in, preferred_element_type=jnp.float32
        ) * (1.0 / double_len)
        gain = lax.dynamic_slice_in_dim(skip_gain, start, own)
        long_out = long_out + gain[None, :, None] * gated_in.astype(jnp.float32)
        gated_out = (gate_out.astype(jnp.float32) * long_out).astype(jnp.bfloat16)

    with jax.named_scope("output_projection"):
        gathered = half_gather(gated_out, 1)
        partial = lax.dot_general(
            gathered, w_cols, (((0,), (0,)), ((), ())), preferred_element_type=jnp.float32
        )
        core = lax.axis_index("chan") % 2
        mine = lax.dynamic_slice_in_dim(partial, core * width_dev, width_dev, axis=1)
        other = lax.dynamic_slice_in_dim(partial, (1 - core) * width_dev, width_dev, axis=1)
        pairs = [(h, h + 1 - 2 * (h % 2)) for h in range(lax.axis_size("chan"))]
        result = (mine + lax.ppermute(other, "chan", pairs)).astype(jnp.bfloat16)
    return result


def solution(mesh):
    return jax.shard_map(
        body,
        mesh=mesh,
        in_specs=(
            P("ctx", "chan"),
            P(None, None, "chan"),
            P(None, None, "chan"),
            P("chan"),
            P("ctx", "chan"),
            P("chan", None),
        ),
        out_specs=P("ctx", "chan"),
        check_vma=False,
    )
```

```python
import math

import functools

import jax
import jax.numpy as jnp
from jax import lax
from jax.experimental import pallas as pl
from jax.experimental.pallas import tpu as pltpu
from jax.sharding import PartitionSpec as P

KERNEL = 3
MESH = pl.DeviceIdType.MESH
PER_Z = 4


def gather_kernel(chips, groups, *refs):
    if groups:
        (x_ref, t_ref, out_ref, t_out_ref, local_sem, cross_send, cross_recv, ring_send, ring_recv,
         sib_send, sib_recv, t_local_sem, t_send, t_recv) = refs
    else:
        (x_ref, out_ref, local_sem, cross_send, cross_recv, ring_send, ring_recv,
         sib_send, sib_recv) = refs
    row = lax.axis_index("ctx")
    me = lax.axis_index("chan")
    z = me // PER_Z
    y_lo = (me // 2) % 2
    core = me % 2
    way = 1 - 2 * core
    after = ((z + way + chips) % chips) * PER_Z + y_lo * 2 + core
    before = ((z - way + chips) % chips) * PER_Z + y_lo * 2 + core
    sibling = me + 1 - 2 * core
    across = me + 2 - 4 * y_lo
    diagonal = across + 1 - 2 * core
    partners = (sibling, across, diagonal)

    barrier = pltpu.get_barrier_semaphore()
    for peer in partners + (after, before):
        pl.semaphore_signal(barrier, inc=1, device_id=(row, peer), device_id_type=MESH)
    for peer in ctx_peers(groups) if groups else ():
        pl.semaphore_signal(barrier, inc=1, device_id=(peer, me), device_id_type=MESH)
    pl.semaphore_wait(barrier, 5 + max(groups - 1, 0))

    if groups:
        t_local, t_sends, t_receipts = exchange_copies(
            groups, t_ref, t_out_ref, t_local_sem, t_send, t_recv)
        t_local.start()
        for copy in t_sends:
            copy.start()

    width = x_ref.shape[1]

    def cols(first, count):
        return out_ref.at[:, pl.ds(pl.multiple_of(first * width, width), count * width)]

    local = pltpu.make_async_copy(x_ref, cols(me, 1), local_sem)
    local.start()

    def cross(k, peer, slot):
        return pltpu.make_async_remote_copy(
            src_ref=x_ref, dst_ref=cols(slot, 1), send_sem=cross_send.at[k],
            recv_sem=cross_recv.at[k], device_id=(row, peer), device_id_type=MESH)

    for k, peer in enumerate(partners):
        cross(k, peer, me).start()
    local.wait()
    for k, peer in enumerate(partners):
        cross(k, peer, me).wait_send()
        cross(k, peer, peer).wait_recv()

    last = chips // 2 - 1

    def part(chip, s, half):
        if s < last:
            return cols(chip * PER_Z, PER_Z)
        return cols(chip * PER_Z + half * (PER_Z // 2), PER_Z // 2)

    def ring(s, chip):
        return pltpu.make_async_remote_copy(
            src_ref=part(chip, s, core), dst_ref=part(chip, s, core), send_sem=ring_send.at[s],
            recv_sem=ring_recv.at[s], device_id=(row, after), device_id_type=MESH)

    def sib(s, chip, half):
        return pltpu.make_async_remote_copy(
            src_ref=part(chip, s, half), dst_ref=part(chip, s, half), send_sem=sib_send.at[s],
            recv_sem=sib_recv.at[s], device_id=(row, sibling), device_id_type=MESH)

    for s in range(last + 1):
        sent = (z - way * s + chips) % chips
        got = (z - way * (s + 1) + chips) % chips
        ring(s, sent).start()
        ring(s, got).wait_recv()
        sib(s, got, core).start()

    for s in range(last + 1):
        sent = (z - way * s + chips) % chips
        got = (z - way * (s + 1) + chips) % chips
        theirs = (z + way * (s + 1) + chips) % chips
        ring(s, sent).wait_send()
        sib(s, got, core).wait_send()
        sib(s, theirs, 1 - core).wait_recv()

    if groups:
        t_local.wait()
        for copy, receipt in zip(t_sends, t_receipts):
            copy.wait_send()
            receipt.wait_recv()


def exchange_copies(groups, x_ref, out_ref, local_sem, send_sem, recv_sem):
    me = lax.axis_index("ctx")
    col = lax.axis_index("chan")
    local = pltpu.make_async_copy(x_ref.at[me], out_ref.at[me], local_sem)

    def send(k, peer, slot):
        return pltpu.make_async_remote_copy(
            src_ref=x_ref.at[peer], dst_ref=out_ref.at[slot], send_sem=send_sem.at[k - 1],
            recv_sem=recv_sem.at[k - 1], device_id=(peer, col), device_id_type=MESH)

    sends = [send(k, (me + k) % groups, me) for k in range(1, groups)]
    sources = [(me - k + groups) % groups for k in range(1, groups)]
    receipts = [send(k, source, source) for k, source in zip(range(1, groups), sources)]
    return local, sends, receipts


def ctx_peers(groups):
    me = lax.axis_index("ctx")
    return [(me + k) % groups for k in range(1, groups)]


def exchange_kernel(groups, x_ref, out_ref, local_sem, send_sem, recv_sem):
    col = lax.axis_index("chan")
    barrier = pltpu.get_barrier_semaphore()
    for peer in ctx_peers(groups):
        pl.semaphore_signal(barrier, inc=1, device_id=(peer, col), device_id_type=MESH)
    pl.semaphore_wait(barrier, groups - 1)
    local, sends, receipts = exchange_copies(groups, x_ref, out_ref, local_sem, send_sem, recv_sem)
    local.start()
    for copy in sends:
        copy.start()
    local.wait()
    for copy, receipt in zip(sends, receipts):
        copy.wait_send()
        receipt.wait_recv()


def ctx_exchange(x, collective_id):
    groups = lax.axis_size("ctx")
    return pl.pallas_call(
        functools.partial(exchange_kernel, groups),
        out_shape=jax.ShapeDtypeStruct(x.shape, x.dtype),
        in_specs=[pl.BlockSpec(memory_space=pltpu.VMEM)],
        out_specs=pl.BlockSpec(memory_space=pltpu.VMEM),
        scratch_shapes=[
            pltpu.SemaphoreType.DMA(()),
            pltpu.SemaphoreType.DMA((groups - 1,)),
            pltpu.SemaphoreType.DMA((groups - 1,)),
        ],
        compiler_params=pltpu.CompilerParams(collective_id=collective_id, has_side_effects=True),
    )(x)


def chan_gather(x, t, collective_id):
    size = lax.axis_size("chan")
    groups = lax.axis_size("ctx") if t is not None else 0
    chips = size // PER_Z
    longest = chips // 2
    assert chips % 2 == 0
    operands = (x,) if t is None else (x, t)
    out_shape = [jax.ShapeDtypeStruct((x.shape[0], size * x.shape[1]), x.dtype)]
    scratch = [
        pltpu.SemaphoreType.DMA(()),
        pltpu.SemaphoreType.DMA((3,)),
        pltpu.SemaphoreType.DMA((3,)),
        pltpu.SemaphoreType.DMA((longest,)),
        pltpu.SemaphoreType.DMA((longest,)),
        pltpu.SemaphoreType.DMA((longest,)),
        pltpu.SemaphoreType.DMA((longest,)),
    ]
    if t is not None:
        out_shape.append(jax.ShapeDtypeStruct(t.shape, t.dtype))
        scratch += [
            pltpu.SemaphoreType.DMA(()),
            pltpu.SemaphoreType.DMA((groups - 1,)),
            pltpu.SemaphoreType.DMA((groups - 1,)),
        ]
    outs = pl.pallas_call(
        functools.partial(gather_kernel, chips, groups),
        out_shape=tuple(out_shape),
        in_specs=[pl.BlockSpec(memory_space=pltpu.VMEM)] * len(operands),
        out_specs=[pl.BlockSpec(memory_space=pltpu.VMEM)] * len(out_shape),
        scratch_shapes=scratch,
        compiler_params=pltpu.CompilerParams(collective_id=collective_id, has_side_effects=True),
    )(*operands)
    gathered = outs[0]
    return gathered if t is None else (gathered, outs[1])


def half_gather_kernel(chips, groups, t_ref, out_ref, x_ref, local_sem, cross_send, cross_recv,
                       up_send, up_recv, down_send, down_recv, t_local_sem, t_send, t_recv):
    row = lax.axis_index("ctx")
    me = lax.axis_index("chan")
    z = me // PER_Z
    y_lo = (me // 2) % 2
    core = me % 2
    across = me + 2 - 4 * y_lo
    ahead = ((z + 1) % chips) * PER_Z + y_lo * 2 + core
    behind = ((z + chips - 1) % chips) * PER_Z + y_lo * 2 + core
    mine = me // 2
    theirs = across // 2

    barrier = pltpu.get_barrier_semaphore()
    for peer in (across, ahead, behind):
        pl.semaphore_signal(barrier, inc=1, device_id=(row, peer), device_id_type=MESH)
    for peer in ctx_peers(groups):
        pl.semaphore_signal(barrier, inc=1, device_id=(peer, me), device_id_type=MESH)
    pl.semaphore_wait(barrier, 3 + groups - 1)

    slab = t_ref.shape[1]

    def slot(g):
        return x_ref.at[pl.ds(pl.multiple_of(g * slab, slab), slab)]

    def give(k, peer, g):
        return pltpu.make_async_remote_copy(
            src_ref=t_ref.at[peer], dst_ref=slot(g), send_sem=t_send.at[k - 1],
            recv_sem=t_recv.at[k - 1], device_id=(peer, me), device_id_type=MESH)

    t_local = pltpu.make_async_copy(t_ref.at[row], slot(row), t_local_sem)
    t_local.start()
    for k in range(1, groups):
        give(k, (row + k) % groups, row).start()
    t_local.wait()
    for k in range(1, groups):
        give(k, (row + k) % groups, row).wait_send()
        source = (row - k + groups) % groups
        give(k, source, source).wait_recv()

    local = pltpu.make_async_copy(x_ref, out_ref.at[mine], local_sem)
    local.start()

    def cross(slot):
        return pltpu.make_async_remote_copy(
            src_ref=x_ref, dst_ref=out_ref.at[slot], send_sem=cross_send,
            recv_sem=cross_recv, device_id=(row, across), device_id_type=MESH)

    cross(mine).start()
    local.wait()
    cross(mine).wait_send()
    cross(theirs).wait_recv()

    def pair(chip):
        return out_ref.at[pl.ds(pl.multiple_of(chip * 2, 2), 2)]

    steps = chips // 2

    def piece(chip, s, half):
        if s < steps - 1:
            return pair(chip)
        return out_ref.at[pl.ds(chip * 2 + half, 1)]

    def up(s, chip):
        return pltpu.make_async_remote_copy(
            src_ref=piece(chip, s, 0), dst_ref=piece(chip, s, 0), send_sem=up_send.at[s],
            recv_sem=up_recv.at[s], device_id=(row, ahead), device_id_type=MESH)

    def down(s, chip):
        return pltpu.make_async_remote_copy(
            src_ref=piece(chip, s, 1), dst_ref=piece(chip, s, 1), send_sem=down_send.at[s],
            recv_sem=down_recv.at[s], device_id=(row, behind), device_id_type=MESH)

    for s in range(steps):
        if s > 0:
            up(s - 1, (z - s + chips) % chips).wait_recv()
        up(s, (z - s + chips) % chips).start()
        if s > 0:
            down(s - 1, (z + s) % chips).wait_recv()
        down(s, (z + s) % chips).start()
    up(steps - 1, (z - steps + chips) % chips).wait_recv()
    down(steps - 1, (z + steps) % chips).wait_recv()
    for s in range(steps):
        up(s, (z - s + chips) % chips).wait_send()
        down(s, (z + s) % chips).wait_send()


def half_gather(t, collective_id):
    size = lax.axis_size("chan")
    groups = lax.axis_size("ctx")
    chips = size // PER_Z
    assert chips % 2 == 0
    ups = downs = chips // 2
    block = (t.shape[0] * t.shape[1], t.shape[2])
    out = pl.pallas_call(
        functools.partial(half_gather_kernel, chips, groups),
        out_shape=jax.ShapeDtypeStruct((size // 2,) + block, t.dtype),
        in_specs=[pl.BlockSpec(memory_space=pltpu.VMEM)],
        out_specs=pl.BlockSpec(memory_space=pltpu.VMEM),
        scratch_shapes=[
            pltpu.VMEM(block, t.dtype),
            pltpu.SemaphoreType.DMA(()),
            pltpu.SemaphoreType.DMA(()),
            pltpu.SemaphoreType.DMA(()),
            pltpu.SemaphoreType.DMA((ups,)),
            pltpu.SemaphoreType.DMA((ups,)),
            pltpu.SemaphoreType.DMA((downs,)),
            pltpu.SemaphoreType.DMA((downs,)),
            pltpu.SemaphoreType.DMA(()),
            pltpu.SemaphoreType.DMA((groups - 1,)),
            pltpu.SemaphoreType.DMA((groups - 1,)),
        ],
        compiler_params=pltpu.CompilerParams(collective_id=collective_id, has_side_effects=True),
    )(t)
    return out.reshape(size // 2 * block[0], block[1])


def matmul_kernel(depth, x_ref, w_ref, out_ref):
    for stream in range(w_ref.shape[0]):
        out_ref[stream] = jnp.dot(
            x_ref[...], w_ref[stream], preferred_element_type=jnp.float32
        ).astype(out_ref.dtype)


def project(x, w):
    depth = 512
    return pl.pallas_call(
        functools.partial(matmul_kernel, depth),
        out_shape=jax.ShapeDtypeStruct((w.shape[0], x.shape[0], w.shape[2]), jnp.bfloat16),
        in_specs=[pl.BlockSpec(memory_space=pltpu.VMEM)] * 2,
        out_specs=pl.BlockSpec(memory_space=pltpu.VMEM),
        cost_estimate=pl.CostEstimate(
            flops=2 * x.shape[0] * x.shape[1] * w.shape[0] * w.shape[2], transcendentals=0,
            bytes_accessed=2 * (x.size + w.size + x.shape[0] * w.shape[0] * w.shape[2])),
    )(x, w)


def dft_table(double_len):
    step = 32
    hi_ids = jnp.arange(double_len // step, dtype=jnp.int32)[:, None]
    lo_ids = jnp.arange(step, dtype=jnp.int32)[:, None]
    cols = jnp.arange(double_len, dtype=jnp.int32)[None, :]
    scale = 2.0 * math.pi / double_len
    hi_angle = scale * (hi_ids * step * cols % double_len).astype(jnp.float32)
    lo_angle = scale * (lo_ids * cols % double_len).astype(jnp.float32)
    hc, hs = jnp.cos(hi_angle)[:, None], jnp.sin(hi_angle)[:, None]
    lc, ls = jnp.cos(lo_angle)[None], jnp.sin(lo_angle)[None]
    cos = (hc * lc - hs * ls).reshape(double_len, double_len)
    sin = (hs * lc + hc * ls).reshape(double_len, double_len)
    return jnp.concatenate([cos, -sin], 0).astype(jnp.bfloat16)


def body(inputs, w_in, conv_taps, skip_gain, filter_taps, w_out):
    span_len, width_dev = inputs.shape
    double_len = 2 * span_len
    groups = lax.axis_size("ctx")
    position = lax.axis_index("ctx")
    own = width_dev // groups

    with jax.named_scope("input_gather_and_filter_to_owner"):
        taps_t = filter_taps.T.reshape(groups, own, span_len)
        inputs_all, taps_t = chan_gather(inputs, taps_t, 0)

    with jax.named_scope("input_projection"):
        projected = project(inputs_all, jnp.transpose(w_in, (1, 0, 2)))

    with jax.named_scope("projection_to_owner"):
        proj_t = projected.reshape(3, span_len, groups, own).transpose(2, 0, 3, 1)
        proj_t = ctx_exchange(proj_t, 3)

    with jax.named_scope("out_weight_columns"):
        w_late, proj_t = lax.optimization_barrier((w_out, proj_t))
        size = lax.axis_size("chan")
        same_core = [list(range(c, size, 2)) for c in range(2)]
        w_cols = lax.all_to_all(w_late, "chan", 1, 0, tiled=True, axis_index_groups=same_core)

    with jax.named_scope("short_conv"):
        start = position * own
        taps = lax.dynamic_slice_in_dim(conv_taps, start, own, axis=2)
        rim = jnp.pad(proj_t[:-1, :, :, span_len - (KERNEL - 1) :], ((1, 0), (0, 0), (0, 0), (0, 0)))
        padded = jnp.concatenate([rim, proj_t], 3)
        filtered = jnp.zeros(proj_t.shape, jnp.float32)
        for lag in range(KERNEL):
            start_row = KERNEL - 1 - lag
            filtered = filtered + taps[lag].astype(jnp.float32)[None, :, :, None] * padded[
                ..., start_row : start_row + span_len
            ].astype(jnp.float32)
        streams = filtered.astype(jnp.bfloat16)
        gate_out = streams[:, 0]
        gated_in = (streams[:, 1].astype(jnp.float32) * streams[:, 2].astype(jnp.float32)).astype(
            jnp.bfloat16
        )

    with jax.named_scope("spectra"):
        table = dft_table(double_len)
        forward_in = table[:, :span_len]
        spectra_in = jnp.einsum(
            "jdb,fb->jdf", gated_in, forward_in, preferred_element_type=jnp.float32
        ).astype(jnp.bfloat16)
        previous = jnp.pad(taps_t[:-1, :, 1:], ((1, 0), (0, 0), (0, 0)))
        padded_taps = jnp.concatenate(
            [taps_t, jnp.zeros((groups, own, 1), jnp.bfloat16), previous], 2
        )
        spectra_taps = jnp.einsum(
            "kdm,fm->kdf", padded_taps, table, preferred_element_type=jnp.float32
        ).astype(jnp.bfloat16)

    with jax.named_scope("mixture"):
        real_g = spectra_taps[:, :, :double_len].astype(jnp.float32)
        imag_g = spectra_taps[:, :, double_len:].astype(jnp.float32)
        real_u = spectra_in[:, :, :double_len].astype(jnp.float32)
        imag_u = spectra_in[:, :, double_len:].astype(jnp.float32)
        acc_r = jnp.zeros(real_u.shape, jnp.float32)
        acc_i = jnp.zeros(real_u.shape, jnp.float32)
        for lag in range(groups):
            keep = groups - lag
            shift = ((lag, 0), (0, 0), (0, 0))
            acc_r = acc_r + jnp.pad(
                real_g[lag] * real_u[:keep] - imag_g[lag] * imag_u[:keep], shift)
            acc_i = acc_i + jnp.pad(
                real_g[lag] * imag_u[:keep] + imag_g[lag] * real_u[:keep], shift)
        mixture = jnp.concatenate([acc_r, acc_i], 2).astype(jnp.bfloat16)

    with jax.named_scope("inverse_and_gate"):
        long_out = jnp.einsum(
            "idf,fa->ida", mixture, forward_in, preferred_element_type=jnp.float32
        ) * (1.0 / double_len)
        gain = lax.dynamic_slice_in_dim(skip_gain, start, own)
        long_out = long_out + gain[None, :, None] * gated_in.astype(jnp.float32)
        gated_out = (gate_out.astype(jnp.float32) * long_out).astype(jnp.bfloat16)

    with jax.named_scope("output_projection"):
        gathered = half_gather(gated_out, 1)
        partial = lax.dot_general(
            gathered, w_cols, (((0,), (0,)), ((), ())), preferred_element_type=jnp.float32
        )
        core = lax.axis_index("chan") % 2
        mine = lax.dynamic_slice_in_dim(partial, core * width_dev, width_dev, axis=1)
        other = lax.dynamic_slice_in_dim(partial, (1 - core) * width_dev, width_dev, axis=1)
        pairs = [(h, h + 1 - 2 * (h % 2)) for h in range(lax.axis_size("chan"))]
        result = (mine + lax.ppermute(other, "chan", pairs)).astype(jnp.bfloat16)
    return result


def solution(mesh):
    return jax.shard_map(
        body,
        mesh=mesh,
        in_specs=(
            P("ctx", "chan"),
            P(None, None, "chan"),
            P(None, None, "chan"),
            P("chan"),
            P("ctx", "chan"),
            P("chan", None),
        ),
        out_specs=P("ctx", "chan"),
        check_vma=False,
    )
```

```python
import math

import functools

import jax
import jax.numpy as jnp
from jax import lax
from jax.experimental import pallas as pl
from jax.experimental.pallas import tpu as pltpu
from jax.sharding import PartitionSpec as P

KERNEL = 3
MESH = pl.DeviceIdType.MESH
PER_Z = 4


def gather_kernel(chips, groups, *refs):
    if groups:
        (x_ref, t_ref, out_ref, t_out_ref, local_sem, cross_send, cross_recv, ring_send, ring_recv,
         sib_send, sib_recv, t_local_sem, t_send, t_recv) = refs
    else:
        (x_ref, out_ref, local_sem, cross_send, cross_recv, ring_send, ring_recv,
         sib_send, sib_recv) = refs
    row = lax.axis_index("ctx")
    me = lax.axis_index("chan")
    z = me // PER_Z
    y_lo = (me // 2) % 2
    core = me % 2
    way = 1 - 2 * core
    after = ((z + way + chips) % chips) * PER_Z + y_lo * 2 + core
    before = ((z - way + chips) % chips) * PER_Z + y_lo * 2 + core
    sibling = me + 1 - 2 * core
    across = me + 2 - 4 * y_lo
    diagonal = across + 1 - 2 * core
    partners = (sibling, across, diagonal)

    barrier = pltpu.get_barrier_semaphore()
    for peer in partners + (after, before):
        pl.semaphore_signal(barrier, inc=1, device_id=(row, peer), device_id_type=MESH)
    for peer in ctx_peers(groups) if groups else ():
        pl.semaphore_signal(barrier, inc=1, device_id=(peer, me), device_id_type=MESH)
    pl.semaphore_wait(barrier, 5 + max(groups - 1, 0))

    if groups:
        t_local, t_sends, t_receipts = exchange_copies(
            groups, t_ref, t_out_ref, t_local_sem, t_send, t_recv)
        t_local.start()
        for copy in t_sends:
            copy.start()

    width = x_ref.shape[1]

    def cols(first, count):
        return out_ref.at[:, pl.ds(pl.multiple_of(first * width, width), count * width)]

    local = pltpu.make_async_copy(x_ref, cols(me, 1), local_sem)
    local.start()

    def cross(k, peer, slot):
        return pltpu.make_async_remote_copy(
            src_ref=x_ref, dst_ref=cols(slot, 1), send_sem=cross_send.at[k],
            recv_sem=cross_recv.at[k], device_id=(row, peer), device_id_type=MESH)

    for k, peer in enumerate(partners):
        cross(k, peer, me).start()
    local.wait()
    for k, peer in enumerate(partners):
        cross(k, peer, me).wait_send()
        cross(k, peer, peer).wait_recv()

    last = chips // 2 - 1

    def part(chip, s, half):
        if s < last:
            return cols(chip * PER_Z, PER_Z)
        return cols(chip * PER_Z + half * (PER_Z // 2), PER_Z // 2)

    def ring(s, chip):
        return pltpu.make_async_remote_copy(
            src_ref=part(chip, s, core), dst_ref=part(chip, s, core), send_sem=ring_send.at[s],
            recv_sem=ring_recv.at[s], device_id=(row, after), device_id_type=MESH)

    def sib(s, chip, half):
        return pltpu.make_async_remote_copy(
            src_ref=part(chip, s, half), dst_ref=part(chip, s, half), send_sem=sib_send.at[s],
            recv_sem=sib_recv.at[s], device_id=(row, sibling), device_id_type=MESH)

    for s in range(last + 1):
        sent = (z - way * s + chips) % chips
        got = (z - way * (s + 1) + chips) % chips
        ring(s, sent).start()
        ring(s, got).wait_recv()
        sib(s, got, core).start()

    for s in range(last + 1):
        sent = (z - way * s + chips) % chips
        got = (z - way * (s + 1) + chips) % chips
        theirs = (z + way * (s + 1) + chips) % chips
        ring(s, sent).wait_send()
        sib(s, got, core).wait_send()
        sib(s, theirs, 1 - core).wait_recv()

    if groups:
        t_local.wait()
        for copy, receipt in zip(t_sends, t_receipts):
            copy.wait_send()
            receipt.wait_recv()


def exchange_copies(groups, x_ref, out_ref, local_sem, send_sem, recv_sem):
    me = lax.axis_index("ctx")
    col = lax.axis_index("chan")
    local = pltpu.make_async_copy(x_ref.at[me], out_ref.at[me], local_sem)

    def send(k, peer, slot):
        return pltpu.make_async_remote_copy(
            src_ref=x_ref.at[peer], dst_ref=out_ref.at[slot], send_sem=send_sem.at[k - 1],
            recv_sem=recv_sem.at[k - 1], device_id=(peer, col), device_id_type=MESH)

    sends = [send(k, (me + k) % groups, me) for k in range(1, groups)]
    sources = [(me - k + groups) % groups for k in range(1, groups)]
    receipts = [send(k, source, source) for k, source in zip(range(1, groups), sources)]
    return local, sends, receipts


def ctx_peers(groups):
    me = lax.axis_index("ctx")
    return [(me + k) % groups for k in range(1, groups)]


def exchange_kernel(groups, x_ref, out_ref, local_sem, send_sem, recv_sem):
    col = lax.axis_index("chan")
    barrier = pltpu.get_barrier_semaphore()
    for peer in ctx_peers(groups):
        pl.semaphore_signal(barrier, inc=1, device_id=(peer, col), device_id_type=MESH)
    pl.semaphore_wait(barrier, groups - 1)
    local, sends, receipts = exchange_copies(groups, x_ref, out_ref, local_sem, send_sem, recv_sem)
    local.start()
    for copy in sends:
        copy.start()
    local.wait()
    for copy, receipt in zip(sends, receipts):
        copy.wait_send()
        receipt.wait_recv()


def ctx_exchange(x, collective_id):
    groups = lax.axis_size("ctx")
    return pl.pallas_call(
        functools.partial(exchange_kernel, groups),
        out_shape=jax.ShapeDtypeStruct(x.shape, x.dtype),
        in_specs=[pl.BlockSpec(memory_space=pltpu.VMEM)],
        out_specs=pl.BlockSpec(memory_space=pltpu.VMEM),
        scratch_shapes=[
            pltpu.SemaphoreType.DMA(()),
            pltpu.SemaphoreType.DMA((groups - 1,)),
            pltpu.SemaphoreType.DMA((groups - 1,)),
        ],
        compiler_params=pltpu.CompilerParams(collective_id=collective_id, has_side_effects=True),
    )(x)


def chan_gather(x, t, collective_id):
    size = lax.axis_size("chan")
    groups = lax.axis_size("ctx") if t is not None else 0
    chips = size // PER_Z
    longest = chips // 2
    assert chips % 2 == 0
    operands = (x,) if t is None else (x, t)
    out_shape = [jax.ShapeDtypeStruct((x.shape[0], size * x.shape[1]), x.dtype)]
    scratch = [
        pltpu.SemaphoreType.DMA(()),
        pltpu.SemaphoreType.DMA((3,)),
        pltpu.SemaphoreType.DMA((3,)),
        pltpu.SemaphoreType.DMA((longest,)),
        pltpu.SemaphoreType.DMA((longest,)),
        pltpu.SemaphoreType.DMA((longest,)),
        pltpu.SemaphoreType.DMA((longest,)),
    ]
    if t is not None:
        out_shape.append(jax.ShapeDtypeStruct(t.shape, t.dtype))
        scratch += [
            pltpu.SemaphoreType.DMA(()),
            pltpu.SemaphoreType.DMA((groups - 1,)),
            pltpu.SemaphoreType.DMA((groups - 1,)),
        ]
    outs = pl.pallas_call(
        functools.partial(gather_kernel, chips, groups),
        out_shape=tuple(out_shape),
        in_specs=[pl.BlockSpec(memory_space=pltpu.VMEM)] * len(operands),
        out_specs=[pl.BlockSpec(memory_space=pltpu.VMEM)] * len(out_shape),
        scratch_shapes=scratch,
        compiler_params=pltpu.CompilerParams(collective_id=collective_id, has_side_effects=True),
    )(*operands)
    gathered = outs[0]
    return gathered if t is None else (gathered, outs[1])


def half_gather_kernel(chips, groups, t_ref, out_ref, x_ref, local_sem, cross_send, cross_recv,
                       up_send, up_recv, down_send, down_recv, t_local_sem, t_send, t_recv):
    row = lax.axis_index("ctx")
    me = lax.axis_index("chan")
    z = me // PER_Z
    y_lo = (me // 2) % 2
    core = me % 2
    across = me + 2 - 4 * y_lo
    ahead = ((z + 1) % chips) * PER_Z + y_lo * 2 + core
    behind = ((z + chips - 1) % chips) * PER_Z + y_lo * 2 + core
    mine = me // 2
    theirs = across // 2

    barrier = pltpu.get_barrier_semaphore()
    for peer in (across, ahead, behind):
        pl.semaphore_signal(barrier, inc=1, device_id=(row, peer), device_id_type=MESH)
    for peer in ctx_peers(groups):
        pl.semaphore_signal(barrier, inc=1, device_id=(peer, me), device_id_type=MESH)
    pl.semaphore_wait(barrier, 3 + groups - 1)

    slab = t_ref.shape[1]

    def slot(g):
        return x_ref.at[pl.ds(pl.multiple_of(g * slab, slab), slab)]

    def give(k, peer, g):
        return pltpu.make_async_remote_copy(
            src_ref=t_ref.at[peer], dst_ref=slot(g), send_sem=t_send.at[k - 1],
            recv_sem=t_recv.at[k - 1], device_id=(peer, me), device_id_type=MESH)

    t_local = pltpu.make_async_copy(t_ref.at[row], slot(row), t_local_sem)
    t_local.start()
    for k in range(1, groups):
        give(k, (row + k) % groups, row).start()
    t_local.wait()
    for k in range(1, groups):
        give(k, (row + k) % groups, row).wait_send()
        source = (row - k + groups) % groups
        give(k, source, source).wait_recv()

    local = pltpu.make_async_copy(x_ref, out_ref.at[mine], local_sem)
    local.start()

    def cross(slot):
        return pltpu.make_async_remote_copy(
            src_ref=x_ref, dst_ref=out_ref.at[slot], send_sem=cross_send,
            recv_sem=cross_recv, device_id=(row, across), device_id_type=MESH)

    cross(mine).start()
    local.wait()
    cross(mine).wait_send()
    cross(theirs).wait_recv()

    def pair(chip):
        return out_ref.at[pl.ds(pl.multiple_of(chip * 2, 2), 2)]

    steps = chips // 2

    def piece(chip, s, half):
        if s < steps - 1:
            return pair(chip)
        return out_ref.at[pl.ds(chip * 2 + half, 1)]

    def up(s, chip):
        return pltpu.make_async_remote_copy(
            src_ref=piece(chip, s, 0), dst_ref=piece(chip, s, 0), send_sem=up_send.at[s],
            recv_sem=up_recv.at[s], device_id=(row, ahead), device_id_type=MESH)

    def down(s, chip):
        return pltpu.make_async_remote_copy(
            src_ref=piece(chip, s, 1), dst_ref=piece(chip, s, 1), send_sem=down_send.at[s],
            recv_sem=down_recv.at[s], device_id=(row, behind), device_id_type=MESH)

    for s in range(steps):
        if s > 0:
            up(s - 1, (z - s + chips) % chips).wait_recv()
        up(s, (z - s + chips) % chips).start()
        if s > 0:
            down(s - 1, (z + s) % chips).wait_recv()
        down(s, (z + s) % chips).start()
    up(steps - 1, (z - steps + chips) % chips).wait_recv()
    down(steps - 1, (z + steps) % chips).wait_recv()
    for s in range(steps):
        up(s, (z - s + chips) % chips).wait_send()
        down(s, (z + s) % chips).wait_send()


def half_gather(t, collective_id):
    size = lax.axis_size("chan")
    groups = lax.axis_size("ctx")
    chips = size // PER_Z
    assert chips % 2 == 0
    ups = downs = chips // 2
    block = (t.shape[0] * t.shape[1], t.shape[2])
    out = pl.pallas_call(
        functools.partial(half_gather_kernel, chips, groups),
        out_shape=jax.ShapeDtypeStruct((size // 2,) + block, t.dtype),
        in_specs=[pl.BlockSpec(memory_space=pltpu.VMEM)],
        out_specs=pl.BlockSpec(memory_space=pltpu.VMEM),
        scratch_shapes=[
            pltpu.VMEM(block, t.dtype),
            pltpu.SemaphoreType.DMA(()),
            pltpu.SemaphoreType.DMA(()),
            pltpu.SemaphoreType.DMA(()),
            pltpu.SemaphoreType.DMA((ups,)),
            pltpu.SemaphoreType.DMA((ups,)),
            pltpu.SemaphoreType.DMA((downs,)),
            pltpu.SemaphoreType.DMA((downs,)),
            pltpu.SemaphoreType.DMA(()),
            pltpu.SemaphoreType.DMA((groups - 1,)),
            pltpu.SemaphoreType.DMA((groups - 1,)),
        ],
        compiler_params=pltpu.CompilerParams(collective_id=collective_id, has_side_effects=True),
    )(t)
    return out.reshape(size // 2 * block[0], block[1])


def matmul_kernel(depth, x_ref, w_ref, out_ref):
    streams, _, width = w_ref.shape
    joined = jnp.concatenate([w_ref[stream] for stream in range(streams)], axis=1)
    total = jnp.dot(x_ref[...], joined, preferred_element_type=jnp.float32)
    for stream in range(streams):
        out_ref[stream] = total[:, stream * width : (stream + 1) * width].astype(out_ref.dtype)


def project(x, w):
    depth = 512
    return pl.pallas_call(
        functools.partial(matmul_kernel, depth),
        out_shape=jax.ShapeDtypeStruct((w.shape[0], x.shape[0], w.shape[2]), jnp.bfloat16),
        in_specs=[pl.BlockSpec(memory_space=pltpu.VMEM)] * 2,
        out_specs=pl.BlockSpec(memory_space=pltpu.VMEM),
        cost_estimate=pl.CostEstimate(
            flops=2 * x.shape[0] * x.shape[1] * w.shape[0] * w.shape[2], transcendentals=0,
            bytes_accessed=2 * (x.size + w.size + x.shape[0] * w.shape[0] * w.shape[2])),
    )(x, w)


def dft_table(double_len):
    step = 32
    hi_ids = jnp.arange(double_len // step, dtype=jnp.int32)[:, None]
    lo_ids = jnp.arange(step, dtype=jnp.int32)[:, None]
    cols = jnp.arange(double_len, dtype=jnp.int32)[None, :]
    scale = 2.0 * math.pi / double_len
    hi_angle = scale * (hi_ids * step * cols % double_len).astype(jnp.float32)
    lo_angle = scale * (lo_ids * cols % double_len).astype(jnp.float32)
    hc, hs = jnp.cos(hi_angle)[:, None], jnp.sin(hi_angle)[:, None]
    lc, ls = jnp.cos(lo_angle)[None], jnp.sin(lo_angle)[None]
    cos = (hc * lc - hs * ls).reshape(double_len, double_len)
    sin = (hs * lc + hc * ls).reshape(double_len, double_len)
    return jnp.concatenate([cos, -sin], 0).astype(jnp.bfloat16)


def body(inputs, w_in, conv_taps, skip_gain, filter_taps, w_out):
    span_len, width_dev = inputs.shape
    double_len = 2 * span_len
    groups = lax.axis_size("ctx")
    position = lax.axis_index("ctx")
    own = width_dev // groups

    with jax.named_scope("input_gather_and_filter_to_owner"):
        taps_t = filter_taps.T.reshape(groups, own, span_len)
        inputs_all, taps_t = chan_gather(inputs, taps_t, 0)

    with jax.named_scope("input_projection"):
        projected = project(inputs_all, jnp.transpose(w_in, (1, 0, 2)))

    with jax.named_scope("projection_to_owner"):
        proj_t = projected.reshape(3, span_len, groups, own).transpose(2, 0, 3, 1)
        proj_t = ctx_exchange(proj_t, 3)

    with jax.named_scope("out_weight_columns"):
        w_late, proj_t = lax.optimization_barrier((w_out, proj_t))
        size = lax.axis_size("chan")
        same_core = [list(range(c, size, 2)) for c in range(2)]
        w_cols = lax.all_to_all(w_late, "chan", 1, 0, tiled=True, axis_index_groups=same_core)

    with jax.named_scope("short_conv"):
        start = position * own
        taps = lax.dynamic_slice_in_dim(conv_taps, start, own, axis=2)
        rim = jnp.pad(proj_t[:-1, :, :, span_len - (KERNEL - 1) :], ((1, 0), (0, 0), (0, 0), (0, 0)))
        padded = jnp.concatenate([rim, proj_t], 3)
        filtered = jnp.zeros(proj_t.shape, jnp.float32)
        for lag in range(KERNEL):
            start_row = KERNEL - 1 - lag
            filtered = filtered + taps[lag].astype(jnp.float32)[None, :, :, None] * padded[
                ..., start_row : start_row + span_len
            ].astype(jnp.float32)
        streams = filtered.astype(jnp.bfloat16)
        gate_out = streams[:, 0]
        gated_in = (streams[:, 1].astype(jnp.float32) * streams[:, 2].astype(jnp.float32)).astype(
            jnp.bfloat16
        )

    with jax.named_scope("spectra"):
        table = dft_table(double_len)
        forward_in = table[:, :span_len]
        spectra_in = jnp.einsum(
            "jdb,fb->jdf", gated_in, forward_in, preferred_element_type=jnp.float32
        ).astype(jnp.bfloat16)
        previous = jnp.pad(taps_t[:-1, :, 1:], ((1, 0), (0, 0), (0, 0)))
        padded_taps = jnp.concatenate(
            [taps_t, jnp.zeros((groups, own, 1), jnp.bfloat16), previous], 2
        )
        spectra_taps = jnp.einsum(
            "kdm,fm->kdf", padded_taps, table, preferred_element_type=jnp.float32
        ).astype(jnp.bfloat16)

    with jax.named_scope("mixture"):
        real_g = spectra_taps[:, :, :double_len].astype(jnp.float32)
        imag_g = spectra_taps[:, :, double_len:].astype(jnp.float32)
        real_u = spectra_in[:, :, :double_len].astype(jnp.float32)
        imag_u = spectra_in[:, :, double_len:].astype(jnp.float32)
        acc_r = jnp.zeros(real_u.shape, jnp.float32)
        acc_i = jnp.zeros(real_u.shape, jnp.float32)
        for lag in range(groups):
            keep = groups - lag
            shift = ((lag, 0), (0, 0), (0, 0))
            acc_r = acc_r + jnp.pad(
                real_g[lag] * real_u[:keep] - imag_g[lag] * imag_u[:keep], shift)
            acc_i = acc_i + jnp.pad(
                real_g[lag] * imag_u[:keep] + imag_g[lag] * real_u[:keep], shift)
        mixture = jnp.concatenate([acc_r, acc_i], 2).astype(jnp.bfloat16)

    with jax.named_scope("inverse_and_gate"):
        long_out = jnp.einsum(
            "idf,fa->ida", mixture, forward_in, preferred_element_type=jnp.float32
        ) * (1.0 / double_len)
        gain = lax.dynamic_slice_in_dim(skip_gain, start, own)
        long_out = long_out + gain[None, :, None] * gated_in.astype(jnp.float32)
        gated_out = (gate_out.astype(jnp.float32) * long_out).astype(jnp.bfloat16)

    with jax.named_scope("output_projection"):
        gathered = half_gather(gated_out, 1)
        partial = lax.dot_general(
            gathered, w_cols, (((0,), (0,)), ((), ())), preferred_element_type=jnp.float32
        )
        core = lax.axis_index("chan") % 2
        mine = lax.dynamic_slice_in_dim(partial, core * width_dev, width_dev, axis=1)
        other = lax.dynamic_slice_in_dim(partial, (1 - core) * width_dev, width_dev, axis=1)
        pairs = [(h, h + 1 - 2 * (h % 2)) for h in range(lax.axis_size("chan"))]
        result = (mine + lax.ppermute(other, "chan", pairs)).astype(jnp.bfloat16)
    return result


def solution(mesh):
    return jax.shard_map(
        body,
        mesh=mesh,
        in_specs=(
            P("ctx", "chan"),
            P(None, None, "chan"),
            P(None, None, "chan"),
            P("chan"),
            P("ctx", "chan"),
            P("chan", None),
        ),
        out_specs=P("ctx", "chan"),
        check_vma=False,
    )
```

```python
import math

import functools

import jax
import jax.numpy as jnp
from jax import lax
from jax.experimental import pallas as pl
from jax.experimental.pallas import tpu as pltpu
from jax.sharding import PartitionSpec as P

KERNEL = 3
MESH = pl.DeviceIdType.MESH
PER_Z = 4


def gather_kernel(chips, groups, *refs):
    if groups:
        (x_ref, t_ref, out_ref, t_out_ref, local_sem, cross_send, cross_recv, ring_send, ring_recv,
         sib_send, sib_recv, t_local_sem, t_send, t_recv) = refs
    else:
        (x_ref, out_ref, local_sem, cross_send, cross_recv, ring_send, ring_recv,
         sib_send, sib_recv) = refs
    row = lax.axis_index("ctx")
    me = lax.axis_index("chan")
    z = me // PER_Z
    y_lo = (me // 2) % 2
    core = me % 2
    way = 1 - 2 * core
    after = ((z + way + chips) % chips) * PER_Z + y_lo * 2 + core
    before = ((z - way + chips) % chips) * PER_Z + y_lo * 2 + core
    sibling = me + 1 - 2 * core
    across = me + 2 - 4 * y_lo
    diagonal = across + 1 - 2 * core
    partners = (sibling, across, diagonal)

    barrier = pltpu.get_barrier_semaphore()
    for peer in partners + (after, before):
        pl.semaphore_signal(barrier, inc=1, device_id=(row, peer), device_id_type=MESH)
    for peer in ctx_peers(groups) if groups else ():
        pl.semaphore_signal(barrier, inc=1, device_id=(peer, me), device_id_type=MESH)
    pl.semaphore_wait(barrier, 5 + max(groups - 1, 0))

    if groups:
        t_local, t_sends, t_receipts = exchange_copies(
            groups, t_ref, t_out_ref, t_local_sem, t_send, t_recv)
        t_local.start()
        for copy in t_sends:
            copy.start()

    width = x_ref.shape[1]

    def cols(first, count):
        return out_ref.at[:, pl.ds(pl.multiple_of(first * width, width), count * width)]

    local = pltpu.make_async_copy(x_ref, cols(me, 1), local_sem)
    local.start()

    def cross(k, peer, slot):
        return pltpu.make_async_remote_copy(
            src_ref=x_ref, dst_ref=cols(slot, 1), send_sem=cross_send.at[k],
            recv_sem=cross_recv.at[k], device_id=(row, peer), device_id_type=MESH)

    for k, peer in enumerate(partners):
        cross(k, peer, me).start()
    local.wait()
    for k, peer in enumerate(partners):
        cross(k, peer, me).wait_send()
        cross(k, peer, peer).wait_recv()

    last = chips // 2 - 1

    def part(chip, s, half):
        if s < last:
            return cols(chip * PER_Z, PER_Z)
        return cols(chip * PER_Z + half * (PER_Z // 2), PER_Z // 2)

    def ring(s, chip):
        return pltpu.make_async_remote_copy(
            src_ref=part(chip, s, core), dst_ref=part(chip, s, core), send_sem=ring_send.at[s],
            recv_sem=ring_recv.at[s], device_id=(row, after), device_id_type=MESH)

    def sib(s, chip, half):
        return pltpu.make_async_remote_copy(
            src_ref=part(chip, s, half), dst_ref=part(chip, s, half), send_sem=sib_send.at[s],
            recv_sem=sib_recv.at[s], device_id=(row, sibling), device_id_type=MESH)

    for s in range(last + 1):
        sent = (z - way * s + chips) % chips
        got = (z - way * (s + 1) + chips) % chips
        ring(s, sent).start()
        ring(s, got).wait_recv()
        sib(s, got, core).start()

    for s in range(last + 1):
        sent = (z - way * s + chips) % chips
        got = (z - way * (s + 1) + chips) % chips
        theirs = (z + way * (s + 1) + chips) % chips
        ring(s, sent).wait_send()
        sib(s, got, core).wait_send()
        sib(s, theirs, 1 - core).wait_recv()

    if groups:
        t_local.wait()
        for copy, receipt in zip(t_sends, t_receipts):
            copy.wait_send()
            receipt.wait_recv()


def exchange_copies(groups, x_ref, out_ref, local_sem, send_sem, recv_sem):
    me = lax.axis_index("ctx")
    col = lax.axis_index("chan")
    local = pltpu.make_async_copy(x_ref.at[me], out_ref.at[me], local_sem)

    def send(k, peer, slot):
        return pltpu.make_async_remote_copy(
            src_ref=x_ref.at[peer], dst_ref=out_ref.at[slot], send_sem=send_sem.at[k - 1],
            recv_sem=recv_sem.at[k - 1], device_id=(peer, col), device_id_type=MESH)

    sends = [send(k, (me + k) % groups, me) for k in range(1, groups)]
    sources = [(me - k + groups) % groups for k in range(1, groups)]
    receipts = [send(k, source, source) for k, source in zip(range(1, groups), sources)]
    return local, sends, receipts


def ctx_peers(groups):
    me = lax.axis_index("ctx")
    return [(me + k) % groups for k in range(1, groups)]


def exchange_kernel(groups, x_ref, out_ref, local_sem, send_sem, recv_sem):
    col = lax.axis_index("chan")
    barrier = pltpu.get_barrier_semaphore()
    for peer in ctx_peers(groups):
        pl.semaphore_signal(barrier, inc=1, device_id=(peer, col), device_id_type=MESH)
    pl.semaphore_wait(barrier, groups - 1)
    local, sends, receipts = exchange_copies(groups, x_ref, out_ref, local_sem, send_sem, recv_sem)
    local.start()
    for copy in sends:
        copy.start()
    local.wait()
    for copy, receipt in zip(sends, receipts):
        copy.wait_send()
        receipt.wait_recv()


def ctx_exchange(x, collective_id):
    groups = lax.axis_size("ctx")
    return pl.pallas_call(
        functools.partial(exchange_kernel, groups),
        out_shape=jax.ShapeDtypeStruct(x.shape, x.dtype),
        in_specs=[pl.BlockSpec(memory_space=pltpu.VMEM)],
        out_specs=pl.BlockSpec(memory_space=pltpu.VMEM),
        scratch_shapes=[
            pltpu.SemaphoreType.DMA(()),
            pltpu.SemaphoreType.DMA((groups - 1,)),
            pltpu.SemaphoreType.DMA((groups - 1,)),
        ],
        compiler_params=pltpu.CompilerParams(collective_id=collective_id, has_side_effects=True),
    )(x)


def chan_gather(x, t, collective_id):
    size = lax.axis_size("chan")
    groups = lax.axis_size("ctx") if t is not None else 0
    chips = size // PER_Z
    longest = chips // 2
    assert chips % 2 == 0
    operands = (x,) if t is None else (x, t)
    out_shape = [jax.ShapeDtypeStruct((x.shape[0], size * x.shape[1]), x.dtype)]
    scratch = [
        pltpu.SemaphoreType.DMA(()),
        pltpu.SemaphoreType.DMA((3,)),
        pltpu.SemaphoreType.DMA((3,)),
        pltpu.SemaphoreType.DMA((longest,)),
        pltpu.SemaphoreType.DMA((longest,)),
        pltpu.SemaphoreType.DMA((longest,)),
        pltpu.SemaphoreType.DMA((longest,)),
    ]
    if t is not None:
        out_shape.append(jax.ShapeDtypeStruct(t.shape, t.dtype))
        scratch += [
            pltpu.SemaphoreType.DMA(()),
            pltpu.SemaphoreType.DMA((groups - 1,)),
            pltpu.SemaphoreType.DMA((groups - 1,)),
        ]
    outs = pl.pallas_call(
        functools.partial(gather_kernel, chips, groups),
        out_shape=tuple(out_shape),
        in_specs=[pl.BlockSpec(memory_space=pltpu.VMEM)] * len(operands),
        out_specs=[pl.BlockSpec(memory_space=pltpu.VMEM)] * len(out_shape),
        scratch_shapes=scratch,
        compiler_params=pltpu.CompilerParams(collective_id=collective_id, has_side_effects=True),
    )(*operands)
    gathered = outs[0]
    return gathered if t is None else (gathered, outs[1])


def half_gather_kernel(chips, groups, t_ref, out_ref, x_ref, local_sem, cross_send, cross_recv,
                       up_send, up_recv, down_send, down_recv, t_local_sem, t_send, t_recv):
    row = lax.axis_index("ctx")
    me = lax.axis_index("chan")
    z = me // PER_Z
    y_lo = (me // 2) % 2
    core = me % 2
    across = me + 2 - 4 * y_lo
    ahead = ((z + 1) % chips) * PER_Z + y_lo * 2 + core
    behind = ((z + chips - 1) % chips) * PER_Z + y_lo * 2 + core
    mine = me // 2
    theirs = across // 2

    barrier = pltpu.get_barrier_semaphore()
    for peer in (across, ahead, behind):
        pl.semaphore_signal(barrier, inc=1, device_id=(row, peer), device_id_type=MESH)
    for peer in ctx_peers(groups):
        pl.semaphore_signal(barrier, inc=1, device_id=(peer, me), device_id_type=MESH)
    pl.semaphore_wait(barrier, 3 + groups - 1)

    slab = t_ref.shape[1]

    def slot(g):
        return x_ref.at[pl.ds(pl.multiple_of(g * slab, slab), slab)]

    def give(k, peer, g):
        return pltpu.make_async_remote_copy(
            src_ref=t_ref.at[peer], dst_ref=slot(g), send_sem=t_send.at[k - 1],
            recv_sem=t_recv.at[k - 1], device_id=(peer, me), device_id_type=MESH)

    t_local = pltpu.make_async_copy(t_ref.at[row], slot(row), t_local_sem)
    t_local.start()
    for k in range(1, groups):
        give(k, (row + k) % groups, row).start()
    t_local.wait()
    for k in range(1, groups):
        give(k, (row + k) % groups, row).wait_send()
        source = (row - k + groups) % groups
        give(k, source, source).wait_recv()

    local = pltpu.make_async_copy(x_ref, out_ref.at[mine], local_sem)
    local.start()

    def cross(slot):
        return pltpu.make_async_remote_copy(
            src_ref=x_ref, dst_ref=out_ref.at[slot], send_sem=cross_send,
            recv_sem=cross_recv, device_id=(row, across), device_id_type=MESH)

    cross(mine).start()
    local.wait()
    cross(mine).wait_send()
    cross(theirs).wait_recv()

    def pair(chip):
        return out_ref.at[pl.ds(pl.multiple_of(chip * 2, 2), 2)]

    steps = chips // 2

    def piece(chip, s, half):
        if s < steps - 1:
            return pair(chip)
        return out_ref.at[pl.ds(chip * 2 + half, 1)]

    def up(s, chip):
        return pltpu.make_async_remote_copy(
            src_ref=piece(chip, s, 0), dst_ref=piece(chip, s, 0), send_sem=up_send.at[s],
            recv_sem=up_recv.at[s], device_id=(row, ahead), device_id_type=MESH)

    def down(s, chip):
        return pltpu.make_async_remote_copy(
            src_ref=piece(chip, s, 1), dst_ref=piece(chip, s, 1), send_sem=down_send.at[s],
            recv_sem=down_recv.at[s], device_id=(row, behind), device_id_type=MESH)

    for s in range(steps):
        if s > 0:
            up(s - 1, (z - s + chips) % chips).wait_recv()
        up(s, (z - s + chips) % chips).start()
        if s > 0:
            down(s - 1, (z + s) % chips).wait_recv()
        down(s, (z + s) % chips).start()
    up(steps - 1, (z - steps + chips) % chips).wait_recv()
    down(steps - 1, (z + steps) % chips).wait_recv()
    for s in range(steps):
        up(s, (z - s + chips) % chips).wait_send()
        down(s, (z + s) % chips).wait_send()


def half_gather(t, collective_id):
    size = lax.axis_size("chan")
    groups = lax.axis_size("ctx")
    chips = size // PER_Z
    assert chips % 2 == 0
    ups = downs = chips // 2
    block = (t.shape[0] * t.shape[1], t.shape[2])
    out = pl.pallas_call(
        functools.partial(half_gather_kernel, chips, groups),
        out_shape=jax.ShapeDtypeStruct((size // 2,) + block, t.dtype),
        in_specs=[pl.BlockSpec(memory_space=pltpu.VMEM)],
        out_specs=pl.BlockSpec(memory_space=pltpu.VMEM),
        scratch_shapes=[
            pltpu.VMEM(block, t.dtype),
            pltpu.SemaphoreType.DMA(()),
            pltpu.SemaphoreType.DMA(()),
            pltpu.SemaphoreType.DMA(()),
            pltpu.SemaphoreType.DMA((ups,)),
            pltpu.SemaphoreType.DMA((ups,)),
            pltpu.SemaphoreType.DMA((downs,)),
            pltpu.SemaphoreType.DMA((downs,)),
            pltpu.SemaphoreType.DMA(()),
            pltpu.SemaphoreType.DMA((groups - 1,)),
            pltpu.SemaphoreType.DMA((groups - 1,)),
        ],
        compiler_params=pltpu.CompilerParams(collective_id=collective_id, has_side_effects=True),
    )(t)
    return out.reshape(size // 2 * block[0], block[1])


def matmul_kernel(x_ref, w_ref, out_ref):
    groups, streams, own, _ = out_ref.shape
    width = w_ref.shape[2]
    joined = jnp.concatenate([w_ref[stream] for stream in range(streams)], axis=1)
    total = jnp.dot(x_ref[...], joined, preferred_element_type=jnp.float32).T
    for stream in range(streams):
        for g in range(groups):
            first = stream * width + g * own
            out_ref[g, stream] = total[first : first + own, :].astype(out_ref.dtype)


def project(x, w, groups):
    streams, _, width = w.shape
    return pl.pallas_call(
        matmul_kernel,
        out_shape=jax.ShapeDtypeStruct((groups, streams, width // groups, x.shape[0]),
                                       jnp.bfloat16),
        in_specs=[pl.BlockSpec(memory_space=pltpu.VMEM)] * 2,
        out_specs=pl.BlockSpec(memory_space=pltpu.VMEM),
        cost_estimate=pl.CostEstimate(
            flops=2 * x.shape[0] * x.shape[1] * streams * width, transcendentals=0,
            bytes_accessed=2 * (x.size + w.size + x.shape[0] * streams * width)),
    )(x, w)


def dft_table(double_len):
    step = 32
    hi_ids = jnp.arange(double_len // step, dtype=jnp.int32)[:, None]
    lo_ids = jnp.arange(step, dtype=jnp.int32)[:, None]
    cols = jnp.arange(double_len, dtype=jnp.int32)[None, :]
    scale = 2.0 * math.pi / double_len
    hi_angle = scale * (hi_ids * step * cols % double_len).astype(jnp.float32)
    lo_angle = scale * (lo_ids * cols % double_len).astype(jnp.float32)
    hc, hs = jnp.cos(hi_angle)[:, None], jnp.sin(hi_angle)[:, None]
    lc, ls = jnp.cos(lo_angle)[None], jnp.sin(lo_angle)[None]
    cos = (hc * lc - hs * ls).reshape(double_len, double_len)
    sin = (hs * lc + hc * ls).reshape(double_len, double_len)
    return jnp.concatenate([cos, -sin], 0).astype(jnp.bfloat16)


def body(inputs, w_in, conv_taps, skip_gain, filter_taps, w_out):
    span_len, width_dev = inputs.shape
    double_len = 2 * span_len
    groups = lax.axis_size("ctx")
    position = lax.axis_index("ctx")
    own = width_dev // groups

    with jax.named_scope("input_gather_and_filter_to_owner"):
        taps_t = filter_taps.T.reshape(groups, own, span_len)
        inputs_all, taps_t = chan_gather(inputs, taps_t, 0)

    with jax.named_scope("input_projection"):
        proj_t = project(inputs_all, jnp.transpose(w_in, (1, 0, 2)), groups)

    with jax.named_scope("projection_to_owner"):
        proj_t = ctx_exchange(proj_t, 3)

    with jax.named_scope("out_weight_columns"):
        w_late, proj_t = lax.optimization_barrier((w_out, proj_t))
        size = lax.axis_size("chan")
        same_core = [list(range(c, size, 2)) for c in range(2)]
        w_cols = lax.all_to_all(w_late, "chan", 1, 0, tiled=True, axis_index_groups=same_core)

    with jax.named_scope("short_conv"):
        start = position * own
        taps = lax.dynamic_slice_in_dim(conv_taps, start, own, axis=2)
        rim = jnp.pad(proj_t[:-1, :, :, span_len - (KERNEL - 1) :], ((1, 0), (0, 0), (0, 0), (0, 0)))
        padded = jnp.concatenate([rim, proj_t], 3)
        filtered = jnp.zeros(proj_t.shape, jnp.float32)
        for lag in range(KERNEL):
            start_row = KERNEL - 1 - lag
            filtered = filtered + taps[lag].astype(jnp.float32)[None, :, :, None] * padded[
                ..., start_row : start_row + span_len
            ].astype(jnp.float32)
        streams = filtered.astype(jnp.bfloat16)
        gate_out = streams[:, 0]
        gated_in = (streams[:, 1].astype(jnp.float32) * streams[:, 2].astype(jnp.float32)).astype(
            jnp.bfloat16
        )

    with jax.named_scope("spectra"):
        table = dft_table(double_len)
        forward_in = table[:, :span_len]
        spectra_in = jnp.einsum(
            "jdb,fb->jdf", gated_in, forward_in, preferred_element_type=jnp.float32
        ).astype(jnp.bfloat16)
        previous = jnp.pad(taps_t[:-1, :, 1:], ((1, 0), (0, 0), (0, 0)))
        padded_taps = jnp.concatenate(
            [taps_t, jnp.zeros((groups, own, 1), jnp.bfloat16), previous], 2
        )
        spectra_taps = jnp.einsum(
            "kdm,fm->kdf", padded_taps, table, preferred_element_type=jnp.float32
        ).astype(jnp.bfloat16)

    with jax.named_scope("mixture"):
        real_g = spectra_taps[:, :, :double_len].astype(jnp.float32)
        imag_g = spectra_taps[:, :, double_len:].astype(jnp.float32)
        real_u = spectra_in[:, :, :double_len].astype(jnp.float32)
        imag_u = spectra_in[:, :, double_len:].astype(jnp.float32)
        acc_r = jnp.zeros(real_u.shape, jnp.float32)
        acc_i = jnp.zeros(real_u.shape, jnp.float32)
        for lag in range(groups):
            keep = groups - lag
            shift = ((lag, 0), (0, 0), (0, 0))
            acc_r = acc_r + jnp.pad(
                real_g[lag] * real_u[:keep] - imag_g[lag] * imag_u[:keep], shift)
            acc_i = acc_i + jnp.pad(
                real_g[lag] * imag_u[:keep] + imag_g[lag] * real_u[:keep], shift)
        mixture = jnp.concatenate([acc_r, acc_i], 2).astype(jnp.bfloat16)

    with jax.named_scope("inverse_and_gate"):
        long_out = jnp.einsum(
            "idf,fa->ida", mixture, forward_in, preferred_element_type=jnp.float32
        ) * (1.0 / double_len)
        gain = lax.dynamic_slice_in_dim(skip_gain, start, own)
        long_out = long_out + gain[None, :, None] * gated_in.astype(jnp.float32)
        gated_out = (gate_out.astype(jnp.float32) * long_out).astype(jnp.bfloat16)

    with jax.named_scope("output_projection"):
        gathered = half_gather(gated_out, 1)
        partial = lax.dot_general(
            gathered, w_cols, (((0,), (0,)), ((), ())), preferred_element_type=jnp.float32
        )
        core = lax.axis_index("chan") % 2
        mine = lax.dynamic_slice_in_dim(partial, core * width_dev, width_dev, axis=1)
        other = lax.dynamic_slice_in_dim(partial, (1 - core) * width_dev, width_dev, axis=1)
        pairs = [(h, h + 1 - 2 * (h % 2)) for h in range(lax.axis_size("chan"))]
        result = (mine + lax.ppermute(other, "chan", pairs)).astype(jnp.bfloat16)
    return result


def solution(mesh):
    return jax.shard_map(
        body,
        mesh=mesh,
        in_specs=(
            P("ctx", "chan"),
            P(None, None, "chan"),
            P(None, None, "chan"),
            P("chan"),
            P("ctx", "chan"),
            P("chan", None),
        ),
        out_specs=P("ctx", "chan"),
        check_vma=False,
    )
```

```python
import math

import functools

import jax
import jax.numpy as jnp
from jax import lax
from jax.experimental import pallas as pl
from jax.experimental.pallas import tpu as pltpu
from jax.sharding import PartitionSpec as P

KERNEL = 3
MESH = pl.DeviceIdType.MESH
PER_Z = 4


def gather_kernel(chips, groups, *refs):
    if groups:
        (x_ref, t_ref, out_ref, t_out_ref, local_sem, cross_send, cross_recv, ring_send, ring_recv,
         sib_send, sib_recv, t_local_sem, t_send, t_recv) = refs
    else:
        (x_ref, out_ref, local_sem, cross_send, cross_recv, ring_send, ring_recv,
         sib_send, sib_recv) = refs
    row = lax.axis_index("ctx")
    me = lax.axis_index("chan")
    z = me // PER_Z
    y_lo = (me // 2) % 2
    core = me % 2
    way = 1 - 2 * core
    after = ((z + way + chips) % chips) * PER_Z + y_lo * 2 + core
    before = ((z - way + chips) % chips) * PER_Z + y_lo * 2 + core
    sibling = me + 1 - 2 * core
    across = me + 2 - 4 * y_lo
    diagonal = across + 1 - 2 * core
    partners = (sibling, across, diagonal)

    barrier = pltpu.get_barrier_semaphore()
    for peer in partners + (after, before):
        pl.semaphore_signal(barrier, inc=1, device_id=(row, peer), device_id_type=MESH)
    for peer in ctx_peers(groups) if groups else ():
        pl.semaphore_signal(barrier, inc=1, device_id=(peer, me), device_id_type=MESH)
    pl.semaphore_wait(barrier, 5 + max(groups - 1, 0))

    if groups:
        t_local, t_sends, t_receipts = exchange_copies(
            groups, t_ref, t_out_ref, t_local_sem, t_send, t_recv)
        t_local.start()
        for copy in t_sends:
            copy.start()

    width = x_ref.shape[1]

    def cols(first, count):
        return out_ref.at[:, pl.ds(pl.multiple_of(first * width, width), count * width)]

    local = pltpu.make_async_copy(x_ref, cols(me, 1), local_sem)
    local.start()

    def cross(k, peer, slot):
        return pltpu.make_async_remote_copy(
            src_ref=x_ref, dst_ref=cols(slot, 1), send_sem=cross_send.at[k],
            recv_sem=cross_recv.at[k], device_id=(row, peer), device_id_type=MESH)

    for k, peer in enumerate(partners):
        cross(k, peer, me).start()
    local.wait()
    for k, peer in enumerate(partners):
        cross(k, peer, me).wait_send()
        cross(k, peer, peer).wait_recv()

    last = chips // 2 - 1

    def part(chip, s, half):
        if s < last:
            return cols(chip * PER_Z, PER_Z)
        return cols(chip * PER_Z + half * (PER_Z // 2), PER_Z // 2)

    def ring(s, chip):
        return pltpu.make_async_remote_copy(
            src_ref=part(chip, s, core), dst_ref=part(chip, s, core), send_sem=ring_send.at[s],
            recv_sem=ring_recv.at[s], device_id=(row, after), device_id_type=MESH)

    def sib(s, chip, half):
        return pltpu.make_async_remote_copy(
            src_ref=part(chip, s, half), dst_ref=part(chip, s, half), send_sem=sib_send.at[s],
            recv_sem=sib_recv.at[s], device_id=(row, sibling), device_id_type=MESH)

    for s in range(last + 1):
        sent = (z - way * s + chips) % chips
        got = (z - way * (s + 1) + chips) % chips
        ring(s, sent).start()
        ring(s, got).wait_recv()
        sib(s, got, core).start()

    for s in range(last + 1):
        sent = (z - way * s + chips) % chips
        got = (z - way * (s + 1) + chips) % chips
        theirs = (z + way * (s + 1) + chips) % chips
        ring(s, sent).wait_send()
        sib(s, got, core).wait_send()
        sib(s, theirs, 1 - core).wait_recv()

    if groups:
        t_local.wait()
        for copy, receipt in zip(t_sends, t_receipts):
            copy.wait_send()
            receipt.wait_recv()


def exchange_copies(groups, x_ref, out_ref, local_sem, send_sem, recv_sem):
    me = lax.axis_index("ctx")
    col = lax.axis_index("chan")
    local = pltpu.make_async_copy(x_ref.at[me], out_ref.at[me], local_sem)

    def send(k, peer, slot):
        return pltpu.make_async_remote_copy(
            src_ref=x_ref.at[peer], dst_ref=out_ref.at[slot], send_sem=send_sem.at[k - 1],
            recv_sem=recv_sem.at[k - 1], device_id=(peer, col), device_id_type=MESH)

    sends = [send(k, (me + k) % groups, me) for k in range(1, groups)]
    sources = [(me - k + groups) % groups for k in range(1, groups)]
    receipts = [send(k, source, source) for k, source in zip(range(1, groups), sources)]
    return local, sends, receipts


def ctx_peers(groups):
    me = lax.axis_index("ctx")
    return [(me + k) % groups for k in range(1, groups)]


def exchange_kernel(groups, x_ref, out_ref, local_sem, send_sem, recv_sem):
    col = lax.axis_index("chan")
    barrier = pltpu.get_barrier_semaphore()
    for peer in ctx_peers(groups):
        pl.semaphore_signal(barrier, inc=1, device_id=(peer, col), device_id_type=MESH)
    pl.semaphore_wait(barrier, groups - 1)
    local, sends, receipts = exchange_copies(groups, x_ref, out_ref, local_sem, send_sem, recv_sem)
    local.start()
    for copy in sends:
        copy.start()
    local.wait()
    for copy, receipt in zip(sends, receipts):
        copy.wait_send()
        receipt.wait_recv()


def ctx_exchange(x, collective_id):
    groups = lax.axis_size("ctx")
    return pl.pallas_call(
        functools.partial(exchange_kernel, groups),
        out_shape=jax.ShapeDtypeStruct(x.shape, x.dtype),
        in_specs=[pl.BlockSpec(memory_space=pltpu.VMEM)],
        out_specs=pl.BlockSpec(memory_space=pltpu.VMEM),
        scratch_shapes=[
            pltpu.SemaphoreType.DMA(()),
            pltpu.SemaphoreType.DMA((groups - 1,)),
            pltpu.SemaphoreType.DMA((groups - 1,)),
        ],
        compiler_params=pltpu.CompilerParams(collective_id=collective_id, has_side_effects=True),
    )(x)


def chan_gather(x, t, collective_id):
    size = lax.axis_size("chan")
    groups = lax.axis_size("ctx") if t is not None else 0
    chips = size // PER_Z
    longest = chips // 2
    assert chips % 2 == 0
    operands = (x,) if t is None else (x, t)
    out_shape = [jax.ShapeDtypeStruct((x.shape[0], size * x.shape[1]), x.dtype)]
    scratch = [
        pltpu.SemaphoreType.DMA(()),
        pltpu.SemaphoreType.DMA((3,)),
        pltpu.SemaphoreType.DMA((3,)),
        pltpu.SemaphoreType.DMA((longest,)),
        pltpu.SemaphoreType.DMA((longest,)),
        pltpu.SemaphoreType.DMA((longest,)),
        pltpu.SemaphoreType.DMA((longest,)),
    ]
    if t is not None:
        out_shape.append(jax.ShapeDtypeStruct(t.shape, t.dtype))
        scratch += [
            pltpu.SemaphoreType.DMA(()),
            pltpu.SemaphoreType.DMA((groups - 1,)),
            pltpu.SemaphoreType.DMA((groups - 1,)),
        ]
    outs = pl.pallas_call(
        functools.partial(gather_kernel, chips, groups),
        out_shape=tuple(out_shape),
        in_specs=[pl.BlockSpec(memory_space=pltpu.VMEM)] * len(operands),
        out_specs=[pl.BlockSpec(memory_space=pltpu.VMEM)] * len(out_shape),
        scratch_shapes=scratch,
        compiler_params=pltpu.CompilerParams(collective_id=collective_id, has_side_effects=True),
    )(*operands)
    gathered = outs[0]
    return gathered if t is None else (gathered, outs[1])


def half_gather_kernel(chips, groups, t_ref, out_ref, x_ref, local_sem, cross_send, cross_recv,
                       up_send, up_recv, down_send, down_recv, t_local_sem, t_send, t_recv):
    row = lax.axis_index("ctx")
    me = lax.axis_index("chan")
    z = me // PER_Z
    y_lo = (me // 2) % 2
    core = me % 2
    across = me + 2 - 4 * y_lo
    ahead = ((z + 1) % chips) * PER_Z + y_lo * 2 + core
    behind = ((z + chips - 1) % chips) * PER_Z + y_lo * 2 + core
    mine = me // 2
    theirs = across // 2

    barrier = pltpu.get_barrier_semaphore()
    for peer in (across, ahead, behind):
        pl.semaphore_signal(barrier, inc=1, device_id=(row, peer), device_id_type=MESH)
    for peer in ctx_peers(groups):
        pl.semaphore_signal(barrier, inc=1, device_id=(peer, me), device_id_type=MESH)
    pl.semaphore_wait(barrier, 3 + groups - 1)

    slab = t_ref.shape[1]

    def slot(g):
        return x_ref.at[pl.ds(pl.multiple_of(g * slab, slab), slab)]

    def give(k, peer, g):
        return pltpu.make_async_remote_copy(
            src_ref=t_ref.at[peer], dst_ref=slot(g), send_sem=t_send.at[k - 1],
            recv_sem=t_recv.at[k - 1], device_id=(peer, me), device_id_type=MESH)

    t_local = pltpu.make_async_copy(t_ref.at[row], slot(row), t_local_sem)
    t_local.start()
    for k in range(1, groups):
        give(k, (row + k) % groups, row).start()
    t_local.wait()
    for k in range(1, groups):
        give(k, (row + k) % groups, row).wait_send()
        source = (row - k + groups) % groups
        give(k, source, source).wait_recv()

    local = pltpu.make_async_copy(x_ref, out_ref.at[mine], local_sem)
    local.start()

    def cross(slot):
        return pltpu.make_async_remote_copy(
            src_ref=x_ref, dst_ref=out_ref.at[slot], send_sem=cross_send,
            recv_sem=cross_recv, device_id=(row, across), device_id_type=MESH)

    cross(mine).start()
    local.wait()
    cross(mine).wait_send()
    cross(theirs).wait_recv()

    def pair(chip):
        return out_ref.at[pl.ds(pl.multiple_of(chip * 2, 2), 2)]

    steps = chips // 2

    def piece(chip, s, half):
        if s < steps - 1:
            return pair(chip)
        return out_ref.at[pl.ds(chip * 2 + half, 1)]

    def up(s, chip):
        return pltpu.make_async_remote_copy(
            src_ref=piece(chip, s, 0), dst_ref=piece(chip, s, 0), send_sem=up_send.at[s],
            recv_sem=up_recv.at[s], device_id=(row, ahead), device_id_type=MESH)

    def down(s, chip):
        return pltpu.make_async_remote_copy(
            src_ref=piece(chip, s, 1), dst_ref=piece(chip, s, 1), send_sem=down_send.at[s],
            recv_sem=down_recv.at[s], device_id=(row, behind), device_id_type=MESH)

    for s in range(steps):
        if s > 0:
            up(s - 1, (z - s + chips) % chips).wait_recv()
        up(s, (z - s + chips) % chips).start()
        if s > 0:
            down(s - 1, (z + s) % chips).wait_recv()
        down(s, (z + s) % chips).start()
    up(steps - 1, (z - steps + chips) % chips).wait_recv()
    down(steps - 1, (z + steps) % chips).wait_recv()
    for s in range(steps):
        up(s, (z - s + chips) % chips).wait_send()
        down(s, (z + s) % chips).wait_send()


def half_gather(t, collective_id):
    size = lax.axis_size("chan")
    groups = lax.axis_size("ctx")
    chips = size // PER_Z
    assert chips % 2 == 0
    ups = downs = chips // 2
    block = (t.shape[0] * t.shape[1], t.shape[2])
    out = pl.pallas_call(
        functools.partial(half_gather_kernel, chips, groups),
        out_shape=jax.ShapeDtypeStruct((size // 2,) + block, t.dtype),
        in_specs=[pl.BlockSpec(memory_space=pltpu.VMEM)],
        out_specs=pl.BlockSpec(memory_space=pltpu.VMEM),
        scratch_shapes=[
            pltpu.VMEM(block, t.dtype),
            pltpu.SemaphoreType.DMA(()),
            pltpu.SemaphoreType.DMA(()),
            pltpu.SemaphoreType.DMA(()),
            pltpu.SemaphoreType.DMA((ups,)),
            pltpu.SemaphoreType.DMA((ups,)),
            pltpu.SemaphoreType.DMA((downs,)),
            pltpu.SemaphoreType.DMA((downs,)),
            pltpu.SemaphoreType.DMA(()),
            pltpu.SemaphoreType.DMA((groups - 1,)),
            pltpu.SemaphoreType.DMA((groups - 1,)),
        ],
        compiler_params=pltpu.CompilerParams(collective_id=collective_id, has_side_effects=True),
    )(t)
    return out.reshape(size // 2 * block[0], block[1])


def matmul_kernel(x_ref, w_ref, out_ref):
    groups, streams, own, _ = out_ref.shape
    width = w_ref.shape[2]
    joined = jnp.concatenate([w_ref[stream] for stream in range(streams)], axis=1)
    total = jnp.dot(x_ref[...], joined, preferred_element_type=jnp.float32).T
    for stream in range(streams):
        for g in range(groups):
            first = stream * width + g * own
            out_ref[g, stream] = total[first : first + own, :].astype(out_ref.dtype)


def project(x, w, groups):
    streams, _, width = w.shape
    return pl.pallas_call(
        matmul_kernel,
        out_shape=jax.ShapeDtypeStruct((groups, streams, width // groups, x.shape[0]),
                                       jnp.bfloat16),
        in_specs=[pl.BlockSpec(memory_space=pltpu.VMEM)] * 2,
        out_specs=pl.BlockSpec(memory_space=pltpu.VMEM),
        cost_estimate=pl.CostEstimate(
            flops=2 * x.shape[0] * x.shape[1] * streams * width, transcendentals=0,
            bytes_accessed=2 * (x.size + w.size + x.shape[0] * streams * width)),
    )(x, w)


def split_kernel(w_ref, out_ref):
    pieces, _, width = out_ref.shape
    for m in range(pieces):
        out_ref[m] = w_ref[:, m * width : (m + 1) * width]


def split_columns(w, pieces):
    rows, cols = w.shape
    return pl.pallas_call(
        split_kernel,
        out_shape=jax.ShapeDtypeStruct((pieces, rows, cols // pieces), w.dtype),
        in_specs=[pl.BlockSpec(memory_space=pltpu.VMEM)],
        out_specs=pl.BlockSpec(memory_space=pltpu.VMEM),
        cost_estimate=pl.CostEstimate(flops=0, transcendentals=0, bytes_accessed=4 * w.size),
    )(w)


def dft_table(double_len):
    step = 32
    hi_ids = jnp.arange(double_len // step, dtype=jnp.int32)[:, None]
    lo_ids = jnp.arange(step, dtype=jnp.int32)[:, None]
    cols = jnp.arange(double_len, dtype=jnp.int32)[None, :]
    scale = 2.0 * math.pi / double_len
    hi_angle = scale * (hi_ids * step * cols % double_len).astype(jnp.float32)
    lo_angle = scale * (lo_ids * cols % double_len).astype(jnp.float32)
    hc, hs = jnp.cos(hi_angle)[:, None], jnp.sin(hi_angle)[:, None]
    lc, ls = jnp.cos(lo_angle)[None], jnp.sin(lo_angle)[None]
    cos = (hc * lc - hs * ls).reshape(double_len, double_len)
    sin = (hs * lc + hc * ls).reshape(double_len, double_len)
    return jnp.concatenate([cos, -sin], 0).astype(jnp.bfloat16)


def body(inputs, w_in, conv_taps, skip_gain, filter_taps, w_out):
    span_len, width_dev = inputs.shape
    double_len = 2 * span_len
    groups = lax.axis_size("ctx")
    position = lax.axis_index("ctx")
    own = width_dev // groups

    with jax.named_scope("input_gather_and_filter_to_owner"):
        taps_t = filter_taps.T.reshape(groups, own, span_len)
        inputs_all, taps_t = chan_gather(inputs, taps_t, 0)

    with jax.named_scope("input_projection"):
        proj_t = project(inputs_all, jnp.transpose(w_in, (1, 0, 2)), groups)

    with jax.named_scope("projection_to_owner"):
        proj_t = ctx_exchange(proj_t, 3)

    with jax.named_scope("out_weight_columns"):
        w_late, proj_t = lax.optimization_barrier((w_out, proj_t))
        size = lax.axis_size("chan")
        same_core = [list(range(c, size, 2)) for c in range(2)]
        pieces = split_columns(w_late, size // 2)
        w_cols = lax.all_to_all(pieces, "chan", 0, 1, tiled=True, axis_index_groups=same_core)
        w_cols = w_cols.reshape(size // 2 * width_dev, -1)

    with jax.named_scope("short_conv"):
        start = position * own
        taps = lax.dynamic_slice_in_dim(conv_taps, start, own, axis=2)
        rim = jnp.pad(proj_t[:-1, :, :, span_len - (KERNEL - 1) :], ((1, 0), (0, 0), (0, 0), (0, 0)))
        padded = jnp.concatenate([rim, proj_t], 3)
        filtered = jnp.zeros(proj_t.shape, jnp.float32)
        for lag in range(KERNEL):
            start_row = KERNEL - 1 - lag
            filtered = filtered + taps[lag].astype(jnp.float32)[None, :, :, None] * padded[
                ..., start_row : start_row + span_len
            ].astype(jnp.float32)
        streams = filtered.astype(jnp.bfloat16)
        gate_out = streams[:, 0]
        gated_in = (streams[:, 1].astype(jnp.float32) * streams[:, 2].astype(jnp.float32)).astype(
            jnp.bfloat16
        )

    with jax.named_scope("spectra"):
        table = dft_table(double_len)
        forward_in = table[:, :span_len]
        spectra_in = jnp.einsum(
            "jdb,fb->jdf", gated_in, forward_in, preferred_element_type=jnp.float32
        ).astype(jnp.bfloat16)
        previous = jnp.pad(taps_t[:-1, :, 1:], ((1, 0), (0, 0), (0, 0)))
        padded_taps = jnp.concatenate(
            [taps_t, jnp.zeros((groups, own, 1), jnp.bfloat16), previous], 2
        )
        spectra_taps = jnp.einsum(
            "kdm,fm->kdf", padded_taps, table, preferred_element_type=jnp.float32
        ).astype(jnp.bfloat16)

    with jax.named_scope("mixture"):
        real_g = spectra_taps[:, :, :double_len].astype(jnp.float32)
        imag_g = spectra_taps[:, :, double_len:].astype(jnp.float32)
        real_u = spectra_in[:, :, :double_len].astype(jnp.float32)
        imag_u = spectra_in[:, :, double_len:].astype(jnp.float32)
        acc_r = jnp.zeros(real_u.shape, jnp.float32)
        acc_i = jnp.zeros(real_u.shape, jnp.float32)
        for lag in range(groups):
            keep = groups - lag
            shift = ((lag, 0), (0, 0), (0, 0))
            acc_r = acc_r + jnp.pad(
                real_g[lag] * real_u[:keep] - imag_g[lag] * imag_u[:keep], shift)
            acc_i = acc_i + jnp.pad(
                real_g[lag] * imag_u[:keep] + imag_g[lag] * real_u[:keep], shift)
        mixture = jnp.concatenate([acc_r, acc_i], 2).astype(jnp.bfloat16)

    with jax.named_scope("inverse_and_gate"):
        long_out = jnp.einsum(
            "idf,fa->ida", mixture, forward_in, preferred_element_type=jnp.float32
        ) * (1.0 / double_len)
        gain = lax.dynamic_slice_in_dim(skip_gain, start, own)
        long_out = long_out + gain[None, :, None] * gated_in.astype(jnp.float32)
        gated_out = (gate_out.astype(jnp.float32) * long_out).astype(jnp.bfloat16)

    with jax.named_scope("output_projection"):
        gathered = half_gather(gated_out, 1)
        partial = lax.dot_general(
            gathered, w_cols, (((0,), (0,)), ((), ())), preferred_element_type=jnp.float32
        )
        core = lax.axis_index("chan") % 2
        mine = lax.dynamic_slice_in_dim(partial, core * width_dev, width_dev, axis=1)
        other = lax.dynamic_slice_in_dim(partial, (1 - core) * width_dev, width_dev, axis=1)
        pairs = [(h, h + 1 - 2 * (h % 2)) for h in range(lax.axis_size("chan"))]
        result = (mine + lax.ppermute(other, "chan", pairs)).astype(jnp.bfloat16)
    return result


def solution(mesh):
    return jax.shard_map(
        body,
        mesh=mesh,
        in_specs=(
            P("ctx", "chan"),
            P(None, None, "chan"),
            P(None, None, "chan"),
            P("chan"),
            P("ctx", "chan"),
            P("chan", None),
        ),
        out_specs=P("ctx", "chan"),
        check_vma=False,
    )
```

```python
import math

import functools

import jax
import jax.numpy as jnp
from jax import lax
from jax.experimental import pallas as pl
from jax.experimental.pallas import tpu as pltpu
from jax.sharding import PartitionSpec as P

KERNEL = 3
MESH = pl.DeviceIdType.MESH
PER_Z = 4


def gather_kernel(chips, groups, *refs):
    if groups:
        (x_ref, t_ref, out_ref, t_out_ref, local_sem, cross_send, cross_recv, ring_send, ring_recv,
         sib_send, sib_recv, t_local_sem, t_send, t_recv) = refs
    else:
        (x_ref, out_ref, local_sem, cross_send, cross_recv, ring_send, ring_recv,
         sib_send, sib_recv) = refs
    row = lax.axis_index("ctx")
    me = lax.axis_index("chan")
    z = me // PER_Z
    y_lo = (me // 2) % 2
    core = me % 2
    way = 1 - 2 * core
    after = ((z + way + chips) % chips) * PER_Z + y_lo * 2 + core
    before = ((z - way + chips) % chips) * PER_Z + y_lo * 2 + core
    sibling = me + 1 - 2 * core
    across = me + 2 - 4 * y_lo
    diagonal = across + 1 - 2 * core
    partners = (sibling, across, diagonal)

    barrier = pltpu.get_barrier_semaphore()
    for peer in partners + (after, before):
        pl.semaphore_signal(barrier, inc=1, device_id=(row, peer), device_id_type=MESH)
    for peer in ctx_peers(groups) if groups else ():
        pl.semaphore_signal(barrier, inc=1, device_id=(peer, me), device_id_type=MESH)
    pl.semaphore_wait(barrier, 5 + max(groups - 1, 0))

    if groups:
        t_local, t_sends, t_receipts = exchange_copies(
            groups, t_ref, t_out_ref, t_local_sem, t_send, t_recv)
        t_local.start()
        for copy in t_sends:
            copy.start()

    width = x_ref.shape[1]

    def cols(first, count):
        return out_ref.at[:, pl.ds(pl.multiple_of(first * width, width), count * width)]

    local = pltpu.make_async_copy(x_ref, cols(me, 1), local_sem)
    local.start()

    def cross(k, peer, slot):
        return pltpu.make_async_remote_copy(
            src_ref=x_ref, dst_ref=cols(slot, 1), send_sem=cross_send.at[k],
            recv_sem=cross_recv.at[k], device_id=(row, peer), device_id_type=MESH)

    for k, peer in enumerate(partners):
        cross(k, peer, me).start()
    local.wait()
    for k, peer in enumerate(partners):
        cross(k, peer, me).wait_send()
        cross(k, peer, peer).wait_recv()

    last = chips // 2 - 1

    def part(chip, s, half):
        if s < last:
            return cols(chip * PER_Z, PER_Z)
        return cols(chip * PER_Z + half * (PER_Z // 2), PER_Z // 2)

    def ring(s, chip):
        return pltpu.make_async_remote_copy(
            src_ref=part(chip, s, core), dst_ref=part(chip, s, core), send_sem=ring_send.at[s],
            recv_sem=ring_recv.at[s], device_id=(row, after), device_id_type=MESH)

    def sib(s, chip, half):
        return pltpu.make_async_remote_copy(
            src_ref=part(chip, s, half), dst_ref=part(chip, s, half), send_sem=sib_send.at[s],
            recv_sem=sib_recv.at[s], device_id=(row, sibling), device_id_type=MESH)

    for s in range(last + 1):
        sent = (z - way * s + chips) % chips
        got = (z - way * (s + 1) + chips) % chips
        ring(s, sent).start()
        ring(s, got).wait_recv()
        sib(s, got, core).start()

    for s in range(last + 1):
        sent = (z - way * s + chips) % chips
        got = (z - way * (s + 1) + chips) % chips
        theirs = (z + way * (s + 1) + chips) % chips
        ring(s, sent).wait_send()
        sib(s, got, core).wait_send()
        sib(s, theirs, 1 - core).wait_recv()

    if groups:
        t_local.wait()
        for copy, receipt in zip(t_sends, t_receipts):
            copy.wait_send()
            receipt.wait_recv()


def exchange_copies(groups, x_ref, out_ref, local_sem, send_sem, recv_sem):
    me = lax.axis_index("ctx")
    col = lax.axis_index("chan")
    local = pltpu.make_async_copy(x_ref.at[me], out_ref.at[me], local_sem)

    def send(k, peer, slot):
        return pltpu.make_async_remote_copy(
            src_ref=x_ref.at[peer], dst_ref=out_ref.at[slot], send_sem=send_sem.at[k - 1],
            recv_sem=recv_sem.at[k - 1], device_id=(peer, col), device_id_type=MESH)

    order = far_first(groups)
    peers = [flip(me, k) for k in order]
    sends = [send(i + 1, peer, me) for i, peer in enumerate(peers)]
    receipts = [send(i + 1, peer, peer) for i, peer in enumerate(peers)]
    return local, sends, receipts


def flip(me, k):
    out, bit = 0, 1
    while bit <= k:
        mine = (me // bit) % 2
        theirs = (k // bit) % 2
        out = out + bit * (mine + theirs - 2 * mine * theirs)
        bit *= 2
    return out + (me // bit) * bit


def far_first(groups):
    hops = lambda k: 2 * (k % 2) + [0, 1, 2, 1][(k // 2) % 4]
    return sorted(range(1, groups), key=lambda k: -hops(k))


def ctx_peers(groups):
    me = lax.axis_index("ctx")
    return [(me + k) % groups for k in range(1, groups)]


def exchange_kernel(groups, x_ref, out_ref, local_sem, send_sem, recv_sem):
    col = lax.axis_index("chan")
    barrier = pltpu.get_barrier_semaphore()
    for peer in ctx_peers(groups):
        pl.semaphore_signal(barrier, inc=1, device_id=(peer, col), device_id_type=MESH)
    pl.semaphore_wait(barrier, groups - 1)
    local, sends, receipts = exchange_copies(groups, x_ref, out_ref, local_sem, send_sem, recv_sem)
    local.start()
    for copy in sends:
        copy.start()
    local.wait()
    for copy, receipt in zip(sends, receipts):
        copy.wait_send()
        receipt.wait_recv()


def ctx_exchange(x, collective_id):
    groups = lax.axis_size("ctx")
    return pl.pallas_call(
        functools.partial(exchange_kernel, groups),
        out_shape=jax.ShapeDtypeStruct(x.shape, x.dtype),
        in_specs=[pl.BlockSpec(memory_space=pltpu.VMEM)],
        out_specs=pl.BlockSpec(memory_space=pltpu.VMEM),
        scratch_shapes=[
            pltpu.SemaphoreType.DMA(()),
            pltpu.SemaphoreType.DMA((groups - 1,)),
            pltpu.SemaphoreType.DMA((groups - 1,)),
        ],
        compiler_params=pltpu.CompilerParams(collective_id=collective_id, has_side_effects=True),
    )(x)


def chan_gather(x, t, collective_id):
    size = lax.axis_size("chan")
    groups = lax.axis_size("ctx") if t is not None else 0
    chips = size // PER_Z
    longest = chips // 2
    assert chips % 2 == 0
    operands = (x,) if t is None else (x, t)
    out_shape = [jax.ShapeDtypeStruct((x.shape[0], size * x.shape[1]), x.dtype)]
    scratch = [
        pltpu.SemaphoreType.DMA(()),
        pltpu.SemaphoreType.DMA((3,)),
        pltpu.SemaphoreType.DMA((3,)),
        pltpu.SemaphoreType.DMA((longest,)),
        pltpu.SemaphoreType.DMA((longest,)),
        pltpu.SemaphoreType.DMA((longest,)),
        pltpu.SemaphoreType.DMA((longest,)),
    ]
    if t is not None:
        out_shape.append(jax.ShapeDtypeStruct(t.shape, t.dtype))
        scratch += [
            pltpu.SemaphoreType.DMA(()),
            pltpu.SemaphoreType.DMA((groups - 1,)),
            pltpu.SemaphoreType.DMA((groups - 1,)),
        ]
    outs = pl.pallas_call(
        functools.partial(gather_kernel, chips, groups),
        out_shape=tuple(out_shape),
        in_specs=[pl.BlockSpec(memory_space=pltpu.VMEM)] * len(operands),
        out_specs=[pl.BlockSpec(memory_space=pltpu.VMEM)] * len(out_shape),
        scratch_shapes=scratch,
        compiler_params=pltpu.CompilerParams(collective_id=collective_id, has_side_effects=True),
    )(*operands)
    gathered = outs[0]
    return gathered if t is None else (gathered, outs[1])


def half_gather_kernel(chips, groups, t_ref, out_ref, x_ref, local_sem, cross_send, cross_recv,
                       up_send, up_recv, down_send, down_recv, t_local_sem, t_send, t_recv):
    row = lax.axis_index("ctx")
    me = lax.axis_index("chan")
    z = me // PER_Z
    y_lo = (me // 2) % 2
    core = me % 2
    across = me + 2 - 4 * y_lo
    ahead = ((z + 1) % chips) * PER_Z + y_lo * 2 + core
    behind = ((z + chips - 1) % chips) * PER_Z + y_lo * 2 + core
    mine = me // 2
    theirs = across // 2

    barrier = pltpu.get_barrier_semaphore()
    for peer in (across, ahead, behind):
        pl.semaphore_signal(barrier, inc=1, device_id=(row, peer), device_id_type=MESH)
    for peer in ctx_peers(groups):
        pl.semaphore_signal(barrier, inc=1, device_id=(peer, me), device_id_type=MESH)
    pl.semaphore_wait(barrier, 3 + groups - 1)

    slab = t_ref.shape[1]

    def slot(g):
        return x_ref.at[pl.ds(pl.multiple_of(g * slab, slab), slab)]

    def give(k, peer, g):
        return pltpu.make_async_remote_copy(
            src_ref=t_ref.at[peer], dst_ref=slot(g), send_sem=t_send.at[k - 1],
            recv_sem=t_recv.at[k - 1], device_id=(peer, me), device_id_type=MESH)

    t_local = pltpu.make_async_copy(t_ref.at[row], slot(row), t_local_sem)
    t_local.start()
    for k in range(1, groups):
        give(k, (row + k) % groups, row).start()
    t_local.wait()
    for k in range(1, groups):
        give(k, (row + k) % groups, row).wait_send()
        source = (row - k + groups) % groups
        give(k, source, source).wait_recv()

    local = pltpu.make_async_copy(x_ref, out_ref.at[mine], local_sem)
    local.start()

    def cross(slot):
        return pltpu.make_async_remote_copy(
            src_ref=x_ref, dst_ref=out_ref.at[slot], send_sem=cross_send,
            recv_sem=cross_recv, device_id=(row, across), device_id_type=MESH)

    cross(mine).start()
    local.wait()
    cross(mine).wait_send()
    cross(theirs).wait_recv()

    def pair(chip):
        return out_ref.at[pl.ds(pl.multiple_of(chip * 2, 2), 2)]

    steps = chips // 2

    def piece(chip, s, half):
        if s < steps - 1:
            return pair(chip)
        return out_ref.at[pl.ds(chip * 2 + half, 1)]

    def up(s, chip):
        return pltpu.make_async_remote_copy(
            src_ref=piece(chip, s, 0), dst_ref=piece(chip, s, 0), send_sem=up_send.at[s],
            recv_sem=up_recv.at[s], device_id=(row, ahead), device_id_type=MESH)

    def down(s, chip):
        return pltpu.make_async_remote_copy(
            src_ref=piece(chip, s, 1), dst_ref=piece(chip, s, 1), send_sem=down_send.at[s],
            recv_sem=down_recv.at[s], device_id=(row, behind), device_id_type=MESH)

    for s in range(steps):
        if s > 0:
            up(s - 1, (z - s + chips) % chips).wait_recv()
        up(s, (z - s + chips) % chips).start()
        if s > 0:
            down(s - 1, (z + s) % chips).wait_recv()
        down(s, (z + s) % chips).start()
    up(steps - 1, (z - steps + chips) % chips).wait_recv()
    down(steps - 1, (z + steps) % chips).wait_recv()
    for s in range(steps):
        up(s, (z - s + chips) % chips).wait_send()
        down(s, (z + s) % chips).wait_send()


def half_gather(t, collective_id):
    size = lax.axis_size("chan")
    groups = lax.axis_size("ctx")
    chips = size // PER_Z
    assert chips % 2 == 0
    ups = downs = chips // 2
    block = (t.shape[0] * t.shape[1], t.shape[2])
    out = pl.pallas_call(
        functools.partial(half_gather_kernel, chips, groups),
        out_shape=jax.ShapeDtypeStruct((size // 2,) + block, t.dtype),
        in_specs=[pl.BlockSpec(memory_space=pltpu.VMEM)],
        out_specs=pl.BlockSpec(memory_space=pltpu.VMEM),
        scratch_shapes=[
            pltpu.VMEM(block, t.dtype),
            pltpu.SemaphoreType.DMA(()),
            pltpu.SemaphoreType.DMA(()),
            pltpu.SemaphoreType.DMA(()),
            pltpu.SemaphoreType.DMA((ups,)),
            pltpu.SemaphoreType.DMA((ups,)),
            pltpu.SemaphoreType.DMA((downs,)),
            pltpu.SemaphoreType.DMA((downs,)),
            pltpu.SemaphoreType.DMA(()),
            pltpu.SemaphoreType.DMA((groups - 1,)),
            pltpu.SemaphoreType.DMA((groups - 1,)),
        ],
        compiler_params=pltpu.CompilerParams(collective_id=collective_id, has_side_effects=True),
    )(t)
    return out.reshape(size // 2 * block[0], block[1])


def matmul_kernel(x_ref, w_ref, out_ref):
    groups, streams, own, _ = out_ref.shape
    width = w_ref.shape[2]
    joined = jnp.concatenate([w_ref[stream] for stream in range(streams)], axis=1)
    total = jnp.dot(x_ref[...], joined, preferred_element_type=jnp.float32).T
    for stream in range(streams):
        for g in range(groups):
            first = stream * width + g * own
            out_ref[g, stream] = total[first : first + own, :].astype(out_ref.dtype)


def project(x, w, groups):
    streams, _, width = w.shape
    return pl.pallas_call(
        matmul_kernel,
        out_shape=jax.ShapeDtypeStruct((groups, streams, width // groups, x.shape[0]),
                                       jnp.bfloat16),
        in_specs=[pl.BlockSpec(memory_space=pltpu.VMEM)] * 2,
        out_specs=pl.BlockSpec(memory_space=pltpu.VMEM),
        cost_estimate=pl.CostEstimate(
            flops=2 * x.shape[0] * x.shape[1] * streams * width, transcendentals=0,
            bytes_accessed=2 * (x.size + w.size + x.shape[0] * streams * width)),
    )(x, w)


def dft_table(double_len):
    step = 32
    hi_ids = jnp.arange(double_len // step, dtype=jnp.int32)[:, None]
    lo_ids = jnp.arange(step, dtype=jnp.int32)[:, None]
    cols = jnp.arange(double_len, dtype=jnp.int32)[None, :]
    scale = 2.0 * math.pi / double_len
    hi_angle = scale * (hi_ids * step * cols % double_len).astype(jnp.float32)
    lo_angle = scale * (lo_ids * cols % double_len).astype(jnp.float32)
    hc, hs = jnp.cos(hi_angle)[:, None], jnp.sin(hi_angle)[:, None]
    lc, ls = jnp.cos(lo_angle)[None], jnp.sin(lo_angle)[None]
    cos = (hc * lc - hs * ls).reshape(double_len, double_len)
    sin = (hs * lc + hc * ls).reshape(double_len, double_len)
    return jnp.concatenate([cos, -sin], 0).astype(jnp.bfloat16)


def body(inputs, w_in, conv_taps, skip_gain, filter_taps, w_out):
    span_len, width_dev = inputs.shape
    double_len = 2 * span_len
    groups = lax.axis_size("ctx")
    position = lax.axis_index("ctx")
    own = width_dev // groups

    with jax.named_scope("input_gather_and_filter_to_owner"):
        taps_t = filter_taps.T.reshape(groups, own, span_len)
        inputs_all, taps_t = chan_gather(inputs, taps_t, 0)

    with jax.named_scope("input_projection"):
        proj_t = project(inputs_all, jnp.transpose(w_in, (1, 0, 2)), groups)

    with jax.named_scope("projection_to_owner"):
        proj_t = ctx_exchange(proj_t, 3)

    with jax.named_scope("out_weight_columns"):
        w_late, proj_t = lax.optimization_barrier((w_out, proj_t))
        size = lax.axis_size("chan")
        same_core = [list(range(c, size, 2)) for c in range(2)]
        w_cols = lax.all_to_all(w_late, "chan", 1, 0, tiled=True, axis_index_groups=same_core)

    with jax.named_scope("short_conv"):
        start = position * own
        taps = lax.dynamic_slice_in_dim(conv_taps, start, own, axis=2)
        rim = jnp.pad(proj_t[:-1, :, :, span_len - (KERNEL - 1) :], ((1, 0), (0, 0), (0, 0), (0, 0)))
        padded = jnp.concatenate([rim, proj_t], 3)
        filtered = jnp.zeros(proj_t.shape, jnp.float32)
        for lag in range(KERNEL):
            start_row = KERNEL - 1 - lag
            filtered = filtered + taps[lag].astype(jnp.float32)[None, :, :, None] * padded[
                ..., start_row : start_row + span_len
            ].astype(jnp.float32)
        streams = filtered.astype(jnp.bfloat16)
        gate_out = streams[:, 0]
        gated_in = (streams[:, 1].astype(jnp.float32) * streams[:, 2].astype(jnp.float32)).astype(
            jnp.bfloat16
        )

    with jax.named_scope("spectra"):
        table = dft_table(double_len)
        forward_in = table[:, :span_len]
        spectra_in = jnp.einsum(
            "jdb,fb->jdf", gated_in, forward_in, preferred_element_type=jnp.float32
        ).astype(jnp.bfloat16)
        previous = jnp.pad(taps_t[:-1, :, 1:], ((1, 0), (0, 0), (0, 0)))
        padded_taps = jnp.concatenate(
            [taps_t, jnp.zeros((groups, own, 1), jnp.bfloat16), previous], 2
        )
        spectra_taps = jnp.einsum(
            "kdm,fm->kdf", padded_taps, table, preferred_element_type=jnp.float32
        ).astype(jnp.bfloat16)

    with jax.named_scope("mixture"):
        real_g = spectra_taps[:, :, :double_len].astype(jnp.float32)
        imag_g = spectra_taps[:, :, double_len:].astype(jnp.float32)
        real_u = spectra_in[:, :, :double_len].astype(jnp.float32)
        imag_u = spectra_in[:, :, double_len:].astype(jnp.float32)
        acc_r = jnp.zeros(real_u.shape, jnp.float32)
        acc_i = jnp.zeros(real_u.shape, jnp.float32)
        for lag in range(groups):
            keep = groups - lag
            shift = ((lag, 0), (0, 0), (0, 0))
            acc_r = acc_r + jnp.pad(
                real_g[lag] * real_u[:keep] - imag_g[lag] * imag_u[:keep], shift)
            acc_i = acc_i + jnp.pad(
                real_g[lag] * imag_u[:keep] + imag_g[lag] * real_u[:keep], shift)
        mixture = jnp.concatenate([acc_r, acc_i], 2).astype(jnp.bfloat16)

    with jax.named_scope("inverse_and_gate"):
        long_out = jnp.einsum(
            "idf,fa->ida", mixture, forward_in, preferred_element_type=jnp.float32
        ) * (1.0 / double_len)
        gain = lax.dynamic_slice_in_dim(skip_gain, start, own)
        long_out = long_out + gain[None, :, None] * gated_in.astype(jnp.float32)
        gated_out = (gate_out.astype(jnp.float32) * long_out).astype(jnp.bfloat16)

    with jax.named_scope("output_projection"):
        gathered = half_gather(gated_out, 1)
        partial = lax.dot_general(
            gathered, w_cols, (((0,), (0,)), ((), ())), preferred_element_type=jnp.float32
        )
        core = lax.axis_index("chan") % 2
        mine = lax.dynamic_slice_in_dim(partial, core * width_dev, width_dev, axis=1)
        other = lax.dynamic_slice_in_dim(partial, (1 - core) * width_dev, width_dev, axis=1)
        pairs = [(h, h + 1 - 2 * (h % 2)) for h in range(lax.axis_size("chan"))]
        result = (mine + lax.ppermute(other, "chan", pairs)).astype(jnp.bfloat16)
    return result


def solution(mesh):
    return jax.shard_map(
        body,
        mesh=mesh,
        in_specs=(
            P("ctx", "chan"),
            P(None, None, "chan"),
            P(None, None, "chan"),
            P("chan"),
            P("ctx", "chan"),
            P("chan", None),
        ),
        out_specs=P("ctx", "chan"),
        check_vma=False,
    )
```
